128 devices in a mesh: ctx: 4 (over x_hi, core), dp: 32 (over y, x_lo, z).
Axes of the slice: x: 4 (x_hi: 2, x_lo: 2; x = x_hi * 2 + x_lo), y: 4, z: 4, core: 2. Of those that a mesh axis runs over, the one named last changes fastest.
Arguments:
- query_in: bfloat16 [32, 1024, 256], P('dp', 'ctx'), may hold values from -6 to 6
- key_in: bfloat16 [32, 1024, 256], P('dp', 'ctx'), may hold values from -6 to 6
- value_in: bfloat16 [32, 1024, 256], P('dp', 'ctx'), may hold values from -6 to 6
- short_taps: float32 [3, 3, 256], replicated, may hold values from -3 to 3
- long_filter: bfloat16 [16, 1024], replicated, may hold values from -1 to 1
- skip_gain: float32 [256], replicated, may hold values from 0.5 to 1.5
- out_weight: bfloat16 [8192, 256], replicated, may hold values from -0.375 to 0.375
- out_cotangent: bfloat16 [32, 1024, 8192], P('dp', 'ctx'), may hold values from -6 to 6
Outputs:
- gated_out: bfloat16 [32, 1024, 256], P('dp', 'ctx')
- grad_query: bfloat16 [32, 1024, 256], P('dp', 'ctx')
- grad_key: bfloat16 [32, 1024, 256], P('dp', 'ctx')
- grad_value: bfloat16 [32, 1024, 256], P('dp', 'ctx')
- grad_taps: float32 [3, 3, 256], replicated
- grad_filter: float32 [16, 1024], replicated
- grad_skip: float32 [256], replicated
- grad_weight: float32 [8192, 256], P('ctx')
The draws below stay inside these ranges and needn't reach their ends.
All inputs are finite; a program needn't handle non-finite values.
Results may differ from the reference program's by a relative error of at most 0.015.
Values may be sent and summed in bfloat16 or wider, within the bound.
No kernel may reach another device: no remote copies, remote signals or barrier semaphores. Data moves between devices by JAX's collectives and lax.ppermute only.
A program may use at most 128 MiB of HBM per device.

```python
import math
import jax
import jax.numpy as jnp
from jax import lax

D = 8192
C = 256
FILTER_GROUPS = 16
SEQUENCE_LENGTH = 1024
SEQS = 32


def draw_long_filter(key, part):
    random_keys = jax.random.split(key, 6)
    token_position = jnp.arange(SEQUENCE_LENGTH, dtype=jnp.float32)[None, :]
    slow_tau = jnp.exp(jax.random.uniform(random_keys[0], (FILTER_GROUPS, 1), minval=jnp.log(SEQUENCE_LENGTH * 1.0), maxval=jnp.log(SEQUENCE_LENGTH * 4.0)))
    fast_tau = jax.random.uniform(random_keys[1], (FILTER_GROUPS, 1), minval=30.0, maxval=50.0)
    chosen = jax.random.randint(random_keys[3], (FILTER_GROUPS, 1), 0, 2)
    decay_length = jnp.where(chosen == 1, fast_tau, slow_tau)
    noise = jnp.clip(jax.random.normal(random_keys[2], (FILTER_GROUPS, SEQUENCE_LENGTH)), -4.0, 4.0)
    spike_position = jax.random.randint(random_keys[4], (FILTER_GROUPS, 2), 1, SEQUENCE_LENGTH).astype(jnp.float32)
    spike_retained = jax.random.uniform(random_keys[5], (FILTER_GROUPS, 2), minval=0.5, maxval=0.8)
    spike_values = jnp.where(token_position >= spike_position[:, 0:1], spike_retained[:, 0:1], 1.0) * jnp.where(token_position >= spike_position[:, 1:2], spike_retained[:, 1:2], 1.0)
    decay_envelope = jnp.exp(-token_position / decay_length) * spike_values * jnp.sqrt(1.0 / jnp.minimum(decay_length, SEQUENCE_LENGTH * 1.0))
    return (noise * decay_envelope).astype(jnp.bfloat16)


def raised(drawn, own_key, source, target, blocks, factor):
    owner, partner = [(jnp.arange(drawn.shape[dim]) // (drawn.shape[dim] // blocks)).reshape([-1 if axis == dim else 1 for axis in range(drawn.ndim)]) for dim in (source, target)]
    chosen = jax.random.permutation(own_key, blocks)[partner]
    strong = (owner == chosen) | (owner == (partner + blocks // 2) % blocks)
    return jnp.where(strong, factor * drawn, drawn)


def block_levels(key, dims, shards, low, top_value):
    def one(position, parts):
        draws = jax.random.uniform(jax.random.fold_in(jax.random.fold_in(key, 6), position), (parts,), jnp.float32, low / len(shards), top_value / len(shards))
        return jnp.repeat(jnp.exp(draws), dims[position] // parts).reshape((-1,) + (1,) * (len(dims) - position - 1))

    gain = one(*shards[0])
    for cut in shards[1:]:
        gain = gain * one(*cut)
    return gain


def gaussian(own_key, shape, spread, bound, cuts=(), kind=jnp.bfloat16):
    array = jax.random.normal(own_key, shape, jnp.float32) * spread
    if len(cuts) > 0:
        array = block_levels(own_key, shape, cuts, -0.22, 0.18) * array
    return jnp.clip(array, min=-bound, max=bound).astype(kind)


def heavy_noise(key, dims, spread, bound, cuts, heavy, kind=jnp.bfloat16):
    result = spread * jax.random.normal(key, dims, jnp.float32)
    if cuts:
        result = result * block_levels(key, dims, cuts, -0.22, 0.18)
    return jnp.clip(raised(result, jax.random.fold_in(key, 3), *heavy), -bound, bound).astype(kind)


def setup_inputs(seed: int = 0) -> dict:
    splits = jax.random.split(jax.random.key(seed), 9)
    query_in = gaussian(splits[0], (SEQS, SEQUENCE_LENGTH, C), 1.0, 6.0, ((0, 32), (1, 4)))
    key_in = gaussian(splits[1], (SEQS, SEQUENCE_LENGTH, C), 1.0, 6.0, ((0, 32), (1, 4)))
    value_in = gaussian(splits[2], (SEQS, SEQUENCE_LENGTH, C), 1.0, 6.0, ((0, 32), (1, 4)))
    short_taps = gaussian(splits[3], (3, 3, C), 0.6, 3.0, (), jnp.float32)
    long_filter = draw_long_filter(jax.random.fold_in(splits[8], 71), 0)
    skip_gain = jnp.clip(jax.random.uniform(splits[5], (C,), jnp.float32, 0.5, 1.5), 0.5, 1.5)
    out_weight = gaussian(splits[6], (D, C), C ** -0.5, 0.375)
    out_cotangent = heavy_noise(splits[7], (SEQS, SEQUENCE_LENGTH, D), 1.0, 6.0, ((0, 32), (1, 4)), (0, 2, 32, 2.75))
    return {"query_in": query_in, "key_in": key_in, "value_in": value_in, "short_taps": short_taps, "long_filter": long_filter, "skip_gain": skip_gain, "out_weight": out_weight, "out_cotangent": out_cotangent}


def short_apply(signal, taps):
    shift_one = jnp.pad(signal, ((0, 0), (1, 0), (0, 0)))[:, :-1]
    shift_two = jnp.pad(signal, ((0, 0), (2, 0), (0, 0)))[:, :-2]
    return taps[0] * signal + taps[1] * shift_one + taps[2] * shift_two

def short_adjoint(grads, taps):
    ahead_one = jnp.pad(grads, ((0, 0), (0, 1), (0, 0)))[:, 1:]
    ahead_two = jnp.pad(grads, ((0, 0), (0, 2), (0, 0)))[:, 2:]
    return taps[0] * grads + taps[1] * ahead_one + taps[2] * ahead_two

def short_grads(grads, signal):
    shift_one = jnp.pad(signal, ((0, 0), (1, 0), (0, 0)))[:, :-1]
    shift_two = jnp.pad(signal, ((0, 0), (2, 0), (0, 0)))[:, :-2]
    return jnp.stack([lax.optimization_barrier(jnp.sum(grads * signal, axis=(0, 1))), lax.optimization_barrier(jnp.sum(grads * shift_one, axis=(0, 1))), lax.optimization_barrier(jnp.sum(grads * shift_two, axis=(0, 1)))])

def reference(query_in, key_in, value_in, short_taps, long_filter, skip_gain, out_weight, out_cotangent):
    seq_count, length, chans = query_in.shape
    groups = long_filter.shape[0]
    width = chans // groups
    highest = lax.Precision.HIGHEST
    query_f = query_in.astype(jnp.float32)
    key_f = key_in.astype(jnp.float32)
    value_f = value_in.astype(jnp.float32)
    q_short = short_apply(query_f, short_taps[0])
    k_short = short_apply(key_f, short_taps[1])
    v_short = short_apply(value_f, short_taps[2])
    mixed = (k_short * v_short).astype(jnp.bfloat16)
    mixed_f = mixed.astype(jnp.float32)
    lag_table = jnp.arange(length, dtype=jnp.int32)[:, None] - jnp.arange(length, dtype=jnp.int32)[None, :]

    def toeplitz(filter_row):
        values = filter_row.astype(jnp.float32)[jnp.clip(lag_table, 0, length - 1)]
        return jnp.where(lag_table >= 0, values, jnp.float32(0.0))

    def to_groups(signal):
        return jnp.transpose(signal.reshape(seq_count, length, groups, width), (2, 0, 1, 3))

    def from_groups(signal):
        return jnp.transpose(signal, (1, 2, 0, 3)).reshape(seq_count, length, chans)

    def forward_group(group_item):
        filter_row, mixed_grp = group_item
        return jnp.einsum('ts,bsw->btw', toeplitz(filter_row), mixed_grp, precision=highest)
    convolved = from_groups(lax.map(forward_group, (long_filter, to_groups(mixed_f))))
    inner = convolved + skip_gain * mixed_f
    gated_out = (q_short * inner).astype(jnp.bfloat16)
    scale = 1.0 / math.sqrt(seq_count * length)
    flat_cot = out_cotangent.reshape(seq_count * length, -1)
    flat_gated = gated_out.reshape(seq_count * length, chans)
    grad_weight = jnp.dot(flat_cot.T, flat_gated, preferred_element_type=jnp.float32) * scale
    d_gated = jnp.dot(flat_cot, out_weight, preferred_element_type=jnp.float32).astype(jnp.bfloat16).reshape(seq_count, length, chans)
    d_gated_f = d_gated.astype(jnp.float32)
    d_inner = (d_gated_f * q_short).astype(jnp.bfloat16)
    d_inner_f = d_inner.astype(jnp.float32)
    d_qs = d_gated_f * inner
    seg_ids = jnp.where(lag_table >= 0, lag_table, length).reshape(-1)

    def backward_group(group_item):
        filter_row, mixed_grp, inner_grp = group_item
        back_part = jnp.einsum('ts,btw->bsw', toeplitz(filter_row), inner_grp, precision=highest)
        outer = jnp.einsum('btw,bsw->ts', inner_grp, mixed_grp, precision=highest)
        lag_sum = jax.ops.segment_sum(outer.reshape(-1), seg_ids, num_segments=length + 1)[:length]
        return (back_part, lag_sum)
    back_parts, lag_sums = lax.map(backward_group, (long_filter, to_groups(mixed_f), to_groups(d_inner_f)))
    d_mixed = from_groups(back_parts) + skip_gain * d_inner_f
    grad_filter = lag_sums * scale
    grad_skip = lax.optimization_barrier(jnp.sum(d_inner_f * mixed_f, axis=(0, 1))) * scale
    d_ks = d_mixed * v_short
    d_vs = d_mixed * k_short
    grad_taps = jnp.stack([short_grads(d_qs, query_f), short_grads(d_ks, key_f), short_grads(d_vs, value_f)]) * scale
    grad_query = short_adjoint(d_qs, short_taps[0]).astype(jnp.bfloat16)
    grad_key = short_adjoint(d_ks, short_taps[1]).astype(jnp.bfloat16)
    grad_value = short_adjoint(d_vs, short_taps[2]).astype(jnp.bfloat16)
    return (gated_out, grad_query, grad_key, grad_value, grad_taps, grad_filter, grad_skip, grad_weight)
```

```python
import math

import jax
import jax.numpy as jnp
from jax import lax
from jax.experimental import pallas as pl
from jax.experimental.pallas import tpu as pltpu
from jax.sharding import Mesh
from jax.sharding import PartitionSpec as P

F32 = jnp.float32
BF16 = jnp.bfloat16
CTX = ("xh", "co")
DP = ("y", "xl", "z")
CHIPS = ("xh", "y", "xl", "z")
ALL = ("xh", "co", "y", "xl", "z")

ROWS = 256
CHANS = 256
GROUPS = 16
LENGTH = 1024
STRIP = 128
WIDE = LENGTH + STRIP
FEATS = 8192
TILE = 1024
SMALL = 64
TAIL = 16
VMEM_LIMIT = 56 * 1024 * 1024


def params(*semantics):
    return pltpu.CompilerParams(vmem_limit_bytes=VMEM_LIMIT)


def lane_groups(rows):
    return lax.broadcasted_iota(jnp.int32, (rows, CHANS), 1) // (CHANS // GROUPS)


def later(x, count):
    row = lax.broadcasted_iota(jnp.int32, x.shape, 0)
    return jnp.where(row >= count, pltpu.roll(x, count, 0), 0.0)


def strip_of(line):
    wide = jnp.broadcast_to(line, (STRIP, WIDE))
    return pltpu.roll(wide, 0, 1, stride=1, stride_axis=0)[:, :LENGTH].astype(BF16)


def pick_groups(result):
    ids = lane_groups(STRIP)
    out = jnp.zeros((STRIP, CHANS), F32)
    for g in range(GROUPS):
        out = jnp.where(ids == g, result[g * STRIP : (g + 1) * STRIP], out)
    return out


def with_tail(tail, block):
    joined = jnp.concatenate([tail, block], axis=0).astype(F32)
    return joined[TAIL:], pltpu.roll(joined, 1, 0)[TAIL:], pltpu.roll(joined, 2, 0)[TAIL:]


def short_sum(taps_ref, i, parts):
    return sum(taps_ref[3 * i + j : 3 * i + j + 1, :] * parts[j] for j in range(3))


def pre_kernel(cot_ref, weight_ref, line_ref, d_gated_ref, strips_ref, acc_ref):
    step = pl.program_id(0)

    @pl.when(step == 0)
    def _():
        acc_ref[...] = jnp.zeros_like(acc_ref)

    acc_ref[...] += jnp.dot(cot_ref[...], weight_ref[...], preferred_element_type=F32)
    for g in range(2):
        strips_ref[g * STRIP : (g + 1) * STRIP, :] = strip_of(line_ref[g])

    @pl.when(step == pl.num_programs(0) - 1)
    def _():
        d_gated_ref[...] = acc_ref[...].astype(BF16)


def pre_call(cot, weight, lines):
    steps = FEATS // TILE
    return pl.pallas_call(
        pre_kernel,
        grid=(steps,),
        in_specs=[
            pl.BlockSpec((ROWS, TILE), lambda i: (0, i)),
            pl.BlockSpec((TILE, CHANS), lambda i: (i, 0)),
            pl.BlockSpec((2, 1, WIDE), lambda i: (i, 0, 0)),
        ],
        out_specs=[
            pl.BlockSpec((ROWS, CHANS), lambda i: (0, 0)),
            pl.BlockSpec((2 * STRIP, LENGTH), lambda i: (i, 0)),
        ],
        out_shape=[
            jax.ShapeDtypeStruct((ROWS, CHANS), BF16),
            jax.ShapeDtypeStruct((GROUPS * STRIP, LENGTH), BF16),
        ],
        scratch_shapes=[pltpu.VMEM((ROWS, CHANS), F32)],
        compiler_params=params(),
        cost_estimate=pl.CostEstimate(
            flops=2 * ROWS * FEATS * CHANS, bytes_accessed=14 << 20, transcendentals=0
        ),
        name="pre",
    )(cot, weight, lines)


def d_inner_kernel(d_gated_ref, query_ref, tail_ref, taps_ref, out_ref):
    q_short = short_sum(taps_ref, 0, with_tail(tail_ref[...], query_ref[...]))
    out_ref[...] = (d_gated_ref[...].astype(F32) * q_short).astype(BF16)


def d_inner_call(d_gated, query, tail, taps):
    return pl.pallas_call(
        d_inner_kernel,
        out_shape=jax.ShapeDtypeStruct((ROWS, CHANS), BF16),
        compiler_params=params(),
        cost_estimate=pl.CostEstimate(flops=1 << 20, bytes_accessed=1 << 19, transcendentals=0),
        name="d_inner",
    )(d_gated, query, tail, taps)


def fwd_kernel(
    strips_ref, far_ref, mid_ref, near_ref, own_ref, query_ref, tail_ref, taps_ref, skip_ref,
    gated_ref, inner_ref, mixed_ref,
):
    both = jnp.concatenate([far_ref[...], mid_ref[...], near_ref[...], own_ref[...]], axis=0)
    both = both.astype(F32)
    shifted = (both, later(both, 1), later(both, 2))
    k_short = short_sum(taps_ref, 1, [part[:, :CHANS] for part in shifted])
    v_short = short_sum(taps_ref, 2, [part[:, CHANS:] for part in shifted])
    mixed = (k_short * v_short).astype(BF16)
    mixed_ref[...] = mixed[LENGTH - ROWS :]
    low = jnp.dot(strips_ref[:, STRIP:], mixed[: LENGTH - STRIP], preferred_element_type=F32)
    high = jnp.dot(strips_ref[...], mixed, preferred_element_type=F32)
    convolved = jnp.concatenate([pick_groups(low), pick_groups(high)], axis=0)
    inner = convolved + skip_ref[...] * mixed[LENGTH - ROWS :].astype(F32)
    inner_ref[...] = inner
    q_short = short_sum(taps_ref, 0, with_tail(tail_ref[...], query_ref[...]))
    gated_ref[...] = (q_short * inner).astype(BF16)


def fwd_call(strips, far, mid, near, own, query, tail, taps, skip):
    return pl.pallas_call(
        fwd_kernel,
        out_shape=[
            jax.ShapeDtypeStruct((ROWS, CHANS), BF16),
            jax.ShapeDtypeStruct((ROWS, CHANS), F32),
            jax.ShapeDtypeStruct((ROWS, CHANS), BF16),
        ],
        compiler_params=params(),
        cost_estimate=pl.CostEstimate(flops=4 << 30, bytes_accessed=6 << 20, transcendentals=0),
        name="fwd",
    )(strips, far, mid, near, own, query, tail, taps, skip)


def weight_kernel(core_ref, own_cot_ref, other_cot_ref, gated_ref, other_gated_ref, out_ref):
    dims = (((0,), (0,)), ((), ()))
    total = lax.dot_general(own_cot_ref[...], gated_ref[...], dims, preferred_element_type=F32)
    total += lax.dot_general(
        other_cot_ref[...], other_gated_ref[...], dims, preferred_element_type=F32
    )
    out_ref[...] = total.astype(BF16)


def weight_call(core, own_cot, other_cot, gated, other_gated):
    share = FEATS // 4 // TILE

    def column(i, core_ref):
        return (0, (i // share) * 2 * share + core_ref[0] * share + i % share)

    return pl.pallas_call(
        weight_kernel,
        grid_spec=pltpu.PrefetchScalarGridSpec(
            num_scalar_prefetch=1,
            grid=(2 * share,),
            in_specs=[
                pl.BlockSpec((ROWS, TILE), column),
                pl.BlockSpec((ROWS, TILE), column),
                pl.BlockSpec((ROWS, CHANS), lambda i, core_ref: (0, 0)),
                pl.BlockSpec((ROWS, CHANS), lambda i, core_ref: (0, 0)),
            ],
            out_specs=pl.BlockSpec((TILE, CHANS), lambda i, core_ref: (i, 0)),
        ),
        out_shape=jax.ShapeDtypeStruct((FEATS // 2, CHANS), BF16),
        compiler_params=params(),
        cost_estimate=pl.CostEstimate(
            flops=2 * ROWS * FEATS * CHANS, bytes_accessed=6 << 20, transcendentals=0
        ),
        name="weight_terms",
    )(core, own_cot, other_cot, gated, other_gated)


def bwd_kernel(
    d0_ref, d1_ref, d2_ref, d3_ref, line_ref, mixed_ref, own_ref, near_ref, query_ref, tail_ref,
    inner_ref, d_gated_ref, taps_ref, skip_ref,
    d_short_ref, filter_ref, small_ref,
    strips_ref, ahead_ref, outer_ref, stack_ref,
):
    for n, ref in enumerate((d0_ref, d1_ref, d2_ref, d3_ref)):
        ahead_ref[n * ROWS : (n + 1) * ROWS, :] = ref[...]
    ahead_ref[LENGTH:, :] = jnp.zeros((ROWS, CHANS), BF16)
    for g in range(GROUPS):
        strips_ref[g * STRIP : (g + 1) * STRIP, :] = strip_of(line_ref[g])
    low = jnp.dot(strips_ref[...], ahead_ref[:LENGTH, :], preferred_element_type=F32)
    d_mixed_low = pick_groups(low)
    high = jnp.dot(
        strips_ref[:, : LENGTH - STRIP], ahead_ref[STRIP:LENGTH, :], preferred_element_type=F32
    )
    d_mixed_high = pick_groups(high)
    d_inner = d0_ref[...].astype(F32)
    mixed = mixed_ref[...]
    d_mixed = jnp.concatenate([d_mixed_low, d_mixed_high], axis=0) + skip_ref[...] * d_inner

    k_parts = with_tail(near_ref[:, :CHANS], own_ref[:, :CHANS])
    v_parts = with_tail(near_ref[:, CHANS:], own_ref[:, CHANS:])
    q_parts = with_tail(tail_ref[...], query_ref[...])
    d_qs = d_gated_ref[...].astype(F32) * inner_ref[...]
    d_ks = d_mixed * short_sum(taps_ref, 2, v_parts)
    d_vs = d_mixed * short_sum(taps_ref, 1, k_parts)
    for i, (grad, parts) in enumerate(((d_qs, q_parts), (d_ks, k_parts), (d_vs, v_parts))):
        d_short_ref[i] = grad
        for j in range(3):
            small_ref[3 * i + j : 3 * i + j + 1, :] = jnp.sum(grad * parts[j], axis=0, keepdims=True)
    small_ref[9:10, :] = jnp.sum(d_inner * mixed.astype(F32), axis=0, keepdims=True)
    small_ref[10:, :] = jnp.zeros((6, CHANS), F32)

    row = lax.broadcasted_iota(jnp.int32, (ROWS, ROWS), 0)
    col = lax.broadcasted_iota(jnp.int32, (ROWS, ROWS), 1)
    turn = ((row // SMALL) * SMALL + (SMALL - 1 - row % SMALL) == col).astype(F32).astype(BF16)
    turned = jnp.dot(turn, mixed, preferred_element_type=F32)
    ids = lane_groups(SMALL)
    for part in range(ROWS // SMALL):
        piece = turned[part * SMALL : (part + 1) * SMALL]
        for g in range(GROUPS):
            stack_ref[g * SMALL : (g + 1) * SMALL, :] = jnp.where(ids == g, piece, 0.0).astype(BF16)
        term = lax.dot_general(
            stack_ref[...],
            ahead_ref[part * SMALL : part * SMALL + LENGTH, :],
            (((1,), (1,)), ((), ())),
            preferred_element_type=F32,
        )
        if part == 0:
            outer_ref[:, :LENGTH] = term
        else:
            outer_ref[:, :LENGTH] += term
    outer_ref[:, LENGTH:] = jnp.zeros((GROUPS * SMALL, STRIP), F32)
    for g in range(GROUPS):
        skewed = pltpu.roll(
            outer_ref[g * SMALL : (g + 1) * SMALL, :], WIDE - (SMALL - 1), 1, stride=1, stride_axis=0
        )
        filter_ref[g : g + 1, :] = jnp.sum(skewed[:, :LENGTH], axis=0, keepdims=True)


def bwd_call(blocks, lines, mixed, own, near, query, tail, inner, d_gated, taps, skip):
    whole = lambda shape: pl.BlockSpec(shape, lambda i: (0,) * len(shape))
    operands = (*blocks, lines, mixed, own, near, query, tail, inner, d_gated, taps, skip)
    specs = [whole(x.shape) for x in operands]
    specs[7] = pl.BlockSpec((TAIL, 2 * CHANS), lambda i: (ROWS // TAIL - 1, 0))
    return pl.pallas_call(
        bwd_kernel,
        grid=(1,),
        in_specs=specs,
        out_specs=[whole((3, ROWS, CHANS)), whole((GROUPS, LENGTH)), whole((16, CHANS))],
        out_shape=[
            jax.ShapeDtypeStruct((3, ROWS, CHANS), F32),
            jax.ShapeDtypeStruct((GROUPS, LENGTH), F32),
            jax.ShapeDtypeStruct((16, CHANS), F32),
        ],
        scratch_shapes=[
            pltpu.VMEM((GROUPS * STRIP, LENGTH), BF16),
            pltpu.VMEM((LENGTH + ROWS, CHANS), BF16),
            pltpu.VMEM((GROUPS * SMALL, WIDE), F32),
            pltpu.VMEM((GROUPS * SMALL, CHANS), BF16),
        ],
        compiler_params=params(),
        cost_estimate=pl.CostEstimate(flops=12 << 30, bytes_accessed=4 << 20, transcendentals=0),
        name="bwd",
    )(*operands)


def input_grad_kernel(d_short_ref, next_ref, taps_ref, query_ref, key_ref, value_ref):
    for i, out_ref in enumerate((query_ref, key_ref, value_ref)):
        joined = jnp.concatenate([d_short_ref[i], next_ref[i]], axis=0)
        rows = joined.shape[0]
        parts = (
            joined[:ROWS],
            pltpu.roll(joined, rows - 1, 0)[:ROWS],
            pltpu.roll(joined, rows - 2, 0)[:ROWS],
        )
        out_ref[...] = short_sum(taps_ref, i, parts).astype(BF16)


def input_grad_call(d_short, following, taps):
    return pl.pallas_call(
        input_grad_kernel,
        out_shape=[jax.ShapeDtypeStruct((ROWS, CHANS), BF16)] * 3,
        compiler_params=params(),
        cost_estimate=pl.CostEstimate(flops=1 << 20, bytes_accessed=2 << 20, transcendentals=0),
        name="input_grads",
    )(d_short, following, taps)


def total_kernel(scale, terms_ref, out_ref):
    total = (jnp.sum(terms_ref[...].astype(F32), axis=0) * scale).astype(BF16)
    out_ref[...] = jnp.broadcast_to(total[None], out_ref.shape)


def total_call(terms, copies, scale):
    return pl.pallas_call(
        lambda *refs: total_kernel(scale, *refs),
        out_shape=jax.ShapeDtypeStruct((copies, *terms.shape[1:]), BF16),
        compiler_params=params(),
        cost_estimate=pl.CostEstimate(flops=1 << 20, bytes_accessed=3 << 20, transcendentals=0),
        name="weight_total",
    )(terms)


def sent(block, distance):
    count = 4
    route = [(i, i + distance) for i in range(count) if 0 <= i + distance < count]
    return lax.ppermute(block, CTX, route)


def shards(
    query_in, key_in, value_in, short_taps, long_filter, skip_gain, out_weight, out_cotangent
):
    query = query_in[0]
    cot = out_cotangent[0]
    taps = short_taps.reshape(9, CHANS)
    skip = skip_gain.reshape(1, CHANS)
    devices = lax.axis_size(ALL)
    tokens = ROWS * devices
    scale = 1.0 / math.sqrt(tokens)
    core = lax.axis_index("co").astype(jnp.int32).reshape(1)

    own = jnp.concatenate([key_in[0], value_in[0]], axis=1)
    near, mid, far = (sent(own, distance) for distance in (1, 2, 3))
    tail = sent(query[ROWS - TAIL :], 1)
    swap = [(0, 1), (1, 0)]
    other_cot = lax.ppermute(cot, "co", swap)

    lags = long_filter.astype(F32)
    pad = jnp.zeros((GROUPS, STRIP), F32)
    back_lines = jnp.concatenate([lags, pad], axis=1)[:, None, :]
    turned = lags[:, ::-1]
    lines = jnp.concatenate([turned[:, STRIP - 1 :], pad, turned[:, : STRIP - 1]], axis=1)[:, None, :]

    d_gated, strips = pre_call(cot, out_weight, lines)
    d_inner = d_inner_call(d_gated, query, tail, taps)
    blocks = [d_inner] + [sent(d_inner, -distance) for distance in (1, 2, 3)]

    gated, inner, mixed = fwd_call(strips, far, mid, near, own, query, tail, taps, skip)
    other_gated = lax.ppermute(gated, "co", swap)
    terms = weight_call(core, cot, other_cot, gated, other_gated)
    chips = devices // 2
    terms = terms.reshape(chips, FEATS // 2 // chips, CHANS)
    terms = lax.all_to_all(terms, CHIPS, 0, 0)

    d_short, filter_part, small_part = bwd_call(
        blocks, back_lines, mixed, own, near, query, tail, inner, d_gated, taps, skip
    )
    following = sent(d_short[:, :8], -1)
    grad_query, grad_key, grad_value = input_grad_call(d_short, following, taps)

    filter_rows = GROUPS * LENGTH // CHANS
    rows = jnp.concatenate([filter_part.reshape(filter_rows, CHANS), small_part], axis=0)
    rows = jnp.pad(rows, ((0, devices - rows.shape[0]), (0, 0)))
    rows = lax.all_to_all(rows.reshape(devices, 1, CHANS), ALL, 0, 0)
    total = jnp.sum(rows, axis=0, keepdims=True) * scale
    rows = lax.all_to_all(jnp.broadcast_to(total, (devices, 1, CHANS)), ALL, 0, 0)
    rows = rows.reshape(devices, CHANS)
    grad_filter = rows[:filter_rows].reshape(GROUPS, LENGTH)
    grad_taps = rows[filter_rows : filter_rows + 9].reshape(3, 3, CHANS)
    grad_skip = rows[filter_rows + 9]

    copies = lax.axis_size(DP)
    shares = lax.all_to_all(total_call(terms, copies, scale), DP, 0, 0)
    grad_weight = shares.reshape(FEATS // 4, CHANS).astype(F32)
    return (
        gated[None],
        grad_query[None],
        grad_key[None],
        grad_value[None],
        grad_taps,
        grad_filter,
        grad_skip,
        grad_weight,
    )


def solution(mesh):
    fine = Mesh(mesh.devices.reshape(2, 2, 4, 2, 4), ALL)
    tokens = P(DP, CTX, None)
    in_specs = (tokens, tokens, tokens, P(), P(), P(), P(), tokens)
    out_specs = (tokens, tokens, tokens, tokens, P(), P(), P(), P(CTX, None))
    return jax.shard_map(
        shards, mesh=fine, in_specs=in_specs, out_specs=out_specs, check_vma=False
    )
```

```python
import math

import jax
import jax.numpy as jnp
from jax import lax
from jax.experimental import pallas as pl
from jax.experimental.pallas import tpu as pltpu
from jax.sharding import Mesh
from jax.sharding import PartitionSpec as P

F32 = jnp.float32
BF16 = jnp.bfloat16
CTX = ("xh", "co")
DP = ("y", "xl", "z")
CHIPS = ("xh", "y", "xl", "z")
ALL = ("xh", "co", "y", "xl", "z")

ROWS = 256
CHANS = 256
GROUPS = 16
LENGTH = 1024
STRIP = 128
WIDE = LENGTH + STRIP
FEATS = 8192
TILE = 1024
SMALL = 64
TAIL = 16
SHARES = 32
FIRST = 48
SECOND = 16
SEGMENT = 8
FWD_GROUPS = 4
VMEM_LIMIT = 56 * 1024 * 1024


def params(*semantics):
    return pltpu.CompilerParams(vmem_limit_bytes=VMEM_LIMIT)


def lane_groups(rows):
    return lax.broadcasted_iota(jnp.int32, (rows, CHANS), 1) // (CHANS // GROUPS)


def later(x, count):
    row = lax.broadcasted_iota(jnp.int32, x.shape, 0)
    return jnp.where(row >= count, pltpu.roll(x, count, 0), 0.0)


def strip_of(line):
    wide = jnp.broadcast_to(line, (STRIP, WIDE))
    return pltpu.roll(wide, 0, 1, stride=1, stride_axis=0)[:, :LENGTH].astype(BF16)


def pick_groups(result, first=0, out=None):
    ids = lane_groups(STRIP)
    if out is None:
        out = jnp.zeros((STRIP, CHANS), F32)
    for g in range(result.shape[0] // STRIP):
        out = jnp.where(ids == first + g, result[g * STRIP : (g + 1) * STRIP], out)
    return out


def with_tail(tail, block):
    joined = jnp.concatenate([tail, block], axis=0).astype(F32)
    return joined[TAIL:], pltpu.roll(joined, 1, 0)[TAIL:], pltpu.roll(joined, 2, 0)[TAIL:]


def short_sum(taps_ref, i, parts):
    return sum(taps_ref[i, j : j + 1, :] * parts[j] for j in range(3))


def pack_kernel(key_ref, value_ref, query_ref, out_ref):
    out_ref[:ROWS, :CHANS] = key_ref[...]
    out_ref[:ROWS, CHANS:] = value_ref[...]
    out_ref[ROWS:, :CHANS] = query_ref[...]
    out_ref[ROWS:, CHANS:] = query_ref[...]


def pack_call(key, value, query):
    whole = pl.BlockSpec((ROWS, CHANS), lambda i: (0, 0))
    return pl.pallas_call(
        pack_kernel,
        grid=(1,),
        in_specs=[whole, whole, pl.BlockSpec((TAIL, CHANS), lambda i: (ROWS // TAIL - 1, 0))],
        out_specs=pl.BlockSpec((ROWS + TAIL, 2 * CHANS), lambda i: (0, 0)),
        out_shape=jax.ShapeDtypeStruct((ROWS + TAIL, 2 * CHANS), BF16),
        compiler_params=params(),
        name="pack",
    )(key, value, query)


def lines_of(filter_ref, turned):
    if not turned:
        return jnp.concatenate(
            [filter_ref[...].astype(F32), jnp.zeros((GROUPS, STRIP), F32)], axis=1
        )
    row = lax.broadcasted_iota(jnp.int32, (CHANS, CHANS), 0)
    col = lax.broadcasted_iota(jnp.int32, (CHANS, CHANS), 1)
    turn = (row + col == CHANS - 1).astype(F32).astype(BF16)
    pieces = [
        jnp.dot(filter_ref[:, n * CHANS : (n + 1) * CHANS], turn, preferred_element_type=F32)
        for n in reversed(range(LENGTH // CHANS))
    ]
    wide = jnp.concatenate([*pieces, jnp.zeros((GROUPS, STRIP), F32)], axis=1)
    return pltpu.roll(wide, WIDE - (STRIP - 1), 1)


def pre_kernel(cot_ref, weight_ref, filter_ref, d_gated_ref, strips_ref, acc_ref, line_ref):
    step = pl.program_id(0)

    @pl.when(step == 0)
    def _():
        acc_ref[...] = jnp.zeros_like(acc_ref)
        line_ref[...] = lines_of(filter_ref, True)

    acc_ref[...] += jnp.dot(cot_ref[...], weight_ref[...], preferred_element_type=F32)
    for g in range(2):
        line = line_ref[pl.ds(2 * step + g, 1), :]
        strips_ref[g * STRIP : (g + 1) * STRIP, :] = strip_of(line)

    @pl.when(step == pl.num_programs(0) - 1)
    def _():
        d_gated_ref[...] = acc_ref[...].astype(BF16)


def pre_call(cot, weight, lags):
    steps = FEATS // TILE
    return pl.pallas_call(
        pre_kernel,
        grid=(steps,),
        in_specs=[
            pl.BlockSpec((ROWS, TILE), lambda i: (0, i)),
            pl.BlockSpec((TILE, CHANS), lambda i: (i, 0)),
            pl.BlockSpec((GROUPS, LENGTH), lambda i: (0, 0)),
        ],
        out_specs=[
            pl.BlockSpec((ROWS, CHANS), lambda i: (0, 0)),
            pl.BlockSpec((2 * STRIP, LENGTH), lambda i: (i, 0)),
        ],
        out_shape=[
            jax.ShapeDtypeStruct((ROWS, CHANS), BF16),
            jax.ShapeDtypeStruct((GROUPS * STRIP, LENGTH), BF16),
        ],
        scratch_shapes=[pltpu.VMEM((ROWS, CHANS), F32), pltpu.VMEM((GROUPS, WIDE), F32)],
        compiler_params=params(),
        cost_estimate=pl.CostEstimate(
            flops=2 * ROWS * FEATS * CHANS, bytes_accessed=14 << 20, transcendentals=0
        ),
        name="pre",
    )(cot, weight, lags)


def d_inner_kernel(d_gated_ref, query_ref, tail_ref, taps_ref, out_ref):
    q_short = short_sum(taps_ref, 0, with_tail(tail_ref[...], query_ref[...]))
    out_ref[...] = (d_gated_ref[...].astype(F32) * q_short).astype(BF16)


def d_inner_call(d_gated, query, near, taps):
    whole = pl.BlockSpec((ROWS, CHANS), lambda i: (0, 0))
    return pl.pallas_call(
        d_inner_kernel,
        grid=(1,),
        in_specs=[
            whole,
            whole,
            pl.BlockSpec((TAIL, CHANS), lambda i: (ROWS // TAIL, 0)),
            pl.BlockSpec((3, 3, CHANS), lambda i: (0, 0, 0)),
        ],
        out_specs=whole,
        out_shape=jax.ShapeDtypeStruct((ROWS, CHANS), BF16),
        compiler_params=params(),
        cost_estimate=pl.CostEstimate(flops=1 << 20, bytes_accessed=1 << 19, transcendentals=0),
        name="d_inner",
    )(d_gated, query, near, taps)


def fwd_kernel(
    strips_ref, far_ref, mid_ref, near_ref, own_ref, query_ref, taps_ref, skip_ref,
    gated_ref, inner_ref, mixed_ref,
    signal_ref, conv_ref,
):
    step = pl.program_id(0)

    @pl.when(step == 0)
    def _():
        both = [ref[:ROWS, :] for ref in (far_ref, mid_ref, near_ref, own_ref)]
        both = jnp.concatenate(both, axis=0).astype(F32)
        shifted = (both, later(both, 1), later(both, 2))
        k_short = short_sum(taps_ref, 1, [part[:, :CHANS] for part in shifted])
        v_short = short_sum(taps_ref, 2, [part[:, CHANS:] for part in shifted])
        mixed = (k_short * v_short).astype(BF16)
        signal_ref[...] = mixed
        mixed_ref[...] = mixed[LENGTH - ROWS :]
        conv_ref[...] = jnp.zeros_like(conv_ref)

    low = jnp.dot(
        strips_ref[:, STRIP:], signal_ref[: LENGTH - STRIP, :], preferred_element_type=F32
    )
    high = jnp.dot(strips_ref[...], signal_ref[...], preferred_element_type=F32)
    conv_ref[:STRIP, :] = pick_groups(low, step * FWD_GROUPS, conv_ref[:STRIP, :])
    conv_ref[STRIP:, :] = pick_groups(high, step * FWD_GROUPS, conv_ref[STRIP:, :])

    @pl.when(step == pl.num_programs(0) - 1)
    def _():
        inner = conv_ref[...] + skip_ref[...] * mixed_ref[...].astype(F32)
        inner_ref[...] = inner
        q_short = short_sum(taps_ref, 0, with_tail(near_ref[ROWS:, :CHANS], query_ref[...]))
        gated_ref[...] = (q_short * inner).astype(BF16)


def fwd_call(strips, far, mid, near, own, query, taps, skip):
    whole = lambda x: pl.BlockSpec(x.shape, lambda i: (0,) * x.ndim)
    rest = (far, mid, near, own, query, taps, skip)
    out = pl.BlockSpec((ROWS, CHANS), lambda i: (0, 0))
    return pl.pallas_call(
        fwd_kernel,
        grid=(GROUPS // FWD_GROUPS,),
        in_specs=[
            pl.BlockSpec((FWD_GROUPS * STRIP, LENGTH), lambda i: (i, 0)),
            *(whole(x) for x in rest),
        ],
        out_specs=[out] * 3,
        out_shape=[
            jax.ShapeDtypeStruct((ROWS, CHANS), BF16),
            jax.ShapeDtypeStruct((ROWS, CHANS), F32),
            jax.ShapeDtypeStruct((ROWS, CHANS), BF16),
        ],
        scratch_shapes=[pltpu.VMEM((LENGTH, CHANS), BF16), pltpu.VMEM((ROWS, CHANS), F32)],
        compiler_params=params(),
        cost_estimate=pl.CostEstimate(flops=4 << 30, bytes_accessed=6 << 20, transcendentals=0),
        name="fwd",
    )(strips, *rest)


def term_tile(own_cot_ref, other_cot_ref, gated_ref, other_gated_ref):
    dims = (((0,), (0,)), ((), ()))
    total = lax.dot_general(own_cot_ref[...], gated_ref[...], dims, preferred_element_type=F32)
    total += lax.dot_general(
        other_cot_ref[...], other_gated_ref[...], dims, preferred_element_type=F32
    )
    return total.astype(BF16)


def first_kernel(core_ref, own_cot_ref, other_cot_ref, gated_ref, other_gated_ref, out_ref):
    out_ref[...] = term_tile(own_cot_ref, other_cot_ref, gated_ref, other_gated_ref)


def two_parts(total):
    rounded = total.astype(BF16).astype(F32)
    left = pltpu.roll(total - rounded, SEGMENT // 2, total.ndim - 2)
    return (rounded + left).astype(BF16)


def second_kernel(
    core_ref, own_cot_ref, other_cot_ref, gated_ref, other_gated_ref, small_ref, other_small_ref,
    out_ref,
):
    tile = term_tile(own_cot_ref, other_cot_ref, gated_ref, other_gated_ref)
    out_ref[:, :SECOND, :] = tile.reshape(SHARES, SECOND, CHANS)
    out_ref[:, SECOND:, :] = two_parts(small_ref[...] + other_small_ref[...])


def weight_call(core, own_cot, other_cot, gated, other_gated, small=None, other_small=None):
    tile = SHARES * SECOND
    share = FEATS // 4 // tile
    first = small is None
    steps = FIRST // SECOND if first else 1
    skipped = 0 if first else FIRST // SECOND

    def column(i, core_ref):
        return (0, (i // steps) * 2 * share + core_ref[0] * share + skipped + i % steps)

    signal = pl.BlockSpec((ROWS, CHANS), lambda i, core_ref: (0, 0))
    specs = [pl.BlockSpec((ROWS, tile), column)] * 2 + [signal] * 2
    operands = (core, own_cot, other_cot, gated, other_gated)
    if first:
        out_spec = pl.BlockSpec((tile, CHANS), lambda i, core_ref: (i, 0))
        out_shape = jax.ShapeDtypeStruct((2 * SHARES * FIRST, CHANS), BF16)
    else:
        specs += [pl.BlockSpec((SHARES, SEGMENT, CHANS), lambda i, core_ref: (0, 0, 0))] * 2
        operands += (small, other_small)
        out_spec = pl.BlockSpec((SHARES, SECOND + SEGMENT, CHANS), lambda i, core_ref: (i, 0, 0))
        out_shape = jax.ShapeDtypeStruct((2 * SHARES, SECOND + SEGMENT, CHANS), BF16)
    out = pl.pallas_call(
        first_kernel if first else second_kernel,
        grid_spec=pltpu.PrefetchScalarGridSpec(
            num_scalar_prefetch=1, grid=(2 * steps,), in_specs=specs, out_specs=out_spec
        ),
        out_shape=out_shape,
        compiler_params=params(),
        cost_estimate=pl.CostEstimate(flops=1 << 10, bytes_accessed=1 << 10, transcendentals=0),
        name="first_terms" if first else "second_terms",
    )(*operands)
    return out.reshape(2 * SHARES, FIRST, CHANS) if first else out


def place(g, n):
    row = g * (LENGTH // CHANS) + n
    return row % SHARES, row // SHARES


def bwd_kernel(
    d0_ref, d1_ref, d2_ref, d3_ref, lags_ref, mixed_ref, own_ref, near_ref, query_ref, inner_ref,
    d_gated_ref, taps_ref, skip_ref,
    d_short_ref, small_ref,
    strips_ref, ahead_ref, outer_ref, stack_ref,
):
    for n, ref in enumerate((d0_ref, d1_ref, d2_ref, d3_ref)):
        ahead_ref[n * ROWS : (n + 1) * ROWS, :] = ref[...]
    ahead_ref[LENGTH:, :] = jnp.zeros((ROWS, CHANS), BF16)
    lines = lines_of(lags_ref, False)
    for g in range(GROUPS):
        strips_ref[g * STRIP : (g + 1) * STRIP, :] = strip_of(lines[g : g + 1])
    low = jnp.dot(strips_ref[...], ahead_ref[:LENGTH, :], preferred_element_type=F32)
    d_mixed_low = pick_groups(low)
    high = jnp.dot(
        strips_ref[:, : LENGTH - STRIP], ahead_ref[STRIP:LENGTH, :], preferred_element_type=F32
    )
    d_mixed_high = pick_groups(high)
    d_inner = d0_ref[...].astype(F32)
    mixed = mixed_ref[...]
    d_mixed = jnp.concatenate([d_mixed_low, d_mixed_high], axis=0) + skip_ref[...] * d_inner

    last = near_ref[ROWS - TAIL : ROWS, :]
    k_parts = with_tail(last[:, :CHANS], own_ref[:ROWS, :CHANS])
    v_parts = with_tail(last[:, CHANS:], own_ref[:ROWS, CHANS:])
    q_parts = with_tail(near_ref[ROWS:, :CHANS], query_ref[...])
    small_ref[...] = jnp.zeros_like(small_ref)
    d_qs = d_gated_ref[...].astype(F32) * inner_ref[...]
    d_ks = d_mixed * short_sum(taps_ref, 2, v_parts)
    d_vs = d_mixed * short_sum(taps_ref, 1, k_parts)
    for i, (grad, parts) in enumerate(((d_qs, q_parts), (d_ks, k_parts), (d_vs, v_parts))):
        d_short_ref[i] = grad
        for j in range(3):
            small_ref[3 * i + j, 2:3, :] = jnp.sum(grad * parts[j], axis=0, keepdims=True)
    small_ref[9, 2:3, :] = jnp.sum(d_inner * mixed.astype(F32), axis=0, keepdims=True)

    row = lax.broadcasted_iota(jnp.int32, (ROWS, ROWS), 0)
    col = lax.broadcasted_iota(jnp.int32, (ROWS, ROWS), 1)
    turn = ((row // SMALL) * SMALL + (SMALL - 1 - row % SMALL) == col).astype(F32).astype(BF16)
    turned = jnp.dot(turn, mixed, preferred_element_type=F32)
    ids = lane_groups(SMALL)
    for part in range(ROWS // SMALL):
        piece = turned[part * SMALL : (part + 1) * SMALL]
        for g in range(GROUPS):
            stack_ref[g * SMALL : (g + 1) * SMALL, :] = jnp.where(ids == g, piece, 0.0).astype(BF16)
        term = lax.dot_general(
            stack_ref[...],
            ahead_ref[part * SMALL : part * SMALL + LENGTH, :],
            (((1,), (1,)), ((), ())),
            preferred_element_type=F32,
        )
        if part == 0:
            outer_ref[:, :LENGTH] = term
        else:
            outer_ref[:, :LENGTH] += term
    outer_ref[:, LENGTH:] = jnp.zeros((GROUPS * SMALL, STRIP), F32)
    for g in range(GROUPS):
        skewed = pltpu.roll(
            outer_ref[g * SMALL : (g + 1) * SMALL, :], WIDE - (SMALL - 1), 1, stride=1, stride_axis=0
        )
        sums = jnp.sum(skewed[:, :LENGTH], axis=0, keepdims=True)
        for n in range(LENGTH // CHANS):
            share, slot = place(g, n)
            small_ref[share, slot : slot + 1, :] = sums[:, n * CHANS : (n + 1) * CHANS]


def bwd_call(blocks, lags, mixed, own, near, query, inner, d_gated, taps, skip):
    whole = lambda shape: pl.BlockSpec(shape, lambda i: (0,) * len(shape))
    operands = (*blocks, lags, mixed, own, near, query, inner, d_gated, taps, skip)
    specs = [whole(x.shape) for x in operands]
    return pl.pallas_call(
        bwd_kernel,
        grid=(1,),
        in_specs=specs,
        out_specs=[whole((3, ROWS, CHANS)), whole((SHARES, SEGMENT, CHANS))],
        out_shape=[
            jax.ShapeDtypeStruct((3, ROWS, CHANS), F32),
            jax.ShapeDtypeStruct((SHARES, SEGMENT, CHANS), F32),
        ],
        scratch_shapes=[
            pltpu.VMEM((GROUPS * STRIP, LENGTH), BF16),
            pltpu.VMEM((LENGTH + ROWS, CHANS), BF16),
            pltpu.VMEM((GROUPS * SMALL, WIDE), F32),
            pltpu.VMEM((GROUPS * SMALL, CHANS), BF16),
        ],
        compiler_params=params(),
        cost_estimate=pl.CostEstimate(flops=1 << 10, bytes_accessed=1 << 10, transcendentals=0),
        name="bwd",
    )(*operands)


def input_grad_kernel(d_short_ref, next_ref, taps_ref, query_ref, key_ref, value_ref):
    for i, out_ref in enumerate((query_ref, key_ref, value_ref)):
        joined = jnp.concatenate([d_short_ref[i], next_ref[i]], axis=0)
        rows = joined.shape[0]
        parts = (
            joined[:ROWS],
            pltpu.roll(joined, rows - 1, 0)[:ROWS],
            pltpu.roll(joined, rows - 2, 0)[:ROWS],
        )
        out_ref[...] = short_sum(taps_ref, i, parts).astype(BF16)


def input_grad_call(d_short, following, taps):
    return pl.pallas_call(
        input_grad_kernel,
        out_shape=[jax.ShapeDtypeStruct((ROWS, CHANS), BF16)] * 3,
        compiler_params=params(),
        cost_estimate=pl.CostEstimate(flops=1 << 20, bytes_accessed=2 << 20, transcendentals=0),
        name="input_grads",
    )(d_short, following, taps)


def first_total_kernel(scale, terms_ref, out_ref):
    out_ref[...] = jnp.sum(terms_ref[...].astype(F32), axis=0) * scale


def first_total_call(terms, scale):
    return pl.pallas_call(
        lambda *refs: first_total_kernel(scale, *refs),
        out_shape=jax.ShapeDtypeStruct((FIRST, CHANS), F32),
        compiler_params=params(),
        cost_estimate=pl.CostEstimate(flops=1 << 10, bytes_accessed=1 << 10, transcendentals=0),
        name="first_total",
    )(terms)


def total_kernel(scale, first_ref, terms_ref, out_ref):
    total = jnp.sum(terms_ref[...].astype(F32), axis=0) * scale
    small = total[SECOND:]
    row = lax.broadcasted_iota(jnp.int32, small.shape, 0)
    small = jnp.where(row < SEGMENT // 2, small + pltpu.roll(small, SEGMENT // 2, 0), 0.0)
    total = jnp.concatenate(
        [first_ref[...].astype(BF16), total[:SECOND].astype(BF16), two_parts(small)], axis=0
    )
    out_ref[...] = jnp.broadcast_to(total[None], out_ref.shape)


def total_call(first, terms, scale):
    rows = FIRST + SECOND + SEGMENT
    return pl.pallas_call(
        lambda *refs: total_kernel(scale, *refs),
        out_shape=jax.ShapeDtypeStruct((SHARES, rows, CHANS), BF16),
        compiler_params=params(),
        cost_estimate=pl.CostEstimate(flops=1 << 20, bytes_accessed=3 << 20, transcendentals=0),
        name="second_total",
    )(first, terms)


def spread_kernel(shares_ref, weight_ref, taps_ref, filter_ref, skip_ref):
    for n in range(SHARES):
        weight_ref[n * FIRST : (n + 1) * FIRST, :] = shares_ref[n, :FIRST, :].astype(F32)
        start = SHARES * FIRST + n * SECOND
        weight_ref[start : start + SECOND, :] = shares_ref[n, FIRST : FIRST + SECOND, :].astype(F32)

    def small(share):
        segment = shares_ref[share, FIRST + SECOND :, :].astype(F32)
        return segment + pltpu.roll(segment, SEGMENT // 2, 0)

    for share in range(SHARES):
        segment = small(share)
        for g in range(GROUPS):
            for n in range(LENGTH // CHANS):
                if place(g, n)[0] == share:
                    slot = place(g, n)[1]
                    filter_ref[g : g + 1, n * CHANS : (n + 1) * CHANS] = segment[slot : slot + 1]
        if share < 9:
            taps_ref[share // 3, share % 3 : share % 3 + 1, :] = segment[2:3]
        if share == 9:
            skip_ref[...] = segment[2:3]


def spread_call(shares):
    return pl.pallas_call(
        spread_kernel,
        out_shape=[
            jax.ShapeDtypeStruct((FEATS // 4, CHANS), F32),
            jax.ShapeDtypeStruct((3, 3, CHANS), F32),
            jax.ShapeDtypeStruct((GROUPS, LENGTH), F32),
            jax.ShapeDtypeStruct((1, CHANS), F32),
        ],
        compiler_params=params(),
        name="spread",
    )(shares)


def sent(block, distance):
    count = 4
    route = [(i, i + distance) for i in range(count) if 0 <= i + distance < count]
    return lax.ppermute(block, CTX, route)


def shards(
    query_in, key_in, value_in, short_taps, long_filter, skip_gain, out_weight, out_cotangent
):
    query = query_in[0]
    cot = out_cotangent[0]
    taps = short_taps
    skip = skip_gain.reshape(1, CHANS)
    devices = lax.axis_size(ALL)
    tokens = ROWS * devices
    scale = 1.0 / math.sqrt(tokens)
    core = lax.axis_index("co").astype(jnp.int32).reshape(1)

    own = pack_call(key_in[0], value_in[0], query)
    near, mid, far = (sent(own, distance) for distance in (1, 2, 3))
    swap = [(0, 1), (1, 0)]
    other_cot = lax.ppermute(cot, "co", swap)

    d_gated, strips = pre_call(cot, out_weight, long_filter)
    gated, inner, mixed = fwd_call(strips, far, mid, near, own, query, taps, skip)
    gated, d_gated = lax.optimization_barrier((gated, d_gated))
    other_gated = lax.ppermute(gated, "co", swap)
    d_inner = d_inner_call(d_gated, query, near, taps)
    operands = (core, cot, other_cot, gated, other_gated)
    first = weight_call(*operands)
    first, d_inner = lax.optimization_barrier((first, d_inner))
    first = lax.all_to_all(first, CHIPS, 0, 0)
    blocks = [d_inner] + [sent(d_inner, -distance) for distance in (1, 2, 3)]
    d_short, small = bwd_call(
        blocks, long_filter, mixed, own, near, query, inner, d_gated, taps, skip
    )
    other_small = lax.ppermute(small, "co", swap)
    second = weight_call(*operands, small, other_small)
    second = lax.all_to_all(second, CHIPS, 0, 0)
    first = first_total_call(first, scale)
    following = sent(d_short[:, :8], -1)
    grad_query, grad_key, grad_value = input_grad_call(d_short, following, taps)

    shares = lax.all_to_all(total_call(first, second, scale), DP, 0, 0)
    grad_weight, grad_taps, grad_filter, grad_skip = spread_call(shares)
    return (
        gated[None],
        grad_query[None],
        grad_key[None],
        grad_value[None],
        grad_taps,
        grad_filter,
        grad_skip.reshape(CHANS),
        grad_weight,
    )


def solution(mesh):
    fine = Mesh(mesh.devices.reshape(2, 2, 4, 2, 4), ALL)
    tokens = P(DP, CTX, None)
    in_specs = (tokens, tokens, tokens, P(), P(), P(), P(), tokens)
    out_specs = (tokens, tokens, tokens, tokens, P(), P(), P(), P(CTX, None))
    return jax.shard_map(
        shards, mesh=fine, in_specs=in_specs, out_specs=out_specs, check_vma=False
    )
```

```python
import math

import jax
import jax.numpy as jnp
from jax import lax
from jax.experimental import pallas as pl
from jax.experimental.pallas import tpu as pltpu
from jax.sharding import Mesh
from jax.sharding import PartitionSpec as P

F32 = jnp.float32
BF16 = jnp.bfloat16
CTX = ("xh", "co")
DP = ("y", "xl", "z")
CHIPS = ("xh", "y", "xl", "z")
ALL = ("xh", "co", "y", "xl", "z")

ROWS = 256
CHANS = 256
GROUPS = 16
LENGTH = 1024
STRIP = 32
PAD = 128
WIDE = LENGTH + PAD
FEATS = 8192
TILE = 1024
SMALL = 32
TAIL = 16
SHARES = 32
SHARE = FEATS // 4
SEGMENT = 8
VMEM_LIMIT = 56 * 1024 * 1024


def params(*semantics):
    return pltpu.CompilerParams(vmem_limit_bytes=VMEM_LIMIT)


def lane_groups(rows):
    return lax.broadcasted_iota(jnp.int32, (rows, CHANS), 1) // (CHANS // GROUPS)


def later(x, count):
    row = lax.broadcasted_iota(jnp.int32, x.shape, 0)
    return jnp.where(row >= count, pltpu.roll(x, count, 0), 0.0)


def strip_of(line):
    wide = jnp.broadcast_to(line, (STRIP, WIDE))
    return pltpu.roll(wide, 0, 1, stride=1, stride_axis=0)[:, :LENGTH].astype(BF16)


def pick_groups(result):
    ids = lane_groups(STRIP)
    out = jnp.zeros((STRIP, CHANS), F32)
    for g in range(GROUPS):
        out = jnp.where(ids == g, result[g * STRIP : (g + 1) * STRIP], out)
    return out


def all_strips(strips_ref, signal_ref):
    parts = []
    for n in range(ROWS // STRIP):
        window = signal_ref[n * STRIP : n * STRIP + LENGTH, :]
        parts.append(pick_groups(jnp.dot(strips_ref[...], window, preferred_element_type=F32)))
    return jnp.concatenate(parts, axis=0)


def with_tail(tail, block):
    joined = jnp.concatenate([tail.astype(F32), block.astype(F32)], axis=0)
    return joined[TAIL:], pltpu.roll(joined, 1, 0)[TAIL:], pltpu.roll(joined, 2, 0)[TAIL:]


def short_sum(taps_ref, i, parts):
    return sum(taps_ref[i, j : j + 1, :] * parts[j] for j in range(3))


def lines_of(filter_ref, turned):
    if not turned:
        return jnp.concatenate(
            [filter_ref[...].astype(F32), jnp.zeros((GROUPS, PAD), F32)], axis=1
        )
    row = lax.broadcasted_iota(jnp.int32, (CHANS, CHANS), 0)
    col = lax.broadcasted_iota(jnp.int32, (CHANS, CHANS), 1)
    turn = (row + col == CHANS - 1).astype(F32).astype(BF16)
    pieces = [
        jnp.dot(filter_ref[:, n * CHANS : (n + 1) * CHANS], turn, preferred_element_type=F32)
        for n in reversed(range(LENGTH // CHANS))
    ]
    wide = jnp.concatenate([*pieces, jnp.zeros((GROUPS, PAD), F32)], axis=1)
    return pltpu.roll(wide, WIDE - (STRIP - 1), 1)


def pre_kernel(cot_ref, weight_ref, filter_ref, d_gated_ref, strips_ref, acc_ref, line_ref):
    step = pl.program_id(0)

    @pl.when(step == 0)
    def _():
        acc_ref[...] = jnp.zeros_like(acc_ref)
        line_ref[...] = lines_of(filter_ref, True)

    acc_ref[...] += jnp.dot(cot_ref[...], weight_ref[...], preferred_element_type=F32)
    for g in range(2):
        line = line_ref[pl.ds(2 * step + g, 1), :]
        strips_ref[g * STRIP : (g + 1) * STRIP, :] = strip_of(line)

    @pl.when(step == pl.num_programs(0) - 1)
    def _():
        d_gated_ref[...] = acc_ref[...].astype(BF16)


def pre_call(cot, weight, lags):
    steps = FEATS // TILE
    return pl.pallas_call(
        pre_kernel,
        grid=(steps,),
        in_specs=[
            pl.BlockSpec((ROWS, TILE), lambda i: (0, i)),
            pl.BlockSpec((TILE, CHANS), lambda i: (i, 0)),
            pl.BlockSpec((GROUPS, LENGTH), lambda i: (0, 0)),
        ],
        out_specs=[
            pl.BlockSpec((ROWS, CHANS), lambda i: (0, 0)),
            pl.BlockSpec((2 * STRIP, LENGTH), lambda i: (i, 0)),
        ],
        out_shape=[
            jax.ShapeDtypeStruct((ROWS, CHANS), BF16),
            jax.ShapeDtypeStruct((GROUPS * STRIP, LENGTH), BF16),
        ],
        scratch_shapes=[pltpu.VMEM((ROWS, CHANS), F32), pltpu.VMEM((GROUPS, WIDE), F32)],
        compiler_params=params(),
        cost_estimate=pl.CostEstimate(
            flops=2 * ROWS * FEATS * CHANS, bytes_accessed=14 << 20, transcendentals=0
        ),
        name="pre",
    )(cot, weight, lags)


def d_inner_kernel(d_gated_ref, query_ref, tail_ref, taps_ref, out_ref):
    q_short = short_sum(taps_ref, 0, with_tail(tail_ref[...], query_ref[...]))
    out_ref[...] = (d_gated_ref[...].astype(F32) * q_short).astype(BF16)


def d_inner_call(d_gated, query, tail, taps):
    return pl.pallas_call(
        d_inner_kernel,
        out_shape=jax.ShapeDtypeStruct((ROWS, CHANS), BF16),
        compiler_params=params(),
        cost_estimate=pl.CostEstimate(flops=1 << 20, bytes_accessed=1 << 19, transcendentals=0),
        name="d_inner",
    )(d_gated, query, tail, taps)


def fwd_kernel(
    core_ref, strips_ref, pair_ref, cross_ref, cross_pair_ref, key_ref, value_ref, query_ref,
    tail_ref, taps_ref, skip_ref,
    gated_ref, inner_ref, mixed_ref,
    signal_ref,
):
    upper = core_ref[0] == 1
    pair = pair_ref[...].astype(F32)
    cross_pair = cross_pair_ref[...].astype(F32)
    near = jnp.where(upper, pair, cross_pair)
    far = jnp.where(upper, cross_pair, 0.0)
    own = jnp.concatenate([key_ref[...], value_ref[...]], axis=1).astype(F32)
    both = jnp.concatenate([far, cross_ref[...].astype(F32), near, own], axis=0)
    shifted = (both, later(both, 1), later(both, 2))
    k_short = short_sum(taps_ref, 1, [part[:, :CHANS] for part in shifted])
    v_short = short_sum(taps_ref, 2, [part[:, CHANS:] for part in shifted])
    mixed = (k_short * v_short).astype(BF16)
    mixed_ref[...] = mixed[LENGTH - ROWS :]
    signal_ref[: ROWS - STRIP, :] = jnp.zeros((ROWS - STRIP, CHANS), BF16)
    signal_ref[ROWS - STRIP :, :] = mixed
    inner = all_strips(strips_ref, signal_ref) + skip_ref[...] * mixed[LENGTH - ROWS :].astype(F32)
    inner_ref[...] = inner
    q_short = short_sum(taps_ref, 0, with_tail(tail_ref[...], query_ref[...]))
    gated_ref[...] = (q_short * inner).astype(BF16)


def with_core(kernel, name, core, operands, out_shape, scratch, flops):
    whole = lambda x: pl.BlockSpec(x.shape, lambda i, core_ref: (0,) * len(x.shape))
    return pl.pallas_call(
        kernel,
        grid_spec=pltpu.PrefetchScalarGridSpec(
            num_scalar_prefetch=1,
            grid=(1,),
            in_specs=[whole(x) for x in operands],
            out_specs=[whole(x) for x in out_shape],
            scratch_shapes=scratch,
        ),
        out_shape=out_shape,
        compiler_params=params(),
        cost_estimate=pl.CostEstimate(flops=flops, bytes_accessed=1 << 10, transcendentals=0),
        name=name,
    )(core, *operands)


def fwd_call(core, *operands):
    return with_core(
        fwd_kernel,
        "fwd",
        core,
        operands,
        [
            jax.ShapeDtypeStruct((ROWS, CHANS), BF16),
            jax.ShapeDtypeStruct((ROWS, CHANS), F32),
            jax.ShapeDtypeStruct((ROWS, CHANS), BF16),
        ],
        [pltpu.VMEM((LENGTH + ROWS - STRIP, CHANS), BF16)],
        4 << 30,
    )


def terms_kernel(core_ref, own_cot_ref, other_cot_ref, gated_ref, other_gated_ref, out_ref):
    dims = (((0,), (0,)), ((), ()))
    total = lax.dot_general(gated_ref[...], own_cot_ref[...], dims, preferred_element_type=F32)
    total += lax.dot_general(
        other_gated_ref[...], other_cot_ref[...], dims, preferred_element_type=F32
    )
    out_ref[0] = total.astype(BF16)


def terms_call(core, own_cot, other_cot, gated, other_gated):
    column = pl.BlockSpec((ROWS, SHARE), lambda i, core_ref: (0, 2 * i + core_ref[0]))
    signal = pl.BlockSpec((ROWS, CHANS), lambda i, core_ref: (0, 0))
    return pl.pallas_call(
        terms_kernel,
        grid_spec=pltpu.PrefetchScalarGridSpec(
            num_scalar_prefetch=1,
            grid=(2,),
            in_specs=[column, column, signal, signal],
            out_specs=pl.BlockSpec((1, CHANS, SHARE), lambda i, core_ref: (i, 0, 0)),
        ),
        out_shape=jax.ShapeDtypeStruct((2, CHANS, SHARE + CHANS), BF16),
        compiler_params=params(),
        cost_estimate=pl.CostEstimate(
            flops=2 * ROWS * FEATS * CHANS, bytes_accessed=6 << 20, transcendentals=0
        ),
        name="terms",
    )(core, own_cot, other_cot, gated, other_gated)


def two_parts(total):
    rounded = total.astype(BF16).astype(F32)
    left = pltpu.roll(total - rounded, SEGMENT // 2, total.ndim - 2)
    return (rounded + left).astype(BF16)


def add_small_kernel(terms_ref, small_ref, other_small_ref, out_ref):
    parts = two_parts(small_ref[...] + other_small_ref[...]).astype(F32)
    out_ref[...] = jnp.broadcast_to(parts.reshape(1, CHANS, CHANS).astype(BF16), out_ref.shape)


def add_small_call(terms, small, other_small):
    whole = pl.BlockSpec((SHARES, SEGMENT, CHANS), lambda i: (0, 0, 0))
    return pl.pallas_call(
        add_small_kernel,
        grid=(1,),
        in_specs=[pl.BlockSpec(memory_space=pl.ANY), whole, whole],
        out_specs=pl.BlockSpec((2, CHANS, CHANS), lambda i: (0, 0, SHARE // CHANS)),
        out_shape=jax.ShapeDtypeStruct(terms.shape, BF16),
        input_output_aliases={0: 0},
        compiler_params=params(),
        name="add_small",
    )(terms, small, other_small)


def place(g, n):
    row = g * (LENGTH // CHANS) + n
    return row % SHARES, row // SHARES


def bwd_kernel(
    core_ref, d0_ref, d1_ref, d2_ref, d3_ref, lags_ref, mixed_ref, key_ref, value_ref, pair_ref,
    cross_pair_ref, query_ref, tail_ref, inner_ref, d_gated_ref, taps_ref, skip_ref,
    d_short_ref, small_ref,
    strips_ref, ahead_ref, outer_ref, stack_ref,
):
    for n, ref in enumerate((d0_ref, d1_ref, d2_ref, d3_ref)):
        ahead_ref[n * ROWS : (n + 1) * ROWS, :] = ref[...]
    ahead_ref[LENGTH:, :] = jnp.zeros((ROWS, CHANS), BF16)
    lines = lines_of(lags_ref, False)
    for g in range(GROUPS):
        strips_ref[g * STRIP : (g + 1) * STRIP, :] = strip_of(lines[g : g + 1])
    d_inner = d0_ref[...].astype(F32)
    mixed = mixed_ref[...]
    d_mixed = all_strips(strips_ref, ahead_ref) + skip_ref[...] * d_inner

    upper = core_ref[0] == 1
    last = slice(ROWS - TAIL, ROWS)
    near = jnp.where(upper, pair_ref[last, :].astype(F32), cross_pair_ref[last, :].astype(F32))
    k_parts = with_tail(near[:, :CHANS], key_ref[...])
    v_parts = with_tail(near[:, CHANS:], value_ref[...])
    q_parts = with_tail(tail_ref[...], query_ref[...])
    small_ref[...] = jnp.zeros_like(small_ref)
    d_qs = d_gated_ref[...].astype(F32) * inner_ref[...]
    d_ks = d_mixed * short_sum(taps_ref, 2, v_parts)
    d_vs = d_mixed * short_sum(taps_ref, 1, k_parts)
    for i, (grad, parts) in enumerate(((d_qs, q_parts), (d_ks, k_parts), (d_vs, v_parts))):
        d_short_ref[i] = grad
        for j in range(3):
            small_ref[3 * i + j, 2:3, :] = jnp.sum(grad * parts[j], axis=0, keepdims=True)
    small_ref[9, 2:3, :] = jnp.sum(d_inner * mixed.astype(F32), axis=0, keepdims=True)

    row = lax.broadcasted_iota(jnp.int32, (ROWS, ROWS), 0)
    col = lax.broadcasted_iota(jnp.int32, (ROWS, ROWS), 1)
    turn = ((row // SMALL) * SMALL + (SMALL - 1 - row % SMALL) == col).astype(F32).astype(BF16)
    turned = jnp.dot(turn, mixed, preferred_element_type=F32)
    ids = lane_groups(SMALL)
    for part in range(ROWS // SMALL):
        piece = turned[part * SMALL : (part + 1) * SMALL]
        for g in range(GROUPS):
            stack_ref[g * SMALL : (g + 1) * SMALL, :] = jnp.where(ids == g, piece, 0.0).astype(BF16)
        term = lax.dot_general(
            stack_ref[...],
            ahead_ref[part * SMALL : part * SMALL + LENGTH, :],
            (((1,), (1,)), ((), ())),
            preferred_element_type=F32,
        )
        if part == 0:
            outer_ref[:, :LENGTH] = term
        else:
            outer_ref[:, :LENGTH] += term
    outer_ref[:, LENGTH:] = jnp.zeros((GROUPS * SMALL, PAD), F32)
    for g in range(GROUPS):
        skewed = pltpu.roll(
            outer_ref[g * SMALL : (g + 1) * SMALL, :], WIDE - (SMALL - 1), 1, stride=1, stride_axis=0
        )
        sums = jnp.sum(skewed[:, :LENGTH], axis=0, keepdims=True)
        for n in range(LENGTH // CHANS):
            share, slot = place(g, n)
            small_ref[share, slot : slot + 1, :] = sums[:, n * CHANS : (n + 1) * CHANS]


def bwd_call(core, *operands):
    return with_core(
        bwd_kernel,
        "bwd",
        core,
        operands,
        [
            jax.ShapeDtypeStruct((3, ROWS, CHANS), F32),
            jax.ShapeDtypeStruct((SHARES, SEGMENT, CHANS), F32),
        ],
        [
            pltpu.VMEM((GROUPS * STRIP, LENGTH), BF16),
            pltpu.VMEM((LENGTH + ROWS, CHANS), BF16),
            pltpu.VMEM((GROUPS * SMALL, WIDE), F32),
            pltpu.VMEM((GROUPS * SMALL, CHANS), BF16),
        ],
        1 << 10,
    )


def input_grad_kernel(d_short_ref, next_ref, taps_ref, query_ref, key_ref, value_ref):
    for i, out_ref in enumerate((query_ref, key_ref, value_ref)):
        joined = jnp.concatenate([d_short_ref[i], next_ref[i]], axis=0)
        rows = joined.shape[0]
        parts = (
            joined[:ROWS],
            pltpu.roll(joined, rows - 1, 0)[:ROWS],
            pltpu.roll(joined, rows - 2, 0)[:ROWS],
        )
        out_ref[...] = short_sum(taps_ref, i, parts).astype(BF16)


def input_grad_call(d_short, following, taps):
    return pl.pallas_call(
        input_grad_kernel,
        out_shape=[jax.ShapeDtypeStruct((ROWS, CHANS), BF16)] * 3,
        compiler_params=params(),
        cost_estimate=pl.CostEstimate(flops=1 << 10, bytes_accessed=1 << 10, transcendentals=0),
        name="input_grads",
    )(d_short, following, taps)


def total_kernel(scale, terms_ref, out_ref):
    total = jnp.sum(terms_ref[...].astype(F32), axis=0) * scale
    small = total[:, SHARE:]
    row = lax.broadcasted_iota(jnp.int32, small.shape, 0)
    small = jnp.where(row < SEGMENT // 2, small + pltpu.roll(small, SEGMENT // 2, 0), 0.0)
    total = jnp.concatenate([total[:, :SHARE].astype(BF16), two_parts(small)], axis=1)
    out_ref[...] = jnp.broadcast_to(total[None], out_ref.shape)


def total_call(terms, scale):
    return pl.pallas_call(
        lambda *refs: total_kernel(scale, *refs),
        out_shape=jax.ShapeDtypeStruct((SHARES, *terms.shape[1:]), BF16),
        compiler_params=params(),
        cost_estimate=pl.CostEstimate(flops=1 << 20, bytes_accessed=3 << 20, transcendentals=0),
        name="total",
    )(terms)


def spread_kernel(shares_ref, small_ref, weight_ref, taps_ref, filter_ref, skip_ref):
    weight_ref[...] = shares_ref[...].astype(F32).T

    @pl.when(pl.program_id(0) == 0)
    def _():
        for share in range(SHARES):
            segment = small_ref[share * SEGMENT : (share + 1) * SEGMENT, :].astype(F32)
            segment = segment + pltpu.roll(segment, SEGMENT // 2, 0)
            for g in range(GROUPS):
                for n in range(LENGTH // CHANS):
                    if place(g, n)[0] == share:
                        slot = place(g, n)[1]
                        filter_ref[g : g + 1, n * CHANS : (n + 1) * CHANS] = segment[slot : slot + 1]
            if share < 9:
                taps_ref[share // 3, share % 3 : share % 3 + 1, :] = segment[2:3]
            if share == 9:
                skip_ref[...] = segment[2:3]


def spread_call(shares):
    shares = shares.reshape(CHANS, SHARE + CHANS)
    tile = 512
    return pl.pallas_call(
        spread_kernel,
        grid=(SHARE // tile,),
        in_specs=[
            pl.BlockSpec((CHANS, tile), lambda i: (0, i)),
            pl.BlockSpec((CHANS, CHANS), lambda i: (0, SHARE // CHANS)),
        ],
        out_specs=[
            pl.BlockSpec((tile, CHANS), lambda i: (i, 0)),
            pl.BlockSpec((3, 3, CHANS), lambda i: (0, 0, 0)),
            pl.BlockSpec((GROUPS, LENGTH), lambda i: (0, 0)),
            pl.BlockSpec((1, CHANS), lambda i: (0, 0)),
        ],
        out_shape=[
            jax.ShapeDtypeStruct((SHARE, CHANS), F32),
            jax.ShapeDtypeStruct((3, 3, CHANS), F32),
            jax.ShapeDtypeStruct((GROUPS, LENGTH), F32),
            jax.ShapeDtypeStruct((1, CHANS), F32),
        ],
        compiler_params=params(),
        name="spread",
    )(shares, shares)


def sent(block, distance):
    count = 4
    route = [(i, i + distance) for i in range(count) if 0 <= i + distance < count]
    return lax.ppermute(block, CTX, route)


def shards(
    query_in, key_in, value_in, short_taps, long_filter, skip_gain, out_weight, out_cotangent
):
    query = query_in[0]
    cot = out_cotangent[0]
    taps = short_taps
    skip = skip_gain.reshape(1, CHANS)
    devices = lax.axis_size(ALL)
    tokens = ROWS * devices
    scale = 1.0 / math.sqrt(tokens)
    core = lax.axis_index("co").astype(jnp.int32).reshape(1)

    key = key_in[0]
    value = value_in[0]
    swap = [(0, 1), (1, 0)]
    own = jnp.concatenate([key, value], axis=1)
    tail = sent(query[ROWS - TAIL :], 1)
    cross = lax.ppermute(own, "xh", [(0, 1)])
    pair = lax.ppermute(own, "co", swap)
    other_cot = lax.ppermute(cot, "co", swap)

    d_gated, strips = pre_call(cot, out_weight, long_filter)
    cross, tail, d_gated, strips = lax.optimization_barrier((cross, tail, d_gated, strips))
    cross_pair = lax.ppermute(cross, "co", swap)
    d_inner = d_inner_call(d_gated, query, tail, taps)
    blocks = [d_inner] + [sent(d_inner, -distance) for distance in (1, 2, 3)]
    gated, inner, mixed = fwd_call(
        core, strips, pair, cross, cross_pair, key, value, query, tail, taps, skip
    )
    other_gated = lax.ppermute(gated, "co", swap)
    d_short, small = bwd_call(
        core, *blocks, long_filter, mixed, key, value, pair, cross_pair, query, tail, inner,
        d_gated, taps, skip,
    )
    other_gated, d_short, small = lax.optimization_barrier((other_gated, d_short, small))
    other_small = lax.ppermute(small, "co", swap)
    following = sent(d_short[:, :8], -1)
    terms = terms_call(core, cot, other_cot, gated, other_gated)
    terms, other_small, following = lax.optimization_barrier((terms, other_small, following))
    terms = add_small_call(terms, small, other_small)
    terms = terms.reshape(2 * SHARES, CHANS // SHARES, SHARE + CHANS)
    terms = lax.all_to_all(terms, CHIPS, 0, 0)
    grad_query, grad_key, grad_value = input_grad_call(d_short, following, taps)

    shares = lax.all_to_all(total_call(terms, scale), DP, 0, 0)
    grad_weight, grad_taps, grad_filter, grad_skip = spread_call(shares)
    return (
        gated[None],
        grad_query[None],
        grad_key[None],
        grad_value[None],
        grad_taps,
        grad_filter,
        grad_skip.reshape(CHANS),
        grad_weight,
    )


def solution(mesh):
    fine = Mesh(mesh.devices.reshape(2, 2, 4, 2, 4), ALL)
    tokens = P(DP, CTX, None)
    in_specs = (tokens, tokens, tokens, P(), P(), P(), P(), tokens)
    out_specs = (tokens, tokens, tokens, tokens, P(), P(), P(), P(CTX, None))
    return jax.shard_map(
        shards, mesh=fine, in_specs=in_specs, out_specs=out_specs, check_vma=False
    )
```

```python
import math

import jax
import jax.numpy as jnp
from jax import lax
from jax.experimental import pallas as pl
from jax.experimental.pallas import tpu as pltpu
from jax.sharding import Mesh
from jax.sharding import PartitionSpec as P

F32 = jnp.float32
BF16 = jnp.bfloat16
CTX = ("xh", "co")
DP = ("y", "xl", "z")
CHIPS = ("xh", "y", "xl", "z")
ALL = ("xh", "co", "y", "xl", "z")

ROWS = 256
CHANS = 256
GROUPS = 16
LENGTH = 1024
STRIP = 32
PAD = 128
WIDE = LENGTH + PAD
FEATS = 8192
SMALL = 32
TAIL = 16
SHARES = 32
SHARE = FEATS // 4
SEGMENT = 8
SPREAD = 4
PIECES = 8
VMEM_LIMIT = 24 * 1024 * 1024


def call(kernel, name, out_shape, operands, scratch=(), scalars=0, flops=1 << 10, **more):
    spec = pl.BlockSpec(memory_space=pltpu.VMEM)
    in_specs = [pl.BlockSpec(memory_space=pltpu.SMEM)] * scalars
    in_specs += [spec] * (len(operands) - scalars)
    defaults = {"in_specs": in_specs, "out_specs": jax.tree.map(lambda _: spec, out_shape)}
    more = {**defaults, **more}
    placed = [
        pltpu.with_memory_space_constraint(x, pltpu.VMEM) if s.memory_space == pltpu.VMEM else x
        for x, s in zip(operands, more["in_specs"])
    ]
    return pl.pallas_call(
        kernel,
        out_shape=out_shape,
        scratch_shapes=list(scratch),
        compiler_params=pltpu.CompilerParams(vmem_limit_bytes=VMEM_LIMIT),
        cost_estimate=pl.CostEstimate(flops=flops, bytes_accessed=1 << 10, transcendentals=0),
        name=name,
        **more,
    )(*placed)


def lane_groups(rows):
    return lax.broadcasted_iota(jnp.int32, (rows, CHANS), 1) // (CHANS // GROUPS)


def later(x, count):
    row = lax.broadcasted_iota(jnp.int32, x.shape, 0)
    return jnp.where(row >= count, pltpu.roll(x, count, 0), 0.0)


def strip_of(line):
    wide = jnp.broadcast_to(line, (STRIP, WIDE))
    return pltpu.roll(wide, 0, 1, stride=1, stride_axis=0)[:, :LENGTH].astype(BF16)


def pick_groups(result):
    ids = lane_groups(STRIP)
    out = jnp.zeros((STRIP, CHANS), F32)
    for g in range(GROUPS):
        out = jnp.where(ids == g, result[g * STRIP : (g + 1) * STRIP], out)
    return out


def all_strips(strips_ref, signal_ref):
    parts = []
    for n in range(ROWS // STRIP):
        window = signal_ref[n * STRIP : n * STRIP + LENGTH, :]
        parts.append(pick_groups(jnp.dot(strips_ref[...], window, preferred_element_type=F32)))
    return jnp.concatenate(parts, axis=0)


def with_tail(tail, block):
    joined = jnp.concatenate([tail.astype(F32), block.astype(F32)], axis=0)
    return joined[TAIL:], pltpu.roll(joined, 1, 0)[TAIL:], pltpu.roll(joined, 2, 0)[TAIL:]


def short_sum(taps_ref, i, parts):
    return sum(taps_ref[i, j : j + 1, :] * parts[j] for j in range(3))


def lines_of(filter_ref, turned):
    if not turned:
        return jnp.concatenate(
            [filter_ref[...].astype(F32), jnp.zeros((GROUPS, PAD), F32)], axis=1
        )
    row = lax.broadcasted_iota(jnp.int32, (CHANS, CHANS), 0)
    col = lax.broadcasted_iota(jnp.int32, (CHANS, CHANS), 1)
    turn = (row + col == CHANS - 1).astype(F32).astype(BF16)
    pieces = [
        jnp.dot(filter_ref[:, n * CHANS : (n + 1) * CHANS], turn, preferred_element_type=F32)
        for n in reversed(range(LENGTH // CHANS))
    ]
    wide = jnp.concatenate([*pieces, jnp.zeros((GROUPS, PAD), F32)], axis=1)
    return pltpu.roll(wide, WIDE - (STRIP - 1), 1)


def pre_kernel(
    cot_ref, weight_ref, filter_ref, d_gated_ref, strips_ref, cot_buffer, weight_buffer, sems
):
    tile = FEATS // PIECES
    copies = []
    for n in range(PIECES):
        piece = slice(n * tile, (n + 1) * tile)
        pair = (
            pltpu.make_async_copy(cot_ref.at[:, piece], cot_buffer.at[n], sems.at[0, n]),
            pltpu.make_async_copy(weight_ref.at[piece, :], weight_buffer.at[n], sems.at[1, n]),
        )
        for copy in pair:
            copy.start()
        copies.append(pair)
    lines = lines_of(filter_ref, True)
    for g in range(GROUPS):
        strips_ref[g * STRIP : (g + 1) * STRIP, :] = strip_of(lines[g : g + 1])
    total = jnp.zeros((ROWS, CHANS), F32)
    for n in range(PIECES):
        for copy in copies[n]:
            copy.wait()
        total += jnp.dot(cot_buffer[n], weight_buffer[n], preferred_element_type=F32)
    d_gated_ref[...] = total.astype(BF16)


def pre_call(cot, weight, lags):
    out_shape = [
        pltpu.VMEM((ROWS, CHANS), BF16),
        pltpu.VMEM((GROUPS * STRIP, LENGTH), BF16),
    ]
    tile = FEATS // PIECES
    scratch = [
        pltpu.VMEM((PIECES, ROWS, tile), BF16),
        pltpu.VMEM((PIECES, tile, CHANS), BF16),
        pltpu.SemaphoreType.DMA((2, PIECES)),
    ]
    far = pl.BlockSpec(memory_space=pl.ANY)
    in_specs = [far, far, pl.BlockSpec(memory_space=pltpu.VMEM)]
    return call(
        pre_kernel, "pre", out_shape, (cot, weight, lags), scratch, in_specs=in_specs, flops=1 << 30
    )


def d_inner_kernel(d_gated_ref, query_ref, tail_ref, taps_ref, out_ref):
    q_short = short_sum(taps_ref, 0, with_tail(tail_ref[...], query_ref[...]))
    out_ref[...] = (d_gated_ref[...].astype(F32) * q_short).astype(BF16)


def d_inner_call(*operands):
    return call(d_inner_kernel, "d_inner", pltpu.VMEM((ROWS, CHANS), BF16), operands)


def fwd_kernel(
    core_ref, strips_ref, pair_ref, cross_ref, cross_pair_ref, key_ref, value_ref, query_ref,
    tail_ref, taps_ref, skip_ref,
    gated_ref, inner_ref, mixed_ref,
    signal_ref,
):
    upper = core_ref[0] == 1
    pair = pair_ref[...].astype(F32)
    cross_pair = cross_pair_ref[...].astype(F32)
    near = jnp.where(upper, pair, cross_pair)
    far = jnp.where(upper, cross_pair, 0.0)
    own = jnp.concatenate([key_ref[...], value_ref[...]], axis=1).astype(F32)
    both = jnp.concatenate([far, cross_ref[...].astype(F32), near, own], axis=0)
    shifted = (both, later(both, 1), later(both, 2))
    k_short = short_sum(taps_ref, 1, [part[:, :CHANS] for part in shifted])
    v_short = short_sum(taps_ref, 2, [part[:, CHANS:] for part in shifted])
    mixed = (k_short * v_short).astype(BF16)
    mixed_ref[...] = mixed[LENGTH - ROWS :]
    signal_ref[: ROWS - STRIP, :] = jnp.zeros((ROWS - STRIP, CHANS), BF16)
    signal_ref[ROWS - STRIP :, :] = mixed
    inner = all_strips(strips_ref, signal_ref) + skip_ref[...] * mixed[LENGTH - ROWS :].astype(F32)
    inner_ref[...] = inner
    q_short = short_sum(taps_ref, 0, with_tail(tail_ref[...], query_ref[...]))
    gated_ref[...] = (q_short * inner).astype(BF16)


def fwd_call(*operands):
    out_shape = [
        pltpu.VMEM((ROWS, CHANS), BF16),
        pltpu.VMEM((ROWS, CHANS), F32),
        pltpu.VMEM((ROWS, CHANS), BF16),
    ]
    scratch = [pltpu.VMEM((LENGTH + ROWS - STRIP, CHANS), BF16)]
    return call(fwd_kernel, "fwd", out_shape, operands, scratch, 1, 4 << 30)


def terms_kernel(core_ref, own_cot_ref, other_cot_ref, gated_ref, other_gated_ref, out_ref):
    dims = (((0,), (0,)), ((), ()))
    for half in range(2):
        start = pl.multiple_of((2 * half + core_ref[0]) * SHARE, SHARE)
        own_cot = own_cot_ref[:, pl.ds(start, SHARE)]
        other_cot = other_cot_ref[:, pl.ds(start, SHARE)]
        total = lax.dot_general(gated_ref[...], own_cot, dims, preferred_element_type=F32)
        total += lax.dot_general(other_gated_ref[...], other_cot, dims, preferred_element_type=F32)
        out_ref[half, :, :SHARE] = total.astype(BF16)


def terms_call(*operands):
    out_shape = pltpu.VMEM((2, CHANS, SHARE + CHANS), BF16)
    return call(terms_kernel, "terms", out_shape, operands, scalars=1, flops=1 << 30)


def two_parts(total):
    rounded = total.astype(BF16).astype(F32)
    left = pltpu.roll(total - rounded, SEGMENT // 2, total.ndim - 2)
    return (rounded + left).astype(BF16)


def add_small_kernel(terms_ref, small_ref, other_small_ref, out_ref):
    parts = two_parts(small_ref[...] + other_small_ref[...]).astype(F32)
    parts = parts.reshape(CHANS, CHANS).astype(BF16)
    for half in range(2):
        out_ref[half, :, SHARE:] = parts


def add_small_call(*operands):
    out_shape = pltpu.VMEM(operands[0].shape, BF16)
    return call(add_small_kernel, "add_small", out_shape, operands, input_output_aliases={0: 0})


def place(g, n):
    row = g * (LENGTH // CHANS) + n
    return row % SHARES, row // SHARES


def bwd_kernel(
    core_ref, d0_ref, d1_ref, d2_ref, d3_ref, lags_ref, mixed_ref, key_ref, value_ref, pair_ref,
    cross_pair_ref, query_ref, tail_ref, inner_ref, d_gated_ref, taps_ref, skip_ref,
    d_short_ref, head_ref, small_ref,
    strips_ref, ahead_ref, outer_ref, stack_ref,
):
    for n, ref in enumerate((d0_ref, d1_ref, d2_ref, d3_ref)):
        ahead_ref[n * ROWS : (n + 1) * ROWS, :] = ref[...]
    ahead_ref[LENGTH:, :] = jnp.zeros((ROWS, CHANS), BF16)
    lines = lines_of(lags_ref, False)
    for g in range(GROUPS):
        strips_ref[g * STRIP : (g + 1) * STRIP, :] = strip_of(lines[g : g + 1])
    d_inner = d0_ref[...].astype(F32)
    mixed = mixed_ref[...]
    d_mixed = all_strips(strips_ref, ahead_ref) + skip_ref[...] * d_inner

    upper = core_ref[0] == 1
    last = slice(ROWS - TAIL, ROWS)
    near = jnp.where(upper, pair_ref[last, :].astype(F32), cross_pair_ref[last, :].astype(F32))
    k_parts = with_tail(near[:, :CHANS], key_ref[...])
    v_parts = with_tail(near[:, CHANS:], value_ref[...])
    q_parts = with_tail(tail_ref[...], query_ref[...])
    small_ref[...] = jnp.zeros_like(small_ref)
    d_qs = d_gated_ref[...].astype(F32) * inner_ref[...]
    d_ks = d_mixed * short_sum(taps_ref, 2, v_parts)
    d_vs = d_mixed * short_sum(taps_ref, 1, k_parts)
    for i, (grad, parts) in enumerate(((d_qs, q_parts), (d_ks, k_parts), (d_vs, v_parts))):
        d_short_ref[i] = grad
        head_ref[i] = grad[:8]
        for j in range(3):
            small_ref[3 * i + j, 2:3, :] = jnp.sum(grad * parts[j], axis=0, keepdims=True)
    small_ref[9, 2:3, :] = jnp.sum(d_inner * mixed.astype(F32), axis=0, keepdims=True)

    row = lax.broadcasted_iota(jnp.int32, (ROWS, ROWS), 0)
    col = lax.broadcasted_iota(jnp.int32, (ROWS, ROWS), 1)
    turn = ((row // SMALL) * SMALL + (SMALL - 1 - row % SMALL) == col).astype(F32).astype(BF16)
    turned = jnp.dot(turn, mixed, preferred_element_type=F32)
    ids = lane_groups(SMALL)
    for part in range(ROWS // SMALL):
        piece = turned[part * SMALL : (part + 1) * SMALL]
        for g in range(GROUPS):
            stack_ref[g * SMALL : (g + 1) * SMALL, :] = jnp.where(ids == g, piece, 0.0).astype(BF16)
        term = lax.dot_general(
            stack_ref[...],
            ahead_ref[part * SMALL : part * SMALL + LENGTH, :],
            (((1,), (1,)), ((), ())),
            preferred_element_type=F32,
        )
        if part == 0:
            outer_ref[:, :LENGTH] = term
        else:
            outer_ref[:, :LENGTH] += term
    outer_ref[:, LENGTH:] = jnp.zeros((GROUPS * SMALL, PAD), F32)
    for g in range(GROUPS):
        skewed = pltpu.roll(
            outer_ref[g * SMALL : (g + 1) * SMALL, :], WIDE - (SMALL - 1), 1, stride=1, stride_axis=0
        )
        sums = jnp.sum(skewed[:, :LENGTH], axis=0, keepdims=True)
        for n in range(LENGTH // CHANS):
            share, slot = place(g, n)
            small_ref[share, slot : slot + 1, :] = sums[:, n * CHANS : (n + 1) * CHANS]


def bwd_call(*operands):
    out_shape = [
        pltpu.VMEM((3, ROWS, CHANS), F32),
        pltpu.VMEM((3, 8, CHANS), F32),
        pltpu.VMEM((SHARES, SEGMENT, CHANS), F32),
    ]
    scratch = [
        pltpu.VMEM((GROUPS * STRIP, LENGTH), BF16),
        pltpu.VMEM((LENGTH + ROWS, CHANS), BF16),
        pltpu.VMEM((GROUPS * SMALL, WIDE), F32),
        pltpu.VMEM((GROUPS * SMALL, CHANS), BF16),
    ]
    return call(bwd_kernel, "bwd", out_shape, operands, scratch, 1)


def input_grad_kernel(d_short_ref, next_ref, taps_ref, query_ref, key_ref, value_ref):
    for i, out_ref in enumerate((query_ref, key_ref, value_ref)):
        joined = jnp.concatenate([d_short_ref[i], next_ref[i]], axis=0)
        rows = joined.shape[0]
        parts = (
            joined[:ROWS],
            pltpu.roll(joined, rows - 1, 0)[:ROWS],
            pltpu.roll(joined, rows - 2, 0)[:ROWS],
        )
        out_ref[...] = short_sum(taps_ref, i, parts).astype(BF16)


def input_grad_call(*operands):
    out_shape = [jax.ShapeDtypeStruct((ROWS, CHANS), BF16)] * 3
    return call(input_grad_kernel, "input_grads", out_shape, operands)


def total_kernel(scale, terms_ref, out_ref):
    total = jnp.sum(terms_ref[...].astype(F32), axis=0) * scale
    small = total[:, SHARE:]
    row = lax.broadcasted_iota(jnp.int32, small.shape, 0)
    small = jnp.where(row < SEGMENT // 2, small + pltpu.roll(small, SEGMENT // 2, 0), 0.0)
    total = jnp.concatenate([total[:, :SHARE].astype(BF16), two_parts(small)], axis=1)
    out_ref[...] = jnp.broadcast_to(total[None], out_ref.shape)


def total_call(terms, scale):
    out_shape = pltpu.VMEM((SHARES, *terms.shape[1:]), BF16)
    return call(lambda *refs: total_kernel(scale, *refs), "total", out_shape, (terms,))


def spread_kernel(
    shares_ref, weight_ref, taps_ref, filter_ref, skip_ref, turned_ref, sems
):
    tile = SHARE // SPREAD
    copies = []
    for n in range(SPREAD):
        piece = slice(n * tile, (n + 1) * tile)
        turned_ref[piece, :] = shares_ref[:, piece].astype(F32).T
        copies.append(
            pltpu.make_async_copy(turned_ref.at[piece, :], weight_ref.at[piece, :], sems.at[n])
        )
        copies[-1].start()
    for share in range(SHARES):
        segment = shares_ref[share * SEGMENT : (share + 1) * SEGMENT, SHARE:].astype(F32)
        segment = segment + pltpu.roll(segment, SEGMENT // 2, 0)
        for g in range(GROUPS):
            for n in range(LENGTH // CHANS):
                if place(g, n)[0] == share:
                    slot = place(g, n)[1]
                    filter_ref[g : g + 1, n * CHANS : (n + 1) * CHANS] = segment[slot : slot + 1]
        if share < 9:
            taps_ref[share // 3, share % 3 : share % 3 + 1, :] = segment[2:3]
        if share == 9:
            skip_ref[...] = segment[2:3]
    for copy in copies:
        copy.wait()


def spread_call(shares):
    out_shape = [
        jax.ShapeDtypeStruct((SHARE, CHANS), F32),
        jax.ShapeDtypeStruct((3, 3, CHANS), F32),
        jax.ShapeDtypeStruct((GROUPS, LENGTH), F32),
        jax.ShapeDtypeStruct((1, CHANS), F32),
    ]
    scratch = [pltpu.VMEM((SHARE, CHANS), F32), pltpu.SemaphoreType.DMA((SPREAD,))]
    out_specs = [pl.BlockSpec(memory_space=pl.ANY)]
    out_specs += [pl.BlockSpec(memory_space=pltpu.VMEM)] * 3
    shares = shares.reshape(CHANS, SHARE + CHANS)
    return call(spread_kernel, "spread", out_shape, (shares,), scratch, out_specs=out_specs)


def sent(block, distance):
    count = 4
    route = [(i, i + distance) for i in range(count) if 0 <= i + distance < count]
    return lax.ppermute(block, CTX, route)


def shards(
    query_in, key_in, value_in, short_taps, long_filter, skip_gain, out_weight, out_cotangent
):
    query = query_in[0]
    cot = out_cotangent[0]
    taps = short_taps
    skip = skip_gain.reshape(1, CHANS)
    devices = lax.axis_size(ALL)
    tokens = ROWS * devices
    scale = 1.0 / math.sqrt(tokens)
    core = lax.axis_index("co").astype(jnp.int32).reshape(1)

    key = key_in[0]
    value = value_in[0]
    swap = [(0, 1), (1, 0)]
    own = jnp.concatenate([key, value], axis=1)
    tail = sent(query[ROWS - TAIL :], 1)
    cross = lax.ppermute(own, "xh", [(0, 1)])
    pair = lax.ppermute(own, "co", swap)
    other_cot = lax.ppermute(cot, "co", swap)

    d_gated, strips = pre_call(cot, out_weight, long_filter)
    cross, tail, d_gated, strips = lax.optimization_barrier((cross, tail, d_gated, strips))
    cross_pair = lax.ppermute(cross, "co", swap)
    d_inner = d_inner_call(d_gated, query, tail, taps)
    blocks = [d_inner] + [sent(d_inner, -distance) for distance in (1, 2, 3)]
    gated, inner, mixed = fwd_call(
        core, strips, pair, cross, cross_pair, key, value, query, tail, taps, skip
    )
    other_gated = lax.ppermute(gated, "co", swap)
    d_short, head, small = bwd_call(
        core, *blocks, long_filter, mixed, key, value, pair, cross_pair, query, tail, inner,
        d_gated, taps, skip,
    )
    other_gated, head, small = lax.optimization_barrier((other_gated, head, small))
    other_small = lax.ppermute(small, "co", swap)
    following = sent(head, -1)
    terms = terms_call(core, cot, other_cot, gated, other_gated)
    terms, other_small, following = lax.optimization_barrier((terms, other_small, following))
    terms = add_small_call(terms, small, other_small)
    terms = terms.reshape(2 * SHARES, CHANS // SHARES, SHARE + CHANS)
    terms = lax.all_to_all(terms, CHIPS, 0, 0)
    grad_query, grad_key, grad_value = input_grad_call(d_short, following, taps)

    shares = lax.all_to_all(total_call(terms, scale), DP, 0, 0)
    grad_weight, grad_taps, grad_filter, grad_skip = spread_call(shares)
    return (
        gated[None],
        grad_query[None],
        grad_key[None],
        grad_value[None],
        grad_taps,
        grad_filter,
        grad_skip.reshape(CHANS),
        grad_weight,
    )


def solution(mesh):
    fine = Mesh(mesh.devices.reshape(2, 2, 4, 2, 4), ALL)
    tokens = P(DP, CTX, None)
    in_specs = (tokens, tokens, tokens, P(), P(), P(), P(), tokens)
    out_specs = (tokens, tokens, tokens, tokens, P(), P(), P(), P(CTX, None))
    return jax.shard_map(
        shards, mesh=fine, in_specs=in_specs, out_specs=out_specs, check_vma=False
    )
```

```python
import math

import jax
import jax.numpy as jnp
from jax import lax
from jax.experimental import pallas as pl
from jax.experimental.pallas import tpu as pltpu
from jax.sharding import Mesh
from jax.sharding import PartitionSpec as P

F32 = jnp.float32
BF16 = jnp.bfloat16
CTX = ("xh", "co")
DP = ("y", "xl", "z")
CHIPS = ("xh", "y", "xl", "z")
ALL = ("xh", "co", "y", "xl", "z")

ROWS = 256
CHANS = 256
GROUPS = 16
LENGTH = 1024
STRIP = 32
PAD = 128
WIDE = LENGTH + PAD
FEATS = 8192
SMALL = 32
TAIL = 16
SHARES = 32
SHARE = FEATS // 4
SEGMENT = 8
SPREAD = 4
PIECES = 8
VMEM_LIMIT = 24 * 1024 * 1024


def call(kernel, name, out_shape, operands, scratch=(), scalars=0, flops=1 << 10, **more):
    spec = pl.BlockSpec(memory_space=pltpu.VMEM)
    in_specs = [pl.BlockSpec(memory_space=pltpu.SMEM)] * scalars
    in_specs += [spec] * (len(operands) - scalars)
    defaults = {"in_specs": in_specs, "out_specs": jax.tree.map(lambda _: spec, out_shape)}
    more = {**defaults, **more}
    placed = [
        x if s.memory_space == pltpu.SMEM else pltpu.with_memory_space_constraint(x, s.memory_space)
        for x, s in zip(operands, more["in_specs"])
    ]
    return pl.pallas_call(
        kernel,
        out_shape=out_shape,
        scratch_shapes=list(scratch),
        compiler_params=pltpu.CompilerParams(vmem_limit_bytes=VMEM_LIMIT),
        cost_estimate=pl.CostEstimate(flops=flops, bytes_accessed=1 << 10, transcendentals=0),
        name=name,
        **more,
    )(*placed)


def lane_groups(rows):
    return lax.broadcasted_iota(jnp.int32, (rows, CHANS), 1) // (CHANS // GROUPS)


def later(x, count):
    row = lax.broadcasted_iota(jnp.int32, x.shape, 0)
    return jnp.where(row >= count, pltpu.roll(x, count, 0), 0.0)


def strip_of(line):
    wide = jnp.broadcast_to(line, (STRIP, WIDE))
    return pltpu.roll(wide, 0, 1, stride=1, stride_axis=0)[:, :LENGTH].astype(BF16)


def pick_groups(result):
    ids = lane_groups(STRIP)
    out = jnp.zeros((STRIP, CHANS), F32)
    for g in range(GROUPS):
        out = jnp.where(ids == g, result[g * STRIP : (g + 1) * STRIP], out)
    return out


def all_strips(strips_ref, signal_ref):
    parts = []
    for n in range(ROWS // STRIP):
        window = signal_ref[n * STRIP : n * STRIP + LENGTH, :]
        parts.append(pick_groups(jnp.dot(strips_ref[...], window, preferred_element_type=F32)))
    return jnp.concatenate(parts, axis=0)


def with_tail(tail, block):
    joined = jnp.concatenate([tail.astype(F32), block.astype(F32)], axis=0)
    return joined[TAIL:], pltpu.roll(joined, 1, 0)[TAIL:], pltpu.roll(joined, 2, 0)[TAIL:]


def short_sum(taps_ref, i, parts):
    return sum(taps_ref[i, j : j + 1, :] * parts[j] for j in range(3))


def lines_of(filter_ref, turned):
    if not turned:
        return jnp.concatenate(
            [filter_ref[...].astype(F32), jnp.zeros((GROUPS, PAD), F32)], axis=1
        )
    row = lax.broadcasted_iota(jnp.int32, (CHANS, CHANS), 0)
    col = lax.broadcasted_iota(jnp.int32, (CHANS, CHANS), 1)
    turn = (row + col == CHANS - 1).astype(F32).astype(BF16)
    pieces = [
        jnp.dot(filter_ref[:, n * CHANS : (n + 1) * CHANS], turn, preferred_element_type=F32)
        for n in reversed(range(LENGTH // CHANS))
    ]
    wide = jnp.concatenate([*pieces, jnp.zeros((GROUPS, PAD), F32)], axis=1)
    return pltpu.roll(wide, WIDE - (STRIP - 1), 1)


def pre_kernel(
    cot_ref, weight_ref, filter_ref, d_gated_ref, strips_ref, cot_buffer, weight_buffer, sems
):
    tile = FEATS // PIECES
    copies = []
    for n in range(PIECES):
        piece = slice(n * tile, (n + 1) * tile)
        pair = (
            pltpu.make_async_copy(cot_ref.at[:, piece], cot_buffer.at[n], sems.at[0, n]),
            pltpu.make_async_copy(weight_ref.at[piece, :], weight_buffer.at[n], sems.at[1, n]),
        )
        for copy in pair:
            copy.start()
        copies.append(pair)
    lines = lines_of(filter_ref, True)
    for g in range(GROUPS):
        strips_ref[g * STRIP : (g + 1) * STRIP, :] = strip_of(lines[g : g + 1])
    total = jnp.zeros((ROWS, CHANS), F32)
    for n in range(PIECES):
        for copy in copies[n]:
            copy.wait()
        total += jnp.dot(cot_buffer[n], weight_buffer[n], preferred_element_type=F32)
    d_gated_ref[...] = total.astype(BF16)


def pre_call(cot, weight, lags):
    out_shape = [
        pltpu.VMEM((ROWS, CHANS), BF16),
        pltpu.VMEM((GROUPS * STRIP, LENGTH), BF16),
    ]
    tile = FEATS // PIECES
    scratch = [
        pltpu.VMEM((PIECES, ROWS, tile), BF16),
        pltpu.VMEM((PIECES, tile, CHANS), BF16),
        pltpu.SemaphoreType.DMA((2, PIECES)),
    ]
    far = pl.BlockSpec(memory_space=pltpu.HBM)
    in_specs = [far, far, pl.BlockSpec(memory_space=pltpu.VMEM)]
    return call(
        pre_kernel, "pre", out_shape, (cot, weight, lags), scratch, in_specs=in_specs, flops=1 << 30
    )


def d_inner_kernel(d_gated_ref, query_ref, tail_ref, taps_ref, out_ref):
    q_short = short_sum(taps_ref, 0, with_tail(tail_ref[...], query_ref[...]))
    out_ref[...] = (d_gated_ref[...].astype(F32) * q_short).astype(BF16)


def d_inner_call(*operands):
    return call(d_inner_kernel, "d_inner", pltpu.VMEM((ROWS, CHANS), BF16), operands)


def fwd_kernel(
    core_ref, strips_ref, pair_ref, cross_ref, cross_pair_ref, key_ref, value_ref, query_ref,
    tail_ref, taps_ref, skip_ref,
    gated_ref, inner_ref, mixed_ref,
    signal_ref,
):
    upper = core_ref[0] == 1
    pair = pair_ref[...].astype(F32)
    cross_pair = cross_pair_ref[...].astype(F32)
    near = jnp.where(upper, pair, cross_pair)
    far = jnp.where(upper, cross_pair, 0.0)
    own = jnp.concatenate([key_ref[...], value_ref[...]], axis=1).astype(F32)
    both = jnp.concatenate([far, cross_ref[...].astype(F32), near, own], axis=0)
    shifted = (both, later(both, 1), later(both, 2))
    k_short = short_sum(taps_ref, 1, [part[:, :CHANS] for part in shifted])
    v_short = short_sum(taps_ref, 2, [part[:, CHANS:] for part in shifted])
    mixed = (k_short * v_short).astype(BF16)
    mixed_ref[...] = mixed[LENGTH - ROWS :]
    signal_ref[: ROWS - STRIP, :] = jnp.zeros((ROWS - STRIP, CHANS), BF16)
    signal_ref[ROWS - STRIP :, :] = mixed
    inner = all_strips(strips_ref, signal_ref) + skip_ref[...] * mixed[LENGTH - ROWS :].astype(F32)
    inner_ref[...] = inner
    q_short = short_sum(taps_ref, 0, with_tail(tail_ref[...], query_ref[...]))
    gated_ref[...] = (q_short * inner).astype(BF16)


def fwd_call(*operands):
    out_shape = [
        pltpu.VMEM((ROWS, CHANS), BF16),
        pltpu.VMEM((ROWS, CHANS), F32),
        pltpu.VMEM((ROWS, CHANS), BF16),
    ]
    scratch = [pltpu.VMEM((LENGTH + ROWS - STRIP, CHANS), BF16)]
    return call(fwd_kernel, "fwd", out_shape, operands, scratch, 1, 4 << 30)


def terms_kernel(core_ref, own_cot_ref, other_cot_ref, gated_ref, other_gated_ref, out_ref):
    dims = (((0,), (0,)), ((), ()))
    for half in range(2):
        start = pl.multiple_of((2 * half + core_ref[0]) * SHARE, SHARE)
        own_cot = own_cot_ref[:, pl.ds(start, SHARE)]
        other_cot = other_cot_ref[:, pl.ds(start, SHARE)]
        total = lax.dot_general(gated_ref[...], own_cot, dims, preferred_element_type=F32)
        total += lax.dot_general(other_gated_ref[...], other_cot, dims, preferred_element_type=F32)
        out_ref[half, :, :SHARE] = total.astype(BF16)


def terms_call(*operands):
    out_shape = pltpu.VMEM((2, CHANS, SHARE + CHANS), BF16)
    return call(terms_kernel, "terms", out_shape, operands, scalars=1, flops=1 << 30)


def two_parts(total):
    rounded = total.astype(BF16).astype(F32)
    left = pltpu.roll(total - rounded, SEGMENT // 2, total.ndim - 2)
    return (rounded + left).astype(BF16)


def add_small_kernel(terms_ref, small_ref, other_small_ref, out_ref):
    parts = two_parts(small_ref[...] + other_small_ref[...]).astype(F32)
    parts = parts.reshape(CHANS, CHANS).astype(BF16)
    for half in range(2):
        out_ref[half, :, SHARE:] = parts


def add_small_call(*operands):
    out_shape = pltpu.VMEM(operands[0].shape, BF16)
    return call(add_small_kernel, "add_small", out_shape, operands, input_output_aliases={0: 0})


def place(g, n):
    row = g * (LENGTH // CHANS) + n
    return row % SHARES, row // SHARES


def bwd_kernel(
    core_ref, d0_ref, d1_ref, d2_ref, d3_ref, lags_ref, mixed_ref, key_ref, value_ref, pair_ref,
    cross_pair_ref, query_ref, tail_ref, inner_ref, d_gated_ref, taps_ref, skip_ref,
    d_short_ref, head_ref, small_ref,
    strips_ref, ahead_ref, outer_ref, stack_ref,
):
    for n, ref in enumerate((d0_ref, d1_ref, d2_ref, d3_ref)):
        ahead_ref[n * ROWS : (n + 1) * ROWS, :] = ref[...]
    ahead_ref[LENGTH:, :] = jnp.zeros((ROWS, CHANS), BF16)
    lines = lines_of(lags_ref, False)
    for g in range(GROUPS):
        strips_ref[g * STRIP : (g + 1) * STRIP, :] = strip_of(lines[g : g + 1])
    d_inner = d0_ref[...].astype(F32)
    mixed = mixed_ref[...]
    d_mixed = all_strips(strips_ref, ahead_ref) + skip_ref[...] * d_inner

    upper = core_ref[0] == 1
    last = slice(ROWS - TAIL, ROWS)
    near = jnp.where(upper, pair_ref[last, :].astype(F32), cross_pair_ref[last, :].astype(F32))
    k_parts = with_tail(near[:, :CHANS], key_ref[...])
    v_parts = with_tail(near[:, CHANS:], value_ref[...])
    q_parts = with_tail(tail_ref[...], query_ref[...])
    small_ref[...] = jnp.zeros_like(small_ref)
    d_qs = d_gated_ref[...].astype(F32) * inner_ref[...]
    d_ks = d_mixed * short_sum(taps_ref, 2, v_parts)
    d_vs = d_mixed * short_sum(taps_ref, 1, k_parts)
    for i, (grad, parts) in enumerate(((d_qs, q_parts), (d_ks, k_parts), (d_vs, v_parts))):
        d_short_ref[i] = grad
        head_ref[i] = grad[:8]
        for j in range(3):
            small_ref[3 * i + j, 2:3, :] = jnp.sum(grad * parts[j], axis=0, keepdims=True)
    small_ref[9, 2:3, :] = jnp.sum(d_inner * mixed.astype(F32), axis=0, keepdims=True)

    row = lax.broadcasted_iota(jnp.int32, (ROWS, ROWS), 0)
    col = lax.broadcasted_iota(jnp.int32, (ROWS, ROWS), 1)
    turn = ((row // SMALL) * SMALL + (SMALL - 1 - row % SMALL) == col).astype(F32).astype(BF16)
    turned = jnp.dot(turn, mixed, preferred_element_type=F32)
    ids = lane_groups(SMALL)
    for part in range(ROWS // SMALL):
        piece = turned[part * SMALL : (part + 1) * SMALL]
        for g in range(GROUPS):
            stack_ref[g * SMALL : (g + 1) * SMALL, :] = jnp.where(ids == g, piece, 0.0).astype(BF16)
        term = lax.dot_general(
            stack_ref[...],
            ahead_ref[part * SMALL : part * SMALL + LENGTH, :],
            (((1,), (1,)), ((), ())),
            preferred_element_type=F32,
        )
        if part == 0:
            outer_ref[:, :LENGTH] = term
        else:
            outer_ref[:, :LENGTH] += term
    outer_ref[:, LENGTH:] = jnp.zeros((GROUPS * SMALL, PAD), F32)
    for g in range(GROUPS):
        skewed = pltpu.roll(
            outer_ref[g * SMALL : (g + 1) * SMALL, :], WIDE - (SMALL - 1), 1, stride=1, stride_axis=0
        )
        sums = jnp.sum(skewed[:, :LENGTH], axis=0, keepdims=True)
        for n in range(LENGTH // CHANS):
            share, slot = place(g, n)
            small_ref[share, slot : slot + 1, :] = sums[:, n * CHANS : (n + 1) * CHANS]


def bwd_call(*operands):
    out_shape = [
        pltpu.VMEM((3, ROWS, CHANS), F32),
        pltpu.VMEM((3, 8, CHANS), F32),
        pltpu.VMEM((SHARES, SEGMENT, CHANS), F32),
    ]
    scratch = [
        pltpu.VMEM((GROUPS * STRIP, LENGTH), BF16),
        pltpu.VMEM((LENGTH + ROWS, CHANS), BF16),
        pltpu.VMEM((GROUPS * SMALL, WIDE), F32),
        pltpu.VMEM((GROUPS * SMALL, CHANS), BF16),
    ]
    return call(bwd_kernel, "bwd", out_shape, operands, scratch, 1)


def input_grad_kernel(d_short_ref, next_ref, taps_ref, query_ref, key_ref, value_ref):
    for i, out_ref in enumerate((query_ref, key_ref, value_ref)):
        joined = jnp.concatenate([d_short_ref[i], next_ref[i]], axis=0)
        rows = joined.shape[0]
        parts = (
            joined[:ROWS],
            pltpu.roll(joined, rows - 1, 0)[:ROWS],
            pltpu.roll(joined, rows - 2, 0)[:ROWS],
        )
        out_ref[...] = short_sum(taps_ref, i, parts).astype(BF16)


def input_grad_call(*operands):
    out_shape = [jax.ShapeDtypeStruct((ROWS, CHANS), BF16)] * 3
    return call(input_grad_kernel, "input_grads", out_shape, operands)


def total_kernel(scale, terms_ref, out_ref):
    total = jnp.sum(terms_ref[...].astype(F32), axis=0) * scale
    small = total[:, SHARE:]
    row = lax.broadcasted_iota(jnp.int32, small.shape, 0)
    small = jnp.where(row < SEGMENT // 2, small + pltpu.roll(small, SEGMENT // 2, 0), 0.0)
    total = jnp.concatenate([total[:, :SHARE].astype(BF16), two_parts(small)], axis=1)
    out_ref[...] = jnp.broadcast_to(total[None], out_ref.shape)


def total_call(terms, scale):
    out_shape = pltpu.VMEM((SHARES, *terms.shape[1:]), BF16)
    return call(lambda *refs: total_kernel(scale, *refs), "total", out_shape, (terms,))


def spread_kernel(
    shares_ref, weight_ref, taps_ref, filter_ref, skip_ref, turned_ref, sems
):
    tile = SHARE // SPREAD
    copies = []
    for n in range(SPREAD):
        piece = slice(n * tile, (n + 1) * tile)
        turned_ref[piece, :] = shares_ref[:, piece].astype(F32).T
        copies.append(
            pltpu.make_async_copy(turned_ref.at[piece, :], weight_ref.at[piece, :], sems.at[n])
        )
        copies[-1].start()
    for share in range(SHARES):
        segment = shares_ref[share * SEGMENT : (share + 1) * SEGMENT, SHARE:].astype(F32)
        segment = segment + pltpu.roll(segment, SEGMENT // 2, 0)
        for g in range(GROUPS):
            for n in range(LENGTH // CHANS):
                if place(g, n)[0] == share:
                    slot = place(g, n)[1]
                    filter_ref[g : g + 1, n * CHANS : (n + 1) * CHANS] = segment[slot : slot + 1]
        if share < 9:
            taps_ref[share // 3, share % 3 : share % 3 + 1, :] = segment[2:3]
        if share == 9:
            skip_ref[...] = segment[2:3]
    for copy in copies:
        copy.wait()


def spread_call(shares):
    out_shape = [
        jax.ShapeDtypeStruct((SHARE, CHANS), F32),
        jax.ShapeDtypeStruct((3, 3, CHANS), F32),
        jax.ShapeDtypeStruct((GROUPS, LENGTH), F32),
        jax.ShapeDtypeStruct((1, CHANS), F32),
    ]
    scratch = [pltpu.VMEM((SHARE, CHANS), F32), pltpu.SemaphoreType.DMA((SPREAD,))]
    out_specs = [pl.BlockSpec(memory_space=pl.ANY)]
    out_specs += [pl.BlockSpec(memory_space=pltpu.VMEM)] * 3
    shares = shares.reshape(CHANS, SHARE + CHANS)
    return call(spread_kernel, "spread", out_shape, (shares,), scratch, out_specs=out_specs)


def sent(block, distance):
    count = 4
    route = [(i, i + distance) for i in range(count) if 0 <= i + distance < count]
    return lax.ppermute(block, CTX, route)


def shards(
    query_in, key_in, value_in, short_taps, long_filter, skip_gain, out_weight, out_cotangent
):
    query = query_in[0]
    cot = out_cotangent[0]
    taps = short_taps
    skip = skip_gain.reshape(1, CHANS)
    devices = lax.axis_size(ALL)
    tokens = ROWS * devices
    scale = 1.0 / math.sqrt(tokens)
    core = lax.axis_index("co").astype(jnp.int32).reshape(1)

    key = key_in[0]
    value = value_in[0]
    swap = [(0, 1), (1, 0)]
    own = jnp.concatenate([key, value], axis=1)
    tail = sent(query[ROWS - TAIL :], 1)
    cross = lax.ppermute(own, "xh", [(0, 1)])
    pair = lax.ppermute(own, "co", swap)
    other_cot = lax.ppermute(cot, "co", swap)

    d_gated, strips = pre_call(cot, out_weight, long_filter)
    cross, tail, d_gated, strips = lax.optimization_barrier((cross, tail, d_gated, strips))
    cross_pair = lax.ppermute(cross, "co", swap)
    d_inner = d_inner_call(d_gated, query, tail, taps)
    blocks = [d_inner] + [sent(d_inner, -distance) for distance in (1, 2, 3)]
    gated, inner, mixed = fwd_call(
        core, strips, pair, cross, cross_pair, key, value, query, tail, taps, skip
    )
    other_gated = lax.ppermute(gated, "co", swap)
    d_short, head, small = bwd_call(
        core, *blocks, long_filter, mixed, key, value, pair, cross_pair, query, tail, inner,
        d_gated, taps, skip,
    )
    other_gated, head, small = lax.optimization_barrier((other_gated, head, small))
    other_small = lax.ppermute(small, "co", swap)
    following = sent(head, -1)
    terms = terms_call(core, cot, other_cot, gated, other_gated)
    terms, other_small, following = lax.optimization_barrier((terms, other_small, following))
    terms = add_small_call(terms, small, other_small)
    terms = terms.reshape(2 * SHARES, CHANS // SHARES, SHARE + CHANS)
    terms = lax.all_to_all(terms, CHIPS, 0, 0)
    grad_query, grad_key, grad_value = input_grad_call(d_short, following, taps)

    shares = lax.all_to_all(total_call(terms, scale), DP, 0, 0)
    grad_weight, grad_taps, grad_filter, grad_skip = spread_call(shares)
    return (
        gated[None],
        grad_query[None],
        grad_key[None],
        grad_value[None],
        grad_taps,
        grad_filter,
        grad_skip.reshape(CHANS),
        grad_weight,
    )


def solution(mesh):
    fine = Mesh(mesh.devices.reshape(2, 2, 4, 2, 4), ALL)
    tokens = P(DP, CTX, None)
    in_specs = (tokens, tokens, tokens, P(), P(), P(), P(), tokens)
    out_specs = (tokens, tokens, tokens, tokens, P(), P(), P(), P(CTX, None))
    return jax.shard_map(
        shards, mesh=fine, in_specs=in_specs, out_specs=out_specs, check_vma=False
    )
```

```python
import math

import jax
import jax.numpy as jnp
from jax import lax
from jax.experimental import pallas as pl
from jax.experimental.pallas import tpu as pltpu
from jax.sharding import Mesh
from jax.sharding import PartitionSpec as P

F32 = jnp.float32
BF16 = jnp.bfloat16
CTX = ("xh", "co")
DP = ("y", "xl", "z")
CHIPS = ("xh", "y", "xl", "z")
ALL = ("xh", "co", "y", "xl", "z")

ROWS = 256
CHANS = 256
GROUPS = 16
LENGTH = 1024
STRIP = 32
PAD = 128
WIDE = LENGTH + PAD
FEATS = 8192
SMALL = 32
TAIL = 16
SHARES = 32
SHARE = FEATS // 4
SEGMENT = 8
SPREAD = 4
PIECES = 8
VMEM_LIMIT = 24 * 1024 * 1024


def call(kernel, name, out_shape, operands, scratch=(), scalars=0, flops=1 << 10, **more):
    spec = pl.BlockSpec(memory_space=pltpu.VMEM)
    in_specs = [pl.BlockSpec(memory_space=pltpu.SMEM)] * scalars
    in_specs += [spec] * (len(operands) - scalars)
    defaults = {"in_specs": in_specs, "out_specs": jax.tree.map(lambda _: spec, out_shape)}
    more = {**defaults, **more}
    placed = [
        x if s.memory_space == pltpu.SMEM else pltpu.with_memory_space_constraint(x, s.memory_space)
        for x, s in zip(operands, more["in_specs"])
    ]
    return pl.pallas_call(
        kernel,
        out_shape=out_shape,
        scratch_shapes=list(scratch),
        compiler_params=pltpu.CompilerParams(vmem_limit_bytes=VMEM_LIMIT),
        cost_estimate=pl.CostEstimate(flops=flops, bytes_accessed=1 << 10, transcendentals=0),
        name=name,
        **more,
    )(*placed)


def lane_groups(rows):
    return lax.broadcasted_iota(jnp.int32, (rows, CHANS), 1) // (CHANS // GROUPS)


def later(x, count):
    row = lax.broadcasted_iota(jnp.int32, x.shape, 0)
    return jnp.where(row >= count, pltpu.roll(x, count, 0), 0.0)


def strip_of(line):
    wide = jnp.broadcast_to(line, (STRIP, WIDE))
    return pltpu.roll(wide, 0, 1, stride=1, stride_axis=0)[:, :LENGTH].astype(BF16)


def pick_groups(result):
    ids = lane_groups(STRIP)
    out = jnp.zeros((STRIP, CHANS), F32)
    for g in range(GROUPS):
        out = jnp.where(ids == g, result[g * STRIP : (g + 1) * STRIP], out)
    return out


def all_strips(strips_ref, signal_ref):
    parts = []
    for n in range(ROWS // STRIP):
        window = signal_ref[n * STRIP : n * STRIP + LENGTH, :]
        parts.append(pick_groups(jnp.dot(strips_ref[...], window, preferred_element_type=F32)))
    return jnp.concatenate(parts, axis=0)


def with_tail(tail, block):
    joined = jnp.concatenate([tail.astype(F32), block.astype(F32)], axis=0)
    return joined[TAIL:], pltpu.roll(joined, 1, 0)[TAIL:], pltpu.roll(joined, 2, 0)[TAIL:]


def short_sum(taps_ref, i, parts):
    return sum(taps_ref[i, j : j + 1, :] * parts[j] for j in range(3))


def lines_of(filter_ref, turned):
    if not turned:
        return jnp.concatenate(
            [filter_ref[...].astype(F32), jnp.zeros((GROUPS, PAD), F32)], axis=1
        )
    row = lax.broadcasted_iota(jnp.int32, (CHANS, CHANS), 0)
    col = lax.broadcasted_iota(jnp.int32, (CHANS, CHANS), 1)
    turn = (row + col == CHANS - 1).astype(F32).astype(BF16)
    pieces = [
        jnp.dot(filter_ref[:, n * CHANS : (n + 1) * CHANS], turn, preferred_element_type=F32)
        for n in reversed(range(LENGTH // CHANS))
    ]
    wide = jnp.concatenate([*pieces, jnp.zeros((GROUPS, PAD), F32)], axis=1)
    return pltpu.roll(wide, WIDE - (STRIP - 1), 1)


def d_gated_kernel(cot_ref, weight_ref, d_gated_ref, cot_buffer, weight_buffer, sems):
    tile = FEATS // PIECES
    copies = []
    for n in range(PIECES):
        piece = slice(n * tile, (n + 1) * tile)
        pair = (
            pltpu.make_async_copy(cot_ref.at[:, piece], cot_buffer.at[n], sems.at[0, n]),
            pltpu.make_async_copy(weight_ref.at[piece, :], weight_buffer.at[n], sems.at[1, n]),
        )
        for copy in pair:
            copy.start()
        copies.append(pair)
    total = jnp.zeros((ROWS, CHANS), F32)
    for n in range(PIECES):
        for copy in copies[n]:
            copy.wait()
        total += jnp.dot(cot_buffer[n], weight_buffer[n], preferred_element_type=F32)
    d_gated_ref[...] = total.astype(BF16)


def d_gated_call(cot, weight):
    tile = FEATS // PIECES
    scratch = [
        pltpu.VMEM((PIECES, ROWS, tile), BF16),
        pltpu.VMEM((PIECES, tile, CHANS), BF16),
        pltpu.SemaphoreType.DMA((2, PIECES)),
    ]
    in_specs = [pl.BlockSpec(memory_space=pltpu.HBM)] * 2
    out_shape = pltpu.VMEM((ROWS, CHANS), BF16)
    return call(
        d_gated_kernel, "d_gated", out_shape, (cot, weight), scratch, in_specs=in_specs,
        flops=1 << 30,
    )


def strips_kernel(filter_ref, strips_ref, back_strips_ref):
    for ref, turned in ((strips_ref, True), (back_strips_ref, False)):
        lines = lines_of(filter_ref, turned)
        for g in range(GROUPS):
            ref[g * STRIP : (g + 1) * STRIP, :] = strip_of(lines[g : g + 1])


def strips_call(lags):
    out_shape = [pltpu.VMEM((GROUPS * STRIP, LENGTH), BF16)] * 2
    return call(strips_kernel, "strips", out_shape, (lags,))


def d_inner_kernel(d_gated_ref, query_ref, tail_ref, taps_ref, out_ref):
    q_short = short_sum(taps_ref, 0, with_tail(tail_ref[...], query_ref[...]))
    out_ref[...] = (d_gated_ref[...].astype(F32) * q_short).astype(BF16)


def d_inner_call(*operands):
    return call(d_inner_kernel, "d_inner", pltpu.VMEM((ROWS, CHANS), BF16), operands)


def fwd_kernel(
    core_ref, strips_ref, pair_ref, cross_ref, cross_pair_ref, key_ref, value_ref, query_ref,
    tail_ref, taps_ref, skip_ref,
    gated_ref, inner_ref, mixed_ref,
    signal_ref,
):
    upper = core_ref[0] == 1
    pair = pair_ref[...].astype(F32)
    cross_pair = cross_pair_ref[...].astype(F32)
    near = jnp.where(upper, pair, cross_pair)
    far = jnp.where(upper, cross_pair, 0.0)
    own = jnp.concatenate([key_ref[...], value_ref[...]], axis=1).astype(F32)
    both = jnp.concatenate([far, cross_ref[...].astype(F32), near, own], axis=0)
    shifted = (both, later(both, 1), later(both, 2))
    k_short = short_sum(taps_ref, 1, [part[:, :CHANS] for part in shifted])
    v_short = short_sum(taps_ref, 2, [part[:, CHANS:] for part in shifted])
    mixed = (k_short * v_short).astype(BF16)
    mixed_ref[...] = mixed[LENGTH - ROWS :]
    signal_ref[: ROWS - STRIP, :] = jnp.zeros((ROWS - STRIP, CHANS), BF16)
    signal_ref[ROWS - STRIP :, :] = mixed
    inner = all_strips(strips_ref, signal_ref) + skip_ref[...] * mixed[LENGTH - ROWS :].astype(F32)
    inner_ref[...] = inner
    q_short = short_sum(taps_ref, 0, with_tail(tail_ref[...], query_ref[...]))
    gated_ref[...] = (q_short * inner).astype(BF16)


def fwd_call(*operands):
    out_shape = [
        pltpu.VMEM((ROWS, CHANS), BF16),
        pltpu.VMEM((ROWS, CHANS), F32),
        pltpu.VMEM((ROWS, CHANS), BF16),
    ]
    scratch = [pltpu.VMEM((LENGTH + ROWS - STRIP, CHANS), BF16)]
    return call(fwd_kernel, "fwd", out_shape, operands, scratch, 1, 4 << 30)


def terms_kernel(core_ref, own_cot_ref, other_cot_ref, gated_ref, other_gated_ref, out_ref):
    dims = (((0,), (0,)), ((), ()))
    for half in range(2):
        start = pl.multiple_of((2 * half + core_ref[0]) * SHARE, SHARE)
        own_cot = own_cot_ref[:, pl.ds(start, SHARE)]
        other_cot = other_cot_ref[:, pl.ds(start, SHARE)]
        total = lax.dot_general(gated_ref[...], own_cot, dims, preferred_element_type=F32)
        total += lax.dot_general(other_gated_ref[...], other_cot, dims, preferred_element_type=F32)
        out_ref[half, :, :SHARE] = total.astype(BF16)


def terms_call(*operands):
    out_shape = pltpu.VMEM((2, CHANS, SHARE + CHANS), BF16)
    return call(terms_kernel, "terms", out_shape, operands, scalars=1, flops=1 << 30)


def two_parts(total):
    rounded = total.astype(BF16).astype(F32)
    left = pltpu.roll(total - rounded, SEGMENT // 2, total.ndim - 2)
    return (rounded + left).astype(BF16)


def add_small_kernel(terms_ref, small_ref, other_small_ref, out_ref):
    parts = two_parts(small_ref[...] + other_small_ref[...]).astype(F32)
    parts = parts.reshape(CHANS, CHANS).astype(BF16)
    for half in range(2):
        out_ref[half, :, SHARE:] = parts


def add_small_call(*operands):
    out_shape = pltpu.VMEM(operands[0].shape, BF16)
    return call(add_small_kernel, "add_small", out_shape, operands, input_output_aliases={0: 0})


def place(g, n):
    row = g * (LENGTH // CHANS) + n
    return row % SHARES, row // SHARES


def bwd_kernel(
    core_ref, d0_ref, d1_ref, d2_ref, d3_ref, strips_ref, mixed_ref, key_ref, value_ref, pair_ref,
    cross_pair_ref, query_ref, tail_ref, inner_ref, d_gated_ref, taps_ref, skip_ref,
    d_short_ref, head_ref, small_ref,
    ahead_ref, outer_ref, stack_ref,
):
    for n, ref in enumerate((d0_ref, d1_ref, d2_ref, d3_ref)):
        ahead_ref[n * ROWS : (n + 1) * ROWS, :] = ref[...]
    ahead_ref[LENGTH:, :] = jnp.zeros((ROWS, CHANS), BF16)
    d_inner = d0_ref[...].astype(F32)
    mixed = mixed_ref[...]
    d_mixed = all_strips(strips_ref, ahead_ref) + skip_ref[...] * d_inner

    upper = core_ref[0] == 1
    last = slice(ROWS - TAIL, ROWS)
    near = jnp.where(upper, pair_ref[last, :].astype(F32), cross_pair_ref[last, :].astype(F32))
    k_parts = with_tail(near[:, :CHANS], key_ref[...])
    v_parts = with_tail(near[:, CHANS:], value_ref[...])
    q_parts = with_tail(tail_ref[...], query_ref[...])
    small_ref[...] = jnp.zeros_like(small_ref)
    d_qs = d_gated_ref[...].astype(F32) * inner_ref[...]
    d_ks = d_mixed * short_sum(taps_ref, 2, v_parts)
    d_vs = d_mixed * short_sum(taps_ref, 1, k_parts)
    for i, (grad, parts) in enumerate(((d_qs, q_parts), (d_ks, k_parts), (d_vs, v_parts))):
        d_short_ref[i] = grad
        head_ref[i] = grad[:8]
        for j in range(3):
            small_ref[3 * i + j, 2:3, :] = jnp.sum(grad * parts[j], axis=0, keepdims=True)
    small_ref[9, 2:3, :] = jnp.sum(d_inner * mixed.astype(F32), axis=0, keepdims=True)

    row = lax.broadcasted_iota(jnp.int32, (ROWS, ROWS), 0)
    col = lax.broadcasted_iota(jnp.int32, (ROWS, ROWS), 1)
    turn = ((row // SMALL) * SMALL + (SMALL - 1 - row % SMALL) == col).astype(F32).astype(BF16)
    turned = jnp.dot(turn, mixed, preferred_element_type=F32)
    ids = lane_groups(SMALL)
    for part in range(ROWS // SMALL):
        piece = turned[part * SMALL : (part + 1) * SMALL]
        for g in range(GROUPS):
            stack_ref[g * SMALL : (g + 1) * SMALL, :] = jnp.where(ids == g, piece, 0.0).astype(BF16)
        term = lax.dot_general(
            stack_ref[...],
            ahead_ref[part * SMALL : part * SMALL + LENGTH, :],
            (((1,), (1,)), ((), ())),
            preferred_element_type=F32,
        )
        if part == 0:
            outer_ref[:, :LENGTH] = term
        else:
            outer_ref[:, :LENGTH] += term
    outer_ref[:, LENGTH:] = jnp.zeros((GROUPS * SMALL, PAD), F32)
    for g in range(GROUPS):
        skewed = pltpu.roll(
            outer_ref[g * SMALL : (g + 1) * SMALL, :], WIDE - (SMALL - 1), 1, stride=1, stride_axis=0
        )
        sums = jnp.sum(skewed[:, :LENGTH], axis=0, keepdims=True)
        for n in range(LENGTH // CHANS):
            share, slot = place(g, n)
            small_ref[share, slot : slot + 1, :] = sums[:, n * CHANS : (n + 1) * CHANS]


def bwd_call(*operands):
    out_shape = [
        pltpu.VMEM((3, ROWS, CHANS), F32),
        pltpu.VMEM((3, 8, CHANS), F32),
        pltpu.VMEM((SHARES, SEGMENT, CHANS), F32),
    ]
    scratch = [
        pltpu.VMEM((LENGTH + ROWS, CHANS), BF16),
        pltpu.VMEM((GROUPS * SMALL, WIDE), F32),
        pltpu.VMEM((GROUPS * SMALL, CHANS), BF16),
    ]
    return call(bwd_kernel, "bwd", out_shape, operands, scratch, 1)


def input_grad_kernel(d_short_ref, next_ref, taps_ref, query_ref, key_ref, value_ref):
    for i, out_ref in enumerate((query_ref, key_ref, value_ref)):
        joined = jnp.concatenate([d_short_ref[i], next_ref[i]], axis=0)
        rows = joined.shape[0]
        parts = (
            joined[:ROWS],
            pltpu.roll(joined, rows - 1, 0)[:ROWS],
            pltpu.roll(joined, rows - 2, 0)[:ROWS],
        )
        out_ref[...] = short_sum(taps_ref, i, parts).astype(BF16)


def input_grad_call(*operands):
    out_shape = [jax.ShapeDtypeStruct((ROWS, CHANS), BF16)] * 3
    return call(input_grad_kernel, "input_grads", out_shape, operands)


def total_kernel(scale, terms_ref, out_ref):
    total = jnp.sum(terms_ref[...].astype(F32), axis=0) * scale
    small = total[:, SHARE:]
    row = lax.broadcasted_iota(jnp.int32, small.shape, 0)
    small = jnp.where(row < SEGMENT // 2, small + pltpu.roll(small, SEGMENT // 2, 0), 0.0)
    total = jnp.concatenate([total[:, :SHARE].astype(BF16), two_parts(small)], axis=1)
    out_ref[...] = jnp.broadcast_to(total[None], out_ref.shape)


def total_call(terms, scale):
    out_shape = pltpu.VMEM((SHARES, *terms.shape[1:]), BF16)
    return call(lambda *refs: total_kernel(scale, *refs), "total", out_shape, (terms,))


def spread_kernel(
    shares_ref, weight_ref, taps_ref, filter_ref, skip_ref, turned_ref, sems
):
    tile = SHARE // SPREAD
    copies = []
    for n in range(SPREAD):
        piece = slice(n * tile, (n + 1) * tile)
        turned_ref[piece, :] = shares_ref[:, piece].astype(F32).T
        copies.append(
            pltpu.make_async_copy(turned_ref.at[piece, :], weight_ref.at[piece, :], sems.at[n])
        )
        copies[-1].start()
    for share in range(SHARES):
        segment = shares_ref[share * SEGMENT : (share + 1) * SEGMENT, SHARE:].astype(F32)
        segment = segment + pltpu.roll(segment, SEGMENT // 2, 0)
        for g in range(GROUPS):
            for n in range(LENGTH // CHANS):
                if place(g, n)[0] == share:
                    slot = place(g, n)[1]
                    filter_ref[g : g + 1, n * CHANS : (n + 1) * CHANS] = segment[slot : slot + 1]
        if share < 9:
            taps_ref[share // 3, share % 3 : share % 3 + 1, :] = segment[2:3]
        if share == 9:
            skip_ref[...] = segment[2:3]
    for copy in copies:
        copy.wait()


def spread_call(shares):
    out_shape = [
        jax.ShapeDtypeStruct((SHARE, CHANS), F32),
        jax.ShapeDtypeStruct((3, 3, CHANS), F32),
        jax.ShapeDtypeStruct((GROUPS, LENGTH), F32),
        jax.ShapeDtypeStruct((1, CHANS), F32),
    ]
    scratch = [pltpu.VMEM((SHARE, CHANS), F32), pltpu.SemaphoreType.DMA((SPREAD,))]
    out_specs = [pl.BlockSpec(memory_space=pl.ANY)]
    out_specs += [pl.BlockSpec(memory_space=pltpu.VMEM)] * 3
    shares = shares.reshape(CHANS, SHARE + CHANS)
    return call(spread_kernel, "spread", out_shape, (shares,), scratch, out_specs=out_specs)


def sent(block, distance):
    count = 4
    route = [(i, i + distance) for i in range(count) if 0 <= i + distance < count]
    return lax.ppermute(block, CTX, route)


def shards(
    query_in, key_in, value_in, short_taps, long_filter, skip_gain, out_weight, out_cotangent
):
    query = query_in[0]
    cot = out_cotangent[0]
    taps = short_taps
    skip = skip_gain.reshape(1, CHANS)
    devices = lax.axis_size(ALL)
    tokens = ROWS * devices
    scale = 1.0 / math.sqrt(tokens)
    core = lax.axis_index("co").astype(jnp.int32).reshape(1)

    key = key_in[0]
    value = value_in[0]
    swap = [(0, 1), (1, 0)]
    own = jnp.concatenate([key, value], axis=1)
    tail = sent(query[ROWS - TAIL :], 1)
    cross = lax.ppermute(own, "xh", [(0, 1)])
    pair = lax.ppermute(own, "co", swap)
    other_cot = lax.ppermute(cot, "co", swap)

    d_gated = d_gated_call(cot, out_weight)
    cross, tail, d_gated, lags = lax.optimization_barrier((cross, tail, d_gated, long_filter))
    cross_pair = lax.ppermute(cross, "co", swap)
    strips, back_strips = strips_call(lags)
    d_inner = d_inner_call(d_gated, query, tail, taps)
    blocks = [d_inner] + [sent(d_inner, -distance) for distance in (1, 2, 3)]
    gated, inner, mixed = fwd_call(
        core, strips, pair, cross, cross_pair, key, value, query, tail, taps, skip
    )
    other_gated = lax.ppermute(gated, "co", swap)
    terms = terms_call(core, cot, other_cot, gated, other_gated)
    terms, inner, *blocks = lax.optimization_barrier((terms, inner, *blocks))
    d_short, head, small = bwd_call(
        core, *blocks, back_strips, mixed, key, value, pair, cross_pair, query, tail, inner,
        d_gated, taps, skip,
    )
    other_small = lax.ppermute(small, "co", swap)
    following = sent(head, -1)
    terms = add_small_call(terms, small, other_small)
    terms, following = lax.optimization_barrier((terms, following))
    terms = terms.reshape(2 * SHARES, CHANS // SHARES, SHARE + CHANS)
    terms = lax.all_to_all(terms, CHIPS, 0, 0)
    grad_query, grad_key, grad_value = input_grad_call(d_short, following, taps)

    shares = lax.all_to_all(total_call(terms, scale), DP, 0, 0)
    grad_weight, grad_taps, grad_filter, grad_skip = spread_call(shares)
    return (
        gated[None],
        grad_query[None],
        grad_key[None],
        grad_value[None],
        grad_taps,
        grad_filter,
        grad_skip.reshape(CHANS),
        grad_weight,
    )


def solution(mesh):
    fine = Mesh(mesh.devices.reshape(2, 2, 4, 2, 4), ALL)
    tokens = P(DP, CTX, None)
    in_specs = (tokens, tokens, tokens, P(), P(), P(), P(), tokens)
    out_specs = (tokens, tokens, tokens, tokens, P(), P(), P(), P(CTX, None))
    return jax.shard_map(
        shards, mesh=fine, in_specs=in_specs, out_specs=out_specs, check_vma=False
    )
```

```python
import math

import jax
import jax.numpy as jnp
from jax import lax
from jax.experimental import pallas as pl
from jax.experimental.pallas import tpu as pltpu
from jax.sharding import Mesh
from jax.sharding import PartitionSpec as P

F32 = jnp.float32
BF16 = jnp.bfloat16
CTX = ("xh", "co")
DP = ("y", "xl", "z")
CHIPS = ("xh", "y", "xl", "z")
ALL = ("xh", "co", "y", "xl", "z")

ROWS = 256
CHANS = 256
GROUPS = 16
LENGTH = 1024
STRIP = 32
PAD = 128
WIDE = LENGTH + PAD
FEATS = 8192
SMALL = 32
TAIL = 16
SHARES = 32
SHARE = FEATS // 4
SEGMENT = 8
SPREAD = 4
PIECES = 8
VMEM_LIMIT = 20 * 1024 * 1024


def call(kernel, name, out_shape, operands, scratch=(), scalars=0, flops=1 << 10, **more):
    spec = pl.BlockSpec(memory_space=pltpu.VMEM)
    in_specs = [pl.BlockSpec(memory_space=pltpu.SMEM)] * scalars
    in_specs += [spec] * (len(operands) - scalars)
    defaults = {"in_specs": in_specs, "out_specs": jax.tree.map(lambda _: spec, out_shape)}
    more = {**defaults, **more}
    placed = [
        x if s.memory_space == pltpu.SMEM else pltpu.with_memory_space_constraint(x, s.memory_space)
        for x, s in zip(operands, more["in_specs"])
    ]
    return pl.pallas_call(
        kernel,
        out_shape=out_shape,
        scratch_shapes=list(scratch),
        compiler_params=pltpu.CompilerParams(vmem_limit_bytes=VMEM_LIMIT),
        cost_estimate=pl.CostEstimate(flops=flops, bytes_accessed=1 << 10, transcendentals=0),
        name=name,
        **more,
    )(*placed)


def lane_groups(rows):
    return lax.broadcasted_iota(jnp.int32, (rows, CHANS), 1) // (CHANS // GROUPS)


def later(x, count):
    row = lax.broadcasted_iota(jnp.int32, x.shape, 0)
    return jnp.where(row >= count, pltpu.roll(x, count, 0), 0.0)


def strip_of(line):
    wide = jnp.broadcast_to(line, (STRIP, WIDE))
    return pltpu.roll(wide, 0, 1, stride=1, stride_axis=0)[:, :LENGTH].astype(BF16)


def pick_groups(result):
    ids = lane_groups(STRIP)
    out = jnp.zeros((STRIP, CHANS), F32)
    for g in range(GROUPS):
        out = jnp.where(ids == g, result[g * STRIP : (g + 1) * STRIP], out)
    return out


def all_strips(strips_ref, signal_ref):
    parts = []
    for n in range(ROWS // STRIP):
        window = signal_ref[n * STRIP : n * STRIP + LENGTH, :]
        parts.append(pick_groups(jnp.dot(strips_ref[...], window, preferred_element_type=F32)))
    return jnp.concatenate(parts, axis=0)


def with_tail(tail, block):
    joined = jnp.concatenate([tail.astype(F32), block.astype(F32)], axis=0)
    return joined[TAIL:], pltpu.roll(joined, 1, 0)[TAIL:], pltpu.roll(joined, 2, 0)[TAIL:]


def short_sum(taps_ref, i, parts):
    return sum(taps_ref[i, j : j + 1, :] * parts[j] for j in range(3))


def lines_of(filter_ref, turned):
    if not turned:
        return jnp.concatenate(
            [filter_ref[...].astype(F32), jnp.zeros((GROUPS, PAD), F32)], axis=1
        )
    row = lax.broadcasted_iota(jnp.int32, (CHANS, CHANS), 0)
    col = lax.broadcasted_iota(jnp.int32, (CHANS, CHANS), 1)
    turn = (row + col == CHANS - 1).astype(F32).astype(BF16)
    pieces = [
        jnp.dot(filter_ref[:, n * CHANS : (n + 1) * CHANS], turn, preferred_element_type=F32)
        for n in reversed(range(LENGTH // CHANS))
    ]
    wide = jnp.concatenate([*pieces, jnp.zeros((GROUPS, PAD), F32)], axis=1)
    return pltpu.roll(wide, WIDE - (STRIP - 1), 1)


def pre_kernel(
    cot_ref, weight_ref, filter_ref, d_gated_ref, strips_ref, back_strips_ref, cot_buffer,
    weight_buffer, sems,
):
    tile = FEATS // PIECES
    copies = []
    for n in range(PIECES):
        piece = slice(n * tile, (n + 1) * tile)
        pair = (
            pltpu.make_async_copy(cot_ref.at[:, piece], cot_buffer.at[n], sems.at[0, n]),
            pltpu.make_async_copy(weight_ref.at[piece, :], weight_buffer.at[n], sems.at[1, n]),
        )
        for copy in pair:
            copy.start()
        copies.append(pair)
    for ref, turned in ((strips_ref, True), (back_strips_ref, False)):
        lines = lines_of(filter_ref, turned)
        for g in range(GROUPS):
            ref[g * STRIP : (g + 1) * STRIP, :] = strip_of(lines[g : g + 1])
    total = jnp.zeros((ROWS, CHANS), F32)
    for n in range(PIECES):
        for copy in copies[n]:
            copy.wait()
        total += jnp.dot(cot_buffer[n], weight_buffer[n], preferred_element_type=F32)
    d_gated_ref[...] = total.astype(BF16)


def pre_call(*operands):
    tile = FEATS // PIECES
    scratch = [
        pltpu.VMEM((PIECES, ROWS, tile), BF16),
        pltpu.VMEM((PIECES, tile, CHANS), BF16),
        pltpu.SemaphoreType.DMA((2, PIECES)),
    ]
    in_specs = [pl.BlockSpec(memory_space=pltpu.HBM)] * 2 + [pl.BlockSpec(memory_space=pltpu.VMEM)]
    out_shape = [pltpu.VMEM((ROWS, CHANS), BF16)]
    out_shape += [pltpu.VMEM((GROUPS * STRIP, LENGTH), BF16)] * 2
    return call(pre_kernel, "pre", out_shape, operands, scratch, in_specs=in_specs, flops=1 << 30)


def d_inner_kernel(d_gated_ref, query_ref, tail_ref, taps_ref, out_ref):
    q_short = short_sum(taps_ref, 0, with_tail(tail_ref[...], query_ref[...]))
    out_ref[...] = (d_gated_ref[...].astype(F32) * q_short).astype(BF16)


def d_inner_call(*operands):
    return call(d_inner_kernel, "d_inner", pltpu.VMEM((ROWS, CHANS), BF16), operands)


def fwd_kernel(
    core_ref, strips_ref, pair_ref, cross_ref, cross_pair_ref, key_ref, value_ref, query_ref,
    tail_ref, taps_ref, skip_ref,
    gated_ref, inner_ref, mixed_ref,
    signal_ref,
):
    upper = core_ref[0] == 1
    pair = pair_ref[...].astype(F32)
    cross_pair = cross_pair_ref[...].astype(F32)
    near = jnp.where(upper, pair, cross_pair)
    far = jnp.where(upper, cross_pair, 0.0)
    own = jnp.concatenate([key_ref[...], value_ref[...]], axis=1).astype(F32)
    both = jnp.concatenate([far, cross_ref[...].astype(F32), near, own], axis=0)
    shifted = (both, later(both, 1), later(both, 2))
    k_short = short_sum(taps_ref, 1, [part[:, :CHANS] for part in shifted])
    v_short = short_sum(taps_ref, 2, [part[:, CHANS:] for part in shifted])
    mixed = (k_short * v_short).astype(BF16)
    mixed_ref[...] = mixed[LENGTH - ROWS :]
    signal_ref[: ROWS - STRIP, :] = jnp.zeros((ROWS - STRIP, CHANS), BF16)
    signal_ref[ROWS - STRIP :, :] = mixed
    inner = all_strips(strips_ref, signal_ref) + skip_ref[...] * mixed[LENGTH - ROWS :].astype(F32)
    inner_ref[...] = inner
    q_short = short_sum(taps_ref, 0, with_tail(tail_ref[...], query_ref[...]))
    gated_ref[...] = (q_short * inner).astype(BF16)


def fwd_call(*operands):
    out_shape = [
        pltpu.VMEM((ROWS, CHANS), BF16),
        pltpu.VMEM((ROWS, CHANS), F32),
        pltpu.VMEM((ROWS, CHANS), BF16),
    ]
    scratch = [pltpu.VMEM((LENGTH + ROWS - STRIP, CHANS), BF16)]
    return call(fwd_kernel, "fwd", out_shape, operands, scratch, 1, 4 << 30)


def terms_kernel(core_ref, own_cot_ref, other_cot_ref, gated_ref, other_gated_ref, out_ref):
    dims = (((0,), (0,)), ((), ()))
    for half in range(2):
        start = pl.multiple_of((2 * half + core_ref[0]) * SHARE, SHARE)
        own_cot = own_cot_ref[:, pl.ds(start, SHARE)]
        other_cot = other_cot_ref[:, pl.ds(start, SHARE)]
        total = lax.dot_general(gated_ref[...], own_cot, dims, preferred_element_type=F32)
        total += lax.dot_general(other_gated_ref[...], other_cot, dims, preferred_element_type=F32)
        out_ref[half, :, :SHARE] = total.astype(BF16)


def terms_call(*operands):
    out_shape = pltpu.VMEM((2, CHANS, SHARE + CHANS), BF16)
    return call(terms_kernel, "terms", out_shape, operands, scalars=1, flops=1 << 30)


def two_parts(total):
    rounded = total.astype(BF16).astype(F32)
    left = pltpu.roll(total - rounded, SEGMENT // 2, total.ndim - 2)
    return (rounded + left).astype(BF16)


def add_small_kernel(terms_ref, small_ref, other_small_ref, out_ref, parts_ref, sems):
    parts = two_parts(small_ref[...] + other_small_ref[...]).astype(F32)
    parts_ref[...] = parts.reshape(CHANS, CHANS).astype(BF16)
    copies = [
        pltpu.make_async_copy(parts_ref, out_ref.at[half, :, pl.ds(SHARE, CHANS)], sems.at[half])
        for half in range(2)
    ]
    for copy in copies:
        copy.start()
    for copy in copies:
        copy.wait()


def add_small_call(*operands):
    place = pl.BlockSpec(memory_space=pl.ANY)
    spec = pl.BlockSpec(memory_space=pltpu.VMEM)
    return pl.pallas_call(
        add_small_kernel,
        in_specs=[place, spec, spec],
        out_specs=place,
        out_shape=jax.ShapeDtypeStruct(operands[0].shape, BF16),
        scratch_shapes=[pltpu.VMEM((CHANS, CHANS), BF16), pltpu.SemaphoreType.DMA((2,))],
        input_output_aliases={0: 0},
        compiler_params=pltpu.CompilerParams(vmem_limit_bytes=VMEM_LIMIT),
        name="add_small",
    )(
        operands[0],
        *(pltpu.with_memory_space_constraint(x, pltpu.VMEM) for x in operands[1:]),
    )


def place(g, n):
    row = g * (LENGTH // CHANS) + n
    return row % SHARES, row // SHARES


def bwd_kernel(
    core_ref, d0_ref, d1_ref, d2_ref, d3_ref, strips_ref, mixed_ref, key_ref, value_ref, pair_ref,
    cross_pair_ref, query_ref, tail_ref, inner_ref, d_gated_ref, taps_ref, skip_ref,
    d_short_ref, head_ref, small_ref,
    ahead_ref, outer_ref, stack_ref,
):
    for n, ref in enumerate((d0_ref, d1_ref, d2_ref, d3_ref)):
        ahead_ref[n * ROWS : (n + 1) * ROWS, :] = ref[...]
    ahead_ref[LENGTH:, :] = jnp.zeros((ROWS, CHANS), BF16)
    d_inner = d0_ref[...].astype(F32)
    mixed = mixed_ref[...]
    d_mixed = all_strips(strips_ref, ahead_ref) + skip_ref[...] * d_inner

    upper = core_ref[0] == 1
    last = slice(ROWS - TAIL, ROWS)
    near = jnp.where(upper, pair_ref[last, :].astype(F32), cross_pair_ref[last, :].astype(F32))
    k_parts = with_tail(near[:, :CHANS], key_ref[...])
    v_parts = with_tail(near[:, CHANS:], value_ref[...])
    q_parts = with_tail(tail_ref[...], query_ref[...])
    small_ref[...] = jnp.zeros_like(small_ref)
    d_qs = d_gated_ref[...].astype(F32) * inner_ref[...]
    d_ks = d_mixed * short_sum(taps_ref, 2, v_parts)
    d_vs = d_mixed * short_sum(taps_ref, 1, k_parts)
    for i, (grad, parts) in enumerate(((d_qs, q_parts), (d_ks, k_parts), (d_vs, v_parts))):
        d_short_ref[i] = grad
        head_ref[i] = grad[:8]
        for j in range(3):
            small_ref[3 * i + j, 2:3, :] = jnp.sum(grad * parts[j], axis=0, keepdims=True)
    small_ref[9, 2:3, :] = jnp.sum(d_inner * mixed.astype(F32), axis=0, keepdims=True)

    row = lax.broadcasted_iota(jnp.int32, (ROWS, ROWS), 0)
    col = lax.broadcasted_iota(jnp.int32, (ROWS, ROWS), 1)
    turn = ((row // SMALL) * SMALL + (SMALL - 1 - row % SMALL) == col).astype(F32).astype(BF16)
    turned = jnp.dot(turn, mixed, preferred_element_type=F32)
    ids = lane_groups(SMALL)
    for part in range(ROWS // SMALL):
        piece = turned[part * SMALL : (part + 1) * SMALL]
        for g in range(GROUPS):
            stack_ref[g * SMALL : (g + 1) * SMALL, :] = jnp.where(ids == g, piece, 0.0).astype(BF16)
        term = lax.dot_general(
            stack_ref[...],
            ahead_ref[part * SMALL : part * SMALL + LENGTH, :],
            (((1,), (1,)), ((), ())),
            preferred_element_type=F32,
        )
        if part == 0:
            outer_ref[:, :LENGTH] = term
        else:
            outer_ref[:, :LENGTH] += term
    outer_ref[:, LENGTH:] = jnp.zeros((GROUPS * SMALL, PAD), F32)
    for g in range(GROUPS):
        skewed = pltpu.roll(
            outer_ref[g * SMALL : (g + 1) * SMALL, :], WIDE - (SMALL - 1), 1, stride=1, stride_axis=0
        )
        sums = jnp.sum(skewed[:, :LENGTH], axis=0, keepdims=True)
        for n in range(LENGTH // CHANS):
            share, slot = place(g, n)
            small_ref[share, slot : slot + 1, :] = sums[:, n * CHANS : (n + 1) * CHANS]


def bwd_call(*operands):
    out_shape = [
        pltpu.VMEM((3, ROWS, CHANS), F32),
        pltpu.VMEM((3, 8, CHANS), F32),
        pltpu.VMEM((SHARES, SEGMENT, CHANS), F32),
    ]
    scratch = [
        pltpu.VMEM((LENGTH + ROWS, CHANS), BF16),
        pltpu.VMEM((GROUPS * SMALL, WIDE), F32),
        pltpu.VMEM((GROUPS * SMALL, CHANS), BF16),
    ]
    return call(bwd_kernel, "bwd", out_shape, operands, scratch, 1)


def input_grad_kernel(d_short_ref, next_ref, taps_ref, query_ref, key_ref, value_ref):
    for i, out_ref in enumerate((query_ref, key_ref, value_ref)):
        joined = jnp.concatenate([d_short_ref[i], next_ref[i]], axis=0)
        rows = joined.shape[0]
        parts = (
            joined[:ROWS],
            pltpu.roll(joined, rows - 1, 0)[:ROWS],
            pltpu.roll(joined, rows - 2, 0)[:ROWS],
        )
        out_ref[...] = short_sum(taps_ref, i, parts).astype(BF16)


def input_grad_call(*operands):
    out_shape = [jax.ShapeDtypeStruct((ROWS, CHANS), BF16)] * 3
    return call(input_grad_kernel, "input_grads", out_shape, operands)


def total_kernel(scale, terms_ref, out_ref):
    total = jnp.sum(terms_ref[...].astype(F32), axis=0) * scale
    small = total[:, SHARE:]
    row = lax.broadcasted_iota(jnp.int32, small.shape, 0)
    small = jnp.where(row < SEGMENT // 2, small + pltpu.roll(small, SEGMENT // 2, 0), 0.0)
    total = jnp.concatenate([total[:, :SHARE].astype(BF16), two_parts(small)], axis=1)
    out_ref[...] = jnp.broadcast_to(total[None], out_ref.shape)


def total_call(terms, scale):
    out_shape = pltpu.VMEM((SHARES, *terms.shape[1:]), BF16)
    return call(lambda *refs: total_kernel(scale, *refs), "total", out_shape, (terms,))


def spread_kernel(
    shares_ref, weight_ref, taps_ref, filter_ref, skip_ref, turned_ref, sems
):
    tile = SHARE // SPREAD
    copies = []
    for n in range(SPREAD):
        piece = slice(n * tile, (n + 1) * tile)
        turned_ref[piece, :] = shares_ref[:, piece].astype(F32).T
        copies.append(
            pltpu.make_async_copy(turned_ref.at[piece, :], weight_ref.at[piece, :], sems.at[n])
        )
        copies[-1].start()
    for share in range(SHARES):
        segment = shares_ref[share * SEGMENT : (share + 1) * SEGMENT, SHARE:].astype(F32)
        segment = segment + pltpu.roll(segment, SEGMENT // 2, 0)
        for g in range(GROUPS):
            for n in range(LENGTH // CHANS):
                if place(g, n)[0] == share:
                    slot = place(g, n)[1]
                    filter_ref[g : g + 1, n * CHANS : (n + 1) * CHANS] = segment[slot : slot + 1]
        if share < 9:
            taps_ref[share // 3, share % 3 : share % 3 + 1, :] = segment[2:3]
        if share == 9:
            skip_ref[...] = segment[2:3]
    for copy in copies:
        copy.wait()


def spread_call(shares):
    out_shape = [
        jax.ShapeDtypeStruct((SHARE, CHANS), F32),
        jax.ShapeDtypeStruct((3, 3, CHANS), F32),
        jax.ShapeDtypeStruct((GROUPS, LENGTH), F32),
        jax.ShapeDtypeStruct((1, CHANS), F32),
    ]
    scratch = [pltpu.VMEM((SHARE, CHANS), F32), pltpu.SemaphoreType.DMA((SPREAD,))]
    out_specs = [pl.BlockSpec(memory_space=pl.ANY)]
    out_specs += [pl.BlockSpec(memory_space=pltpu.VMEM)] * 3
    shares = shares.reshape(CHANS, SHARE + CHANS)
    return call(spread_kernel, "spread", out_shape, (shares,), scratch, out_specs=out_specs)


def sent(block, distance):
    count = 4
    route = [(i, i + distance) for i in range(count) if 0 <= i + distance < count]
    return lax.ppermute(block, CTX, route)


def shards(
    query_in, key_in, value_in, short_taps, long_filter, skip_gain, out_weight, out_cotangent
):
    query = query_in[0]
    cot = out_cotangent[0]
    taps = short_taps
    skip = skip_gain.reshape(1, CHANS)
    devices = lax.axis_size(ALL)
    tokens = ROWS * devices
    scale = 1.0 / math.sqrt(tokens)
    core = lax.axis_index("co").astype(jnp.int32).reshape(1)

    key = key_in[0]
    value = value_in[0]
    swap = [(0, 1), (1, 0)]
    own = jnp.concatenate([key, value], axis=1)
    tail = sent(query[ROWS - TAIL :], 1)
    cross = lax.ppermute(own, "xh", [(0, 1)])
    pair = lax.ppermute(own, "co", swap)
    other_cot = lax.ppermute(cot, "co", swap)

    d_gated, strips, back_strips = pre_call(cot, out_weight, long_filter)
    cross, tail, d_gated = lax.optimization_barrier((cross, tail, d_gated))
    cross_pair = lax.ppermute(cross, "co", swap)
    d_inner = d_inner_call(d_gated, query, tail, taps)
    blocks = [d_inner] + [sent(d_inner, -distance) for distance in (1, 2, 3)]
    gated, inner, mixed = fwd_call(
        core, strips, pair, cross, cross_pair, key, value, query, tail, taps, skip
    )
    other_gated = lax.ppermute(gated, "co", swap)
    d_short, head, small = bwd_call(
        core, *blocks, back_strips, mixed, key, value, pair, cross_pair, query, tail, inner,
        d_gated, taps, skip,
    )
    other_gated, head, small = lax.optimization_barrier((other_gated, head, small))
    other_small = lax.ppermute(small, "co", swap)
    terms = terms_call(core, cot, other_cot, gated, other_gated)
    terms, other_small = lax.optimization_barrier((terms, other_small))
    terms = add_small_call(terms, small, other_small)
    terms, head = lax.optimization_barrier((terms, head))
    terms = terms.reshape(2 * SHARES, CHANS // SHARES, SHARE + CHANS)
    terms = lax.all_to_all(terms, CHIPS, 0, 0)
    following = sent(head, -1)
    grad_query, grad_key, grad_value = input_grad_call(d_short, following, taps)

    shares = lax.all_to_all(total_call(terms, scale), DP, 0, 0)
    grad_weight, grad_taps, grad_filter, grad_skip = spread_call(shares)
    return (
        gated[None],
        grad_query[None],
        grad_key[None],
        grad_value[None],
        grad_taps,
        grad_filter,
        grad_skip.reshape(CHANS),
        grad_weight,
    )


def solution(mesh):
    fine = Mesh(mesh.devices.reshape(2, 2, 4, 2, 4), ALL)
    tokens = P(DP, CTX, None)
    in_specs = (tokens, tokens, tokens, P(), P(), P(), P(), tokens)
    out_specs = (tokens, tokens, tokens, tokens, P(), P(), P(), P(CTX, None))
    return jax.shard_map(
        shards, mesh=fine, in_specs=in_specs, out_specs=out_specs, check_vma=False
    )
```

```python
import math

import jax
import jax.numpy as jnp
from jax import lax
from jax.experimental import pallas as pl
from jax.experimental.pallas import tpu as pltpu
from jax.sharding import Mesh
from jax.sharding import PartitionSpec as P

F32 = jnp.float32
BF16 = jnp.bfloat16
CTX = ("xh", "co")
DP = ("y", "xl", "z")
CHIPS = ("xh", "y", "xl", "z")
ALL = ("xh", "co", "y", "xl", "z")

ROWS = 256
CHANS = 256
GROUPS = 16
LENGTH = 1024
STRIP = 32
PAD = 128
WIDE = LENGTH + PAD
FEATS = 8192
TAIL = 16
SHARES = 32
SHARE = FEATS // 4
SEGMENT = 8
SPREAD = 4
PIECES = 8
VMEM_LIMIT = 20 * 1024 * 1024


def call(kernel, name, out_shape, operands, scratch=(), scalars=0, flops=1 << 10, **more):
    spec = pl.BlockSpec(memory_space=pltpu.VMEM)
    in_specs = [pl.BlockSpec(memory_space=pltpu.SMEM)] * scalars
    in_specs += [spec] * (len(operands) - scalars)
    defaults = {"in_specs": in_specs, "out_specs": jax.tree.map(lambda _: spec, out_shape)}
    more = {**defaults, **more}
    placed = [
        x if s.memory_space == pltpu.SMEM else pltpu.with_memory_space_constraint(x, s.memory_space)
        for x, s in zip(operands, more["in_specs"])
    ]
    return pl.pallas_call(
        kernel,
        out_shape=out_shape,
        scratch_shapes=list(scratch),
        compiler_params=pltpu.CompilerParams(vmem_limit_bytes=VMEM_LIMIT),
        cost_estimate=pl.CostEstimate(flops=flops, bytes_accessed=1 << 10, transcendentals=0),
        name=name,
        **more,
    )(*placed)


def lane_groups(rows):
    return lax.broadcasted_iota(jnp.int32, (rows, CHANS), 1) // (CHANS // GROUPS)


def later(x, count):
    row = lax.broadcasted_iota(jnp.int32, x.shape, 0)
    return jnp.where(row >= count, pltpu.roll(x, count, 0), 0.0)


def strip_of(line):
    wide = jnp.broadcast_to(line, (STRIP, WIDE))
    return pltpu.roll(wide, 0, 1, stride=1, stride_axis=0)[:, :LENGTH].astype(BF16)


def pick_groups(result):
    ids = lane_groups(STRIP)
    out = jnp.zeros((STRIP, CHANS), F32)
    for g in range(GROUPS):
        out = jnp.where(ids == g, result[g * STRIP : (g + 1) * STRIP], out)
    return out


def all_strips(strips_ref, signal_ref):
    parts = []
    for n in range(ROWS // STRIP):
        window = signal_ref[n * STRIP : n * STRIP + LENGTH, :]
        parts.append(pick_groups(jnp.dot(strips_ref[...], window, preferred_element_type=F32)))
    return jnp.concatenate(parts, axis=0)


def with_tail(tail, block):
    joined = jnp.concatenate([tail.astype(F32), block.astype(F32)], axis=0)
    return joined[TAIL:], pltpu.roll(joined, 1, 0)[TAIL:], pltpu.roll(joined, 2, 0)[TAIL:]


def short_sum(taps_ref, i, parts):
    return sum(taps_ref[i, j : j + 1, :] * parts[j] for j in range(3))


def lines_of(filter_ref, turned):
    if not turned:
        return jnp.concatenate(
            [filter_ref[...].astype(F32), jnp.zeros((GROUPS, PAD), F32)], axis=1
        )
    row = lax.broadcasted_iota(jnp.int32, (CHANS, CHANS), 0)
    col = lax.broadcasted_iota(jnp.int32, (CHANS, CHANS), 1)
    turn = (row + col == CHANS - 1).astype(F32).astype(BF16)
    pieces = [
        jnp.dot(filter_ref[:, n * CHANS : (n + 1) * CHANS], turn, preferred_element_type=F32)
        for n in reversed(range(LENGTH // CHANS))
    ]
    wide = jnp.concatenate([*pieces, jnp.zeros((GROUPS, PAD), F32)], axis=1)
    return pltpu.roll(wide, WIDE - (STRIP - 1), 1)


def pre_kernel(
    cot_ref, weight_ref, lags_ref, d_gated_ref, strips_ref, cot_buffer, weight_buffer, filter_ref,
    sems, lags_sem,
):
    tile = FEATS // PIECES
    lags_copy = pltpu.make_async_copy(lags_ref, filter_ref, lags_sem)
    lags_copy.start()
    copies = []
    for n in range(PIECES):
        piece = slice(n * tile, (n + 1) * tile)
        pair = (
            pltpu.make_async_copy(cot_ref.at[:, piece], cot_buffer.at[n], sems.at[0, n]),
            pltpu.make_async_copy(weight_ref.at[piece, :], weight_buffer.at[n], sems.at[1, n]),
        )
        for copy in pair:
            copy.start()
        copies.append(pair)
    lags_copy.wait()
    lines = lines_of(filter_ref, True)
    for g in range(GROUPS):
        strips_ref[g * STRIP : (g + 1) * STRIP, :] = strip_of(lines[g : g + 1])
    total = jnp.zeros((ROWS, CHANS), F32)
    for n in range(PIECES):
        for copy in copies[n]:
            copy.wait()
        total += jnp.dot(cot_buffer[n], weight_buffer[n], preferred_element_type=F32)
    d_gated_ref[...] = total.astype(BF16)


def pre_call(*operands):
    tile = FEATS // PIECES
    scratch = [
        pltpu.VMEM((PIECES, ROWS, tile), BF16),
        pltpu.VMEM((PIECES, tile, CHANS), BF16),
        pltpu.VMEM((GROUPS, LENGTH), BF16),
        pltpu.SemaphoreType.DMA((2, PIECES)),
        pltpu.SemaphoreType.DMA,
    ]
    in_specs = [pl.BlockSpec(memory_space=pltpu.HBM)] * 3
    out_shape = [
        pltpu.VMEM((ROWS, CHANS), BF16),
        pltpu.VMEM((GROUPS * STRIP, LENGTH), BF16),
    ]
    return call(pre_kernel, "pre", out_shape, operands, scratch, in_specs=in_specs, flops=1 << 30)


def d_inner_kernel(d_gated_ref, query_ref, tail_ref, taps_ref, out_ref):
    q_short = short_sum(taps_ref, 0, with_tail(tail_ref[...], query_ref[...]))
    out_ref[...] = (d_gated_ref[...].astype(F32) * q_short).astype(BF16)


def d_inner_call(*operands):
    return call(d_inner_kernel, "d_inner", pltpu.VMEM((ROWS, CHANS), BF16), operands)


def fwd_kernel(
    core_ref, strips_ref, pair_ref, cross_ref, cross_pair_ref, key_ref, value_ref, query_ref,
    tail_ref, taps_ref, skip_ref,
    gated_ref, inner_ref, signal_ref,
):
    upper = core_ref[0] == 1
    pair = pair_ref[...].astype(F32)
    cross_pair = cross_pair_ref[...].astype(F32)
    near = jnp.where(upper, pair, cross_pair)
    far = jnp.where(upper, cross_pair, 0.0)
    own = jnp.concatenate([key_ref[...], value_ref[...]], axis=1).astype(F32)
    both = jnp.concatenate([far, cross_ref[...].astype(F32), near, own], axis=0)
    shifted = (both, later(both, 1), later(both, 2))
    k_short = short_sum(taps_ref, 1, [part[:, :CHANS] for part in shifted])
    v_short = short_sum(taps_ref, 2, [part[:, CHANS:] for part in shifted])
    mixed = (k_short * v_short).astype(BF16)
    signal_ref[: ROWS - STRIP, :] = jnp.zeros((ROWS - STRIP, CHANS), BF16)
    signal_ref[ROWS - STRIP :, :] = mixed
    inner = all_strips(strips_ref, signal_ref) + skip_ref[...] * mixed[LENGTH - ROWS :].astype(F32)
    inner_ref[...] = inner
    q_short = short_sum(taps_ref, 0, with_tail(tail_ref[...], query_ref[...]))
    gated_ref[...] = (q_short * inner).astype(BF16)


def fwd_call(*operands):
    out_shape = [
        pltpu.VMEM((ROWS, CHANS), BF16),
        pltpu.VMEM((ROWS, CHANS), F32),
        pltpu.VMEM((LENGTH + ROWS - STRIP, CHANS), BF16),
    ]
    return call(fwd_kernel, "fwd", out_shape, operands, (), 1, 4 << 30)


def terms_kernel(core_ref, own_cot_ref, other_cot_ref, gated_ref, other_gated_ref, out_ref):
    dims = (((0,), (0,)), ((), ()))
    for half in range(2):
        start = pl.multiple_of((2 * half + core_ref[0]) * SHARE, SHARE)
        own_cot = own_cot_ref[:, pl.ds(start, SHARE)]
        other_cot = other_cot_ref[:, pl.ds(start, SHARE)]
        total = lax.dot_general(gated_ref[...], own_cot, dims, preferred_element_type=F32)
        total += lax.dot_general(other_gated_ref[...], other_cot, dims, preferred_element_type=F32)
        out_ref[half, :, :SHARE] = total.astype(BF16)


def terms_call(*operands):
    out_shape = pltpu.VMEM((2, CHANS, SHARE + CHANS), BF16)
    return call(terms_kernel, "terms", out_shape, operands, scalars=1, flops=1 << 30)


def two_parts(total):
    rounded = total.astype(BF16).astype(F32)
    left = pltpu.roll(total - rounded, SEGMENT // 2, total.ndim - 2)
    return (rounded + left).astype(BF16)


def add_small_kernel(terms_ref, small_ref, other_small_ref, out_ref, parts_ref, sems):
    parts = two_parts(small_ref[...] + other_small_ref[...]).astype(F32)
    parts_ref[...] = parts.reshape(CHANS, CHANS).astype(BF16)
    copies = [
        pltpu.make_async_copy(parts_ref, out_ref.at[half, :, pl.ds(SHARE, CHANS)], sems.at[half])
        for half in range(2)
    ]
    for copy in copies:
        copy.start()
    for copy in copies:
        copy.wait()


def add_small_call(*operands):
    place = pl.BlockSpec(memory_space=pl.ANY)
    spec = pl.BlockSpec(memory_space=pltpu.VMEM)
    return pl.pallas_call(
        add_small_kernel,
        in_specs=[place, spec, spec],
        out_specs=place,
        out_shape=jax.ShapeDtypeStruct(operands[0].shape, BF16),
        scratch_shapes=[pltpu.VMEM((CHANS, CHANS), BF16), pltpu.SemaphoreType.DMA((2,))],
        input_output_aliases={0: 0},
        compiler_params=pltpu.CompilerParams(vmem_limit_bytes=VMEM_LIMIT),
        name="add_small",
    )(
        operands[0],
        *(pltpu.with_memory_space_constraint(x, pltpu.VMEM) for x in operands[1:]),
    )


def place(g, n):
    row = g * (LENGTH // CHANS) + n
    return row % SHARES, row // SHARES


def turn_matrix(size, block):
    row = lax.broadcasted_iota(jnp.int32, (size, size), 0)
    col = lax.broadcasted_iota(jnp.int32, (size, size), 1)
    return ((row // block) * block + (block - 1 - row % block) == col).astype(F32)


def lag_kernel(d_inner_ref, signal_ref, filter_ref, outer_ref, stack_ref, sums_ref):
    turn = turn_matrix(ROWS, STRIP).astype(BF16)
    turned = jnp.dot(turn, d_inner_ref[...], preferred_element_type=F32)
    ids = lane_groups(STRIP)
    outer_ref[:, LENGTH:] = jnp.zeros((GROUPS * STRIP, PAD), F32)
    for n in range(ROWS // STRIP):
        piece = turned[n * STRIP : (n + 1) * STRIP]
        for g in range(GROUPS):
            stack_ref[g * STRIP : (g + 1) * STRIP, :] = jnp.where(ids == g, piece, 0.0).astype(BF16)
        term = lax.dot_general(
            stack_ref[...],
            signal_ref[n * STRIP : n * STRIP + LENGTH, :],
            (((1,), (1,)), ((), ())),
            preferred_element_type=F32,
        )
        if n == 0:
            outer_ref[:, :LENGTH] = term
        else:
            outer_ref[:, :LENGTH] += term
    for g in range(GROUPS):
        rows = outer_ref[g * STRIP : (g + 1) * STRIP, :]
        skewed = pltpu.roll(rows, WIDE - (STRIP - 1), 1, stride=1, stride_axis=0)
        sums_ref[g : g + 1, :] = jnp.sum(skewed, axis=0, keepdims=True)
    sums = pltpu.roll(sums_ref[...], STRIP - 1, 1)
    turn = turn_matrix(CHANS, CHANS)
    last = LENGTH // CHANS - 1
    for n in range(LENGTH // CHANS):
        filter_ref[:, n * CHANS : (n + 1) * CHANS] = jnp.dot(
            sums[:, (last - n) * CHANS : (last - n + 1) * CHANS],
            turn,
            precision=lax.Precision.HIGHEST,
            preferred_element_type=F32,
        )


def lag_call(*operands):
    scratch = [
        pltpu.VMEM((GROUPS * STRIP, WIDE), F32),
        pltpu.VMEM((GROUPS * STRIP, CHANS), BF16),
        pltpu.VMEM((GROUPS, WIDE), F32),
    ]
    return call(lag_kernel, "lag_sums", pltpu.VMEM((GROUPS, LENGTH), F32), operands, scratch)


def bwd_kernel(
    core_ref, d0_ref, d1_ref, d2_ref, d3_ref, lags_ref, filter_ref, signal_ref, key_ref, value_ref,
    pair_ref, cross_pair_ref, query_ref, tail_ref, inner_ref, d_gated_ref, taps_ref, skip_ref,
    d_short_ref, head_ref, small_ref,
    strips_ref, ahead_ref,
):
    for n, ref in enumerate((d0_ref, d1_ref, d2_ref, d3_ref)):
        ahead_ref[n * ROWS : (n + 1) * ROWS, :] = ref[...]
    ahead_ref[LENGTH:, :] = jnp.zeros((ROWS, CHANS), BF16)
    lines = lines_of(lags_ref, False)
    for g in range(GROUPS):
        strips_ref[g * STRIP : (g + 1) * STRIP, :] = strip_of(lines[g : g + 1])
    d_inner = d0_ref[...].astype(F32)
    mixed = signal_ref[LENGTH - STRIP :, :]
    d_mixed = all_strips(strips_ref, ahead_ref) + skip_ref[...] * d_inner

    upper = core_ref[0] == 1
    last = slice(ROWS - TAIL, ROWS)
    near = jnp.where(upper, pair_ref[last, :].astype(F32), cross_pair_ref[last, :].astype(F32))
    k_parts = with_tail(near[:, :CHANS], key_ref[...])
    v_parts = with_tail(near[:, CHANS:], value_ref[...])
    q_parts = with_tail(tail_ref[...], query_ref[...])
    small_ref[...] = jnp.zeros_like(small_ref)
    d_qs = d_gated_ref[...].astype(F32) * inner_ref[...]
    d_ks = d_mixed * short_sum(taps_ref, 2, v_parts)
    d_vs = d_mixed * short_sum(taps_ref, 1, k_parts)
    for i, (grad, parts) in enumerate(((d_qs, q_parts), (d_ks, k_parts), (d_vs, v_parts))):
        d_short_ref[i] = grad
        head_ref[i] = grad[:8]
        for j in range(3):
            small_ref[3 * i + j, 2:3, :] = jnp.sum(grad * parts[j], axis=0, keepdims=True)
    small_ref[9, 2:3, :] = jnp.sum(d_inner * mixed.astype(F32), axis=0, keepdims=True)

    for g in range(GROUPS):
        for n in range(LENGTH // CHANS):
            share, slot = place(g, n)
            small_ref[share, slot : slot + 1, :] = filter_ref[g : g + 1, n * CHANS : (n + 1) * CHANS]


def bwd_call(*operands):
    out_shape = [
        pltpu.VMEM((3, ROWS, CHANS), F32),
        pltpu.VMEM((3, 8, CHANS), F32),
        pltpu.VMEM((SHARES, SEGMENT, CHANS), F32),
    ]
    scratch = [
        pltpu.VMEM((GROUPS * STRIP, LENGTH), BF16),
        pltpu.VMEM((LENGTH + ROWS, CHANS), BF16),
    ]
    return call(bwd_kernel, "bwd", out_shape, operands, scratch, 1)


def input_grad_kernel(d_short_ref, next_ref, taps_ref, query_ref, key_ref, value_ref):
    for i, out_ref in enumerate((query_ref, key_ref, value_ref)):
        joined = jnp.concatenate([d_short_ref[i], next_ref[i]], axis=0)
        rows = joined.shape[0]
        parts = (
            joined[:ROWS],
            pltpu.roll(joined, rows - 1, 0)[:ROWS],
            pltpu.roll(joined, rows - 2, 0)[:ROWS],
        )
        out_ref[...] = short_sum(taps_ref, i, parts).astype(BF16)


def input_grad_call(*operands):
    out_shape = [jax.ShapeDtypeStruct((ROWS, CHANS), BF16)] * 3
    return call(input_grad_kernel, "input_grads", out_shape, operands)


def total_kernel(scale, terms_ref, out_ref):
    total = jnp.sum(terms_ref[...].astype(F32), axis=0) * scale
    small = total[:, SHARE:]
    row = lax.broadcasted_iota(jnp.int32, small.shape, 0)
    small = jnp.where(row < SEGMENT // 2, small + pltpu.roll(small, SEGMENT // 2, 0), 0.0)
    total = jnp.concatenate([total[:, :SHARE].astype(BF16), two_parts(small)], axis=1)
    out_ref[...] = jnp.broadcast_to(total[None], out_ref.shape)


def total_call(terms, scale):
    out_shape = pltpu.VMEM((SHARES, *terms.shape[1:]), BF16)
    return call(lambda *refs: total_kernel(scale, *refs), "total", out_shape, (terms,))


def spread_kernel(
    shares_ref, weight_ref, taps_ref, filter_ref, skip_ref, turned_ref, sems
):
    tile = SHARE // SPREAD
    copies = []
    for n in range(SPREAD):
        piece = slice(n * tile, (n + 1) * tile)
        turned_ref[piece, :] = shares_ref[:, piece].astype(F32).T
        copies.append(
            pltpu.make_async_copy(turned_ref.at[piece, :], weight_ref.at[piece, :], sems.at[n])
        )
        copies[-1].start()
    for share in range(SHARES):
        segment = shares_ref[share * SEGMENT : (share + 1) * SEGMENT, SHARE:].astype(F32)
        segment = segment + pltpu.roll(segment, SEGMENT // 2, 0)
        for g in range(GROUPS):
            for n in range(LENGTH // CHANS):
                if place(g, n)[0] == share:
                    slot = place(g, n)[1]
                    filter_ref[g : g + 1, n * CHANS : (n + 1) * CHANS] = segment[slot : slot + 1]
        if share < 9:
            taps_ref[share // 3, share % 3 : share % 3 + 1, :] = segment[2:3]
        if share == 9:
            skip_ref[...] = segment[2:3]
    for copy in copies:
        copy.wait()


def spread_call(shares):
    out_shape = [
        jax.ShapeDtypeStruct((SHARE, CHANS), F32),
        jax.ShapeDtypeStruct((3, 3, CHANS), F32),
        jax.ShapeDtypeStruct((GROUPS, LENGTH), F32),
        jax.ShapeDtypeStruct((1, CHANS), F32),
    ]
    scratch = [pltpu.VMEM((SHARE, CHANS), F32), pltpu.SemaphoreType.DMA((SPREAD,))]
    out_specs = [pl.BlockSpec(memory_space=pl.ANY)]
    out_specs += [pl.BlockSpec(memory_space=pltpu.VMEM)] * 3
    shares = shares.reshape(CHANS, SHARE + CHANS)
    return call(spread_kernel, "spread", out_shape, (shares,), scratch, out_specs=out_specs)


def sent(block, distance):
    count = 4
    route = [(i, i + distance) for i in range(count) if 0 <= i + distance < count]
    return lax.ppermute(block, CTX, route)


def shards(
    query_in, key_in, value_in, short_taps, long_filter, skip_gain, out_weight, out_cotangent
):
    query = query_in[0]
    cot = out_cotangent[0]
    taps = short_taps
    skip = skip_gain.reshape(1, CHANS)
    devices = lax.axis_size(ALL)
    tokens = ROWS * devices
    scale = 1.0 / math.sqrt(tokens)
    core = lax.axis_index("co").astype(jnp.int32).reshape(1)

    key = key_in[0]
    value = value_in[0]
    swap = [(0, 1), (1, 0)]
    own = jnp.concatenate([key, value], axis=1)
    tail = sent(query[ROWS - TAIL :], 1)
    cross = lax.ppermute(own, "xh", [(0, 1)])
    pair = lax.ppermute(own, "co", swap)
    other_cot = lax.ppermute(cot, "co", swap)

    d_gated, strips = pre_call(cot, out_weight, long_filter)
    cross, tail, d_gated = lax.optimization_barrier((cross, tail, d_gated))
    cross_pair = lax.ppermute(cross, "co", swap)
    d_inner = d_inner_call(d_gated, query, tail, taps)
    blocks = [d_inner] + [sent(d_inner, -distance) for distance in (1, 2, 3)]
    gated, inner, signal = fwd_call(
        core, strips, pair, cross, cross_pair, key, value, query, tail, taps, skip
    )
    other_gated = lax.ppermute(gated, "co", swap)
    lag_sums = lag_call(d_inner, signal)
    d_short, head, small = bwd_call(
        core, *blocks, long_filter, lag_sums, signal, key, value, pair, cross_pair, query, tail,
        inner, d_gated, taps, skip,
    )
    other_gated, head, small = lax.optimization_barrier((other_gated, head, small))
    other_small = lax.ppermute(small, "co", swap)
    terms = terms_call(core, cot, other_cot, gated, other_gated)
    terms, other_small = lax.optimization_barrier((terms, other_small))
    terms = add_small_call(terms, small, other_small)
    terms, head = lax.optimization_barrier((terms, head))
    terms = terms.reshape(2 * SHARES, CHANS // SHARES, SHARE + CHANS)
    terms = lax.all_to_all(terms, CHIPS, 0, 0)
    following = sent(head, -1)
    grad_query, grad_key, grad_value = input_grad_call(d_short, following, taps)

    shares = lax.all_to_all(total_call(terms, scale), DP, 0, 0)
    grad_weight, grad_taps, grad_filter, grad_skip = spread_call(shares)
    return (
        gated[None],
        grad_query[None],
        grad_key[None],
        grad_value[None],
        grad_taps,
        grad_filter,
        grad_skip.reshape(CHANS),
        grad_weight,
    )


def solution(mesh):
    fine = Mesh(mesh.devices.reshape(2, 2, 4, 2, 4), ALL)
    tokens = P(DP, CTX, None)
    in_specs = (tokens, tokens, tokens, P(), P(), P(), P(), tokens)
    out_specs = (tokens, tokens, tokens, tokens, P(), P(), P(), P(CTX, None))
    return jax.shard_map(
        shards, mesh=fine, in_specs=in_specs, out_specs=out_specs, check_vma=False
    )
```

```python
import math

import jax
import jax.numpy as jnp
from jax import lax
from jax.experimental import pallas as pl
from jax.experimental.pallas import tpu as pltpu
from jax.sharding import Mesh
from jax.sharding import PartitionSpec as P

F32 = jnp.float32
BF16 = jnp.bfloat16
CTX = ("xh", "co")
DP = ("y", "xl", "z")
CHIPS = ("xh", "y", "xl", "z")
ALL = ("xh", "co", "y", "xl", "z")

ROWS = 256
CHANS = 256
HALF = CHANS // 2
GROUPS = 16
LENGTH = 1024
STRIP = 32
PAD = 128
WIDE = LENGTH + PAD
FEATS = 8192
TAIL = 16
SHARES = 32
SHARE = FEATS // 4
SEGMENT = 8
SPREAD = 4
PIECES = 8
VMEM_LIMIT = 20 * 1024 * 1024


def call(kernel, name, out_shape, operands, scratch=(), scalars=0, flops=1 << 10, **more):
    spec = pl.BlockSpec(memory_space=pltpu.VMEM)
    in_specs = [pl.BlockSpec(memory_space=pltpu.SMEM)] * scalars
    in_specs += [spec] * (len(operands) - scalars)
    defaults = {"in_specs": in_specs, "out_specs": jax.tree.map(lambda _: spec, out_shape)}
    more = {**defaults, **more}
    placed = [
        x if s.memory_space == pltpu.SMEM else pltpu.with_memory_space_constraint(x, s.memory_space)
        for x, s in zip(operands, more["in_specs"])
    ]
    return pl.pallas_call(
        kernel,
        out_shape=out_shape,
        scratch_shapes=list(scratch),
        compiler_params=pltpu.CompilerParams(vmem_limit_bytes=VMEM_LIMIT),
        cost_estimate=pl.CostEstimate(flops=flops, bytes_accessed=1 << 10, transcendentals=0),
        name=name,
        **more,
    )(*placed)


def lane_groups():
    return lax.broadcasted_iota(jnp.int32, (STRIP, HALF), 1) // (CHANS // GROUPS)


def later(x, count):
    row = lax.broadcasted_iota(jnp.int32, x.shape, 0)
    return jnp.where(row >= count, pltpu.roll(x, count, 0), 0.0)


def strip_of(line):
    wide = jnp.broadcast_to(line, (STRIP, WIDE))
    return pltpu.roll(wide, 0, 1, stride=1, stride_axis=0)[:, :LENGTH].astype(BF16)


def two_windows(signal_ref, n, half):
    lanes = slice(half * HALF, (half + 1) * HALF)
    windows = [signal_ref[m * STRIP : m * STRIP + LENGTH, lanes] for m in (n, n + 1)]
    return jnp.concatenate(windows, axis=1)


def all_strips(strips_ref, signal_ref):
    ids = lane_groups()
    rows = GROUPS * STRIP // 2
    columns = []
    for half in range(2):
        parts = []
        for n in range(0, ROWS // STRIP, 2):
            result = jnp.dot(
                strips_ref[half * rows : (half + 1) * rows, :],
                two_windows(signal_ref, n, half),
                preferred_element_type=F32,
            )
            for m in range(2):
                out = jnp.zeros((STRIP, HALF), F32)
                for g in range(GROUPS // 2):
                    piece = result[g * STRIP : (g + 1) * STRIP, m * HALF : (m + 1) * HALF]
                    out = jnp.where(ids == g, piece, out)
                parts.append(out)
        columns.append(jnp.concatenate(parts, axis=0))
    return jnp.concatenate(columns, axis=1)


def with_tail(tail, block):
    joined = jnp.concatenate([tail.astype(F32), block.astype(F32)], axis=0)
    return joined[TAIL:], pltpu.roll(joined, 1, 0)[TAIL:], pltpu.roll(joined, 2, 0)[TAIL:]


def short_sum(taps_ref, i, parts):
    return sum(taps_ref[i, j : j + 1, :] * parts[j] for j in range(3))


def lines_of(filter_ref, turned):
    if not turned:
        return jnp.concatenate(
            [filter_ref[...].astype(F32), jnp.zeros((GROUPS, PAD), F32)], axis=1
        )
    row = lax.broadcasted_iota(jnp.int32, (CHANS, CHANS), 0)
    col = lax.broadcasted_iota(jnp.int32, (CHANS, CHANS), 1)
    turn = (row + col == CHANS - 1).astype(F32).astype(BF16)
    pieces = [
        jnp.dot(filter_ref[:, n * CHANS : (n + 1) * CHANS], turn, preferred_element_type=F32)
        for n in reversed(range(LENGTH // CHANS))
    ]
    wide = jnp.concatenate([*pieces, jnp.zeros((GROUPS, PAD), F32)], axis=1)
    return pltpu.roll(wide, WIDE - (STRIP - 1), 1)


def pre_kernel(
    cot_ref, weight_ref, lags_ref, d_gated_ref, strips_ref, cot_buffer, weight_buffer, filter_ref,
    sems, lags_sem,
):
    tile = FEATS // PIECES
    lags_copy = pltpu.make_async_copy(lags_ref, filter_ref, lags_sem)
    lags_copy.start()
    copies = []
    for n in range(PIECES):
        piece = slice(n * tile, (n + 1) * tile)
        pair = (
            pltpu.make_async_copy(cot_ref.at[:, piece], cot_buffer.at[n], sems.at[0, n]),
            pltpu.make_async_copy(weight_ref.at[piece, :], weight_buffer.at[n], sems.at[1, n]),
        )
        for copy in pair:
            copy.start()
        copies.append(pair)
    lags_copy.wait()
    lines = lines_of(filter_ref, True)
    for g in range(GROUPS):
        strips_ref[g * STRIP : (g + 1) * STRIP, :] = strip_of(lines[g : g + 1])
    total = jnp.zeros((ROWS, CHANS), F32)
    for n in range(PIECES):
        for copy in copies[n]:
            copy.wait()
        total += jnp.dot(cot_buffer[n], weight_buffer[n], preferred_element_type=F32)
    d_gated_ref[...] = total.astype(BF16)


def pre_call(*operands):
    tile = FEATS // PIECES
    scratch = [
        pltpu.VMEM((PIECES, ROWS, tile), BF16),
        pltpu.VMEM((PIECES, tile, CHANS), BF16),
        pltpu.VMEM((GROUPS, LENGTH), BF16),
        pltpu.SemaphoreType.DMA((2, PIECES)),
        pltpu.SemaphoreType.DMA,
    ]
    in_specs = [pl.BlockSpec(memory_space=pltpu.HBM)] * 3
    out_shape = [
        pltpu.VMEM((ROWS, CHANS), BF16),
        pltpu.VMEM((GROUPS * STRIP, LENGTH), BF16),
    ]
    return call(pre_kernel, "pre", out_shape, operands, scratch, in_specs=in_specs, flops=1 << 30)


def d_inner_kernel(d_gated_ref, query_ref, tail_ref, taps_ref, out_ref):
    q_short = short_sum(taps_ref, 0, with_tail(tail_ref[...], query_ref[...]))
    out_ref[...] = (d_gated_ref[...].astype(F32) * q_short).astype(BF16)


def d_inner_call(*operands):
    return call(d_inner_kernel, "d_inner", pltpu.VMEM((ROWS, CHANS), BF16), operands)


def fwd_kernel(
    core_ref, strips_ref, pair_ref, cross_ref, cross_pair_ref, key_ref, value_ref, query_ref,
    tail_ref, taps_ref, skip_ref,
    gated_ref, inner_ref, signal_ref,
):
    upper = core_ref[0] == 1
    pair = pair_ref[...].astype(F32)
    cross_pair = cross_pair_ref[...].astype(F32)
    near = jnp.where(upper, pair, cross_pair)
    far = jnp.where(upper, cross_pair, 0.0)
    own = jnp.concatenate([key_ref[...], value_ref[...]], axis=1).astype(F32)
    both = jnp.concatenate([far, cross_ref[...].astype(F32), near, own], axis=0)
    shifted = (both, later(both, 1), later(both, 2))
    k_short = short_sum(taps_ref, 1, [part[:, :CHANS] for part in shifted])
    v_short = short_sum(taps_ref, 2, [part[:, CHANS:] for part in shifted])
    mixed = (k_short * v_short).astype(BF16)
    signal_ref[: ROWS - STRIP, :] = jnp.zeros((ROWS - STRIP, CHANS), BF16)
    signal_ref[ROWS - STRIP :, :] = mixed
    inner = all_strips(strips_ref, signal_ref) + skip_ref[...] * mixed[LENGTH - ROWS :].astype(F32)
    inner_ref[...] = inner
    q_short = short_sum(taps_ref, 0, with_tail(tail_ref[...], query_ref[...]))
    gated_ref[...] = (q_short * inner).astype(BF16)


def fwd_call(*operands):
    out_shape = [
        pltpu.VMEM((ROWS, CHANS), BF16),
        pltpu.VMEM((ROWS, CHANS), F32),
        pltpu.VMEM((LENGTH + ROWS - STRIP, CHANS), BF16),
    ]
    return call(fwd_kernel, "fwd", out_shape, operands, (), 1, 4 << 30)


def terms_kernel(core_ref, own_cot_ref, other_cot_ref, gated_ref, other_gated_ref, out_ref):
    dims = (((0,), (0,)), ((), ()))
    for half in range(2):
        start = pl.multiple_of((2 * half + core_ref[0]) * SHARE, SHARE)
        own_cot = own_cot_ref[:, pl.ds(start, SHARE)]
        other_cot = other_cot_ref[:, pl.ds(start, SHARE)]
        total = lax.dot_general(gated_ref[...], own_cot, dims, preferred_element_type=F32)
        total += lax.dot_general(other_gated_ref[...], other_cot, dims, preferred_element_type=F32)
        out_ref[half, :, :SHARE] = total.astype(BF16)


def terms_call(*operands):
    out_shape = pltpu.VMEM((2, CHANS, SHARE + CHANS), BF16)
    return call(terms_kernel, "terms", out_shape, operands, scalars=1, flops=1 << 30)


def two_parts(total):
    rounded = total.astype(BF16).astype(F32)
    left = pltpu.roll(total - rounded, SEGMENT // 2, total.ndim - 2)
    return (rounded + left).astype(BF16)


def add_small_kernel(terms_ref, small_ref, other_small_ref, out_ref, parts_ref, sems):
    parts = two_parts(small_ref[...] + other_small_ref[...]).astype(F32)
    parts_ref[...] = parts.reshape(CHANS, CHANS).astype(BF16)
    copies = [
        pltpu.make_async_copy(parts_ref, out_ref.at[half, :, pl.ds(SHARE, CHANS)], sems.at[half])
        for half in range(2)
    ]
    for copy in copies:
        copy.start()
    for copy in copies:
        copy.wait()


def add_small_call(*operands):
    place = pl.BlockSpec(memory_space=pl.ANY)
    spec = pl.BlockSpec(memory_space=pltpu.VMEM)
    return pl.pallas_call(
        add_small_kernel,
        in_specs=[place, spec, spec],
        out_specs=place,
        out_shape=jax.ShapeDtypeStruct(operands[0].shape, BF16),
        scratch_shapes=[pltpu.VMEM((CHANS, CHANS), BF16), pltpu.SemaphoreType.DMA((2,))],
        input_output_aliases={0: 0},
        compiler_params=pltpu.CompilerParams(vmem_limit_bytes=VMEM_LIMIT),
        name="add_small",
    )(
        operands[0],
        *(pltpu.with_memory_space_constraint(x, pltpu.VMEM) for x in operands[1:]),
    )


def place(g, n):
    row = g * (LENGTH // CHANS) + n
    return row % SHARES, row // SHARES


def turn_matrix(size, block):
    row = lax.broadcasted_iota(jnp.int32, (size, size), 0)
    col = lax.broadcasted_iota(jnp.int32, (size, size), 1)
    return ((row // block) * block + (block - 1 - row % block) == col).astype(F32)


def lag_kernel(d_inner_ref, signal_ref, filter_ref, outer_ref, stack_ref, sums_ref):
    turn = turn_matrix(ROWS, STRIP).astype(BF16)
    turned = jnp.dot(turn, d_inner_ref[...], preferred_element_type=F32)
    ids = lane_groups()
    count = GROUPS * STRIP // 2
    outer_ref[:, LENGTH:] = jnp.zeros((GROUPS * STRIP, PAD), F32)
    for half in range(2):
        rows = slice(half * count, (half + 1) * count)
        for n in range(0, ROWS // STRIP, 2):
            for m in range(2):
                start = (n + m) * STRIP
                piece = turned[start : start + STRIP, half * HALF : (half + 1) * HALF]
                for g in range(GROUPS // 2):
                    stack_ref[g * STRIP : (g + 1) * STRIP, m * HALF : (m + 1) * HALF] = jnp.where(
                        ids == g, piece, 0.0
                    ).astype(BF16)
            term = lax.dot_general(
                stack_ref[...],
                two_windows(signal_ref, n, half),
                (((1,), (1,)), ((), ())),
                preferred_element_type=F32,
            )
            if n == 0:
                outer_ref[rows, :LENGTH] = term
            else:
                outer_ref[rows, :LENGTH] += term
    for g in range(GROUPS):
        rows = outer_ref[g * STRIP : (g + 1) * STRIP, :]
        skewed = pltpu.roll(rows, WIDE - (STRIP - 1), 1, stride=1, stride_axis=0)
        sums_ref[g : g + 1, :] = jnp.sum(skewed, axis=0, keepdims=True)
    sums = pltpu.roll(sums_ref[...], STRIP - 1, 1)
    turn = turn_matrix(CHANS, CHANS)
    last = LENGTH // CHANS - 1
    for n in range(LENGTH // CHANS):
        filter_ref[:, n * CHANS : (n + 1) * CHANS] = jnp.dot(
            sums[:, (last - n) * CHANS : (last - n + 1) * CHANS],
            turn,
            precision=lax.Precision.HIGHEST,
            preferred_element_type=F32,
        )


def lag_call(*operands):
    scratch = [
        pltpu.VMEM((GROUPS * STRIP, WIDE), F32),
        pltpu.VMEM((GROUPS * STRIP // 2, CHANS), BF16),
        pltpu.VMEM((GROUPS, WIDE), F32),
    ]
    return call(lag_kernel, "lag_sums", pltpu.VMEM((GROUPS, LENGTH), F32), operands, scratch)


def bwd_kernel(
    core_ref, d0_ref, d1_ref, d2_ref, d3_ref, lags_ref, filter_ref, signal_ref, key_ref, value_ref,
    pair_ref, cross_pair_ref, query_ref, tail_ref, inner_ref, d_gated_ref, taps_ref, skip_ref,
    d_short_ref, head_ref, small_ref,
    strips_ref, ahead_ref,
):
    for n, ref in enumerate((d0_ref, d1_ref, d2_ref, d3_ref)):
        ahead_ref[n * ROWS : (n + 1) * ROWS, :] = ref[...]
    ahead_ref[LENGTH:, :] = jnp.zeros((ROWS, CHANS), BF16)
    lines = lines_of(lags_ref, False)
    for g in range(GROUPS):
        strips_ref[g * STRIP : (g + 1) * STRIP, :] = strip_of(lines[g : g + 1])
    d_inner = d0_ref[...].astype(F32)
    mixed = signal_ref[LENGTH - STRIP :, :]
    d_mixed = all_strips(strips_ref, ahead_ref) + skip_ref[...] * d_inner

    upper = core_ref[0] == 1
    last = slice(ROWS - TAIL, ROWS)
    near = jnp.where(upper, pair_ref[last, :].astype(F32), cross_pair_ref[last, :].astype(F32))
    k_parts = with_tail(near[:, :CHANS], key_ref[...])
    v_parts = with_tail(near[:, CHANS:], value_ref[...])
    q_parts = with_tail(tail_ref[...], query_ref[...])
    small_ref[...] = jnp.zeros_like(small_ref)
    d_qs = d_gated_ref[...].astype(F32) * inner_ref[...]
    d_ks = d_mixed * short_sum(taps_ref, 2, v_parts)
    d_vs = d_mixed * short_sum(taps_ref, 1, k_parts)
    for i, (grad, parts) in enumerate(((d_qs, q_parts), (d_ks, k_parts), (d_vs, v_parts))):
        d_short_ref[i] = grad
        head_ref[i] = grad[:8]
        for j in range(3):
            small_ref[3 * i + j, 2:3, :] = jnp.sum(grad * parts[j], axis=0, keepdims=True)
    small_ref[9, 2:3, :] = jnp.sum(d_inner * mixed.astype(F32), axis=0, keepdims=True)

    for g in range(GROUPS):
        for n in range(LENGTH // CHANS):
            share, slot = place(g, n)
            small_ref[share, slot : slot + 1, :] = filter_ref[g : g + 1, n * CHANS : (n + 1) * CHANS]


def bwd_call(*operands):
    out_shape = [
        pltpu.VMEM((3, ROWS, CHANS), F32),
        pltpu.VMEM((3, 8, CHANS), F32),
        pltpu.VMEM((SHARES, SEGMENT, CHANS), F32),
    ]
    scratch = [
        pltpu.VMEM((GROUPS * STRIP, LENGTH), BF16),
        pltpu.VMEM((LENGTH + ROWS, CHANS), BF16),
    ]
    return call(bwd_kernel, "bwd", out_shape, operands, scratch, 1)


def input_grad_kernel(d_short_ref, next_ref, taps_ref, query_ref, key_ref, value_ref):
    for i, out_ref in enumerate((query_ref, key_ref, value_ref)):
        joined = jnp.concatenate([d_short_ref[i], next_ref[i]], axis=0)
        rows = joined.shape[0]
        parts = (
            joined[:ROWS],
            pltpu.roll(joined, rows - 1, 0)[:ROWS],
            pltpu.roll(joined, rows - 2, 0)[:ROWS],
        )
        out_ref[...] = short_sum(taps_ref, i, parts).astype(BF16)


def input_grad_call(*operands):
    out_shape = [jax.ShapeDtypeStruct((ROWS, CHANS), BF16)] * 3
    return call(input_grad_kernel, "input_grads", out_shape, operands)


def total_kernel(scale, terms_ref, out_ref):
    total = jnp.sum(terms_ref[...].astype(F32), axis=0) * scale
    small = total[:, SHARE:]
    row = lax.broadcasted_iota(jnp.int32, small.shape, 0)
    small = jnp.where(row < SEGMENT // 2, small + pltpu.roll(small, SEGMENT // 2, 0), 0.0)
    total = jnp.concatenate([total[:, :SHARE].astype(BF16), two_parts(small)], axis=1)
    out_ref[...] = jnp.broadcast_to(total[None], out_ref.shape)


def total_call(terms, scale):
    out_shape = pltpu.VMEM((SHARES, *terms.shape[1:]), BF16)
    return call(lambda *refs: total_kernel(scale, *refs), "total", out_shape, (terms,))


def spread_kernel(
    shares_ref, weight_ref, taps_ref, filter_ref, skip_ref, turned_ref, sems
):
    tile = SHARE // SPREAD
    copies = []
    for n in range(SPREAD):
        piece = slice(n * tile, (n + 1) * tile)
        turned_ref[piece, :] = shares_ref[:, piece].astype(F32).T
        copies.append(
            pltpu.make_async_copy(turned_ref.at[piece, :], weight_ref.at[piece, :], sems.at[n])
        )
        copies[-1].start()
    for share in range(SHARES):
        segment = shares_ref[share * SEGMENT : (share + 1) * SEGMENT, SHARE:].astype(F32)
        segment = segment + pltpu.roll(segment, SEGMENT // 2, 0)
        for g in range(GROUPS):
            for n in range(LENGTH // CHANS):
                if place(g, n)[0] == share:
                    slot = place(g, n)[1]
                    filter_ref[g : g + 1, n * CHANS : (n + 1) * CHANS] = segment[slot : slot + 1]
        if share < 9:
            taps_ref[share // 3, share % 3 : share % 3 + 1, :] = segment[2:3]
        if share == 9:
            skip_ref[...] = segment[2:3]
    for copy in copies:
        copy.wait()


def spread_call(shares):
    out_shape = [
        jax.ShapeDtypeStruct((SHARE, CHANS), F32),
        jax.ShapeDtypeStruct((3, 3, CHANS), F32),
        jax.ShapeDtypeStruct((GROUPS, LENGTH), F32),
        jax.ShapeDtypeStruct((1, CHANS), F32),
    ]
    scratch = [pltpu.VMEM((SHARE, CHANS), F32), pltpu.SemaphoreType.DMA((SPREAD,))]
    out_specs = [pl.BlockSpec(memory_space=pl.ANY)]
    out_specs += [pl.BlockSpec(memory_space=pltpu.VMEM)] * 3
    shares = shares.reshape(CHANS, SHARE + CHANS)
    return call(spread_kernel, "spread", out_shape, (shares,), scratch, out_specs=out_specs)


def sent(block, distance):
    count = 4
    route = [(i, i + distance) for i in range(count) if 0 <= i + distance < count]
    return lax.ppermute(block, CTX, route)


def shards(
    query_in, key_in, value_in, short_taps, long_filter, skip_gain, out_weight, out_cotangent
):
    query = query_in[0]
    cot = out_cotangent[0]
    taps = short_taps
    skip = skip_gain.reshape(1, CHANS)
    devices = lax.axis_size(ALL)
    tokens = ROWS * devices
    scale = 1.0 / math.sqrt(tokens)
    core = lax.axis_index("co").astype(jnp.int32).reshape(1)

    key = key_in[0]
    value = value_in[0]
    swap = [(0, 1), (1, 0)]
    own = jnp.concatenate([key, value], axis=1)
    tail = sent(query[ROWS - TAIL :], 1)
    cross = lax.ppermute(own, "xh", [(0, 1)])
    pair = lax.ppermute(own, "co", swap)
    other_cot = lax.ppermute(cot, "co", swap)

    d_gated, strips = pre_call(cot, out_weight, long_filter)
    cross, tail, d_gated = lax.optimization_barrier((cross, tail, d_gated))
    cross_pair = lax.ppermute(cross, "co", swap)
    d_inner = d_inner_call(d_gated, query, tail, taps)
    blocks = [d_inner] + [sent(d_inner, -distance) for distance in (1, 2, 3)]
    gated, inner, signal = fwd_call(
        core, strips, pair, cross, cross_pair, key, value, query, tail, taps, skip
    )
    other_gated = lax.ppermute(gated, "co", swap)
    lag_sums = lag_call(d_inner, signal)
    d_short, head, small = bwd_call(
        core, *blocks, long_filter, lag_sums, signal, key, value, pair, cross_pair, query, tail,
        inner, d_gated, taps, skip,
    )
    other_gated, head, small = lax.optimization_barrier((other_gated, head, small))
    other_small = lax.ppermute(small, "co", swap)
    terms = terms_call(core, cot, other_cot, gated, other_gated)
    terms, other_small = lax.optimization_barrier((terms, other_small))
    terms = add_small_call(terms, small, other_small)
    terms, head = lax.optimization_barrier((terms, head))
    terms = terms.reshape(2 * SHARES, CHANS // SHARES, SHARE + CHANS)
    terms = lax.all_to_all(terms, CHIPS, 0, 0)
    following = sent(head, -1)
    grad_query, grad_key, grad_value = input_grad_call(d_short, following, taps)

    shares = lax.all_to_all(total_call(terms, scale), DP, 0, 0)
    grad_weight, grad_taps, grad_filter, grad_skip = spread_call(shares)
    return (
        gated[None],
        grad_query[None],
        grad_key[None],
        grad_value[None],
        grad_taps,
        grad_filter,
        grad_skip.reshape(CHANS),
        grad_weight,
    )


def solution(mesh):
    fine = Mesh(mesh.devices.reshape(2, 2, 4, 2, 4), ALL)
    tokens = P(DP, CTX, None)
    in_specs = (tokens, tokens, tokens, P(), P(), P(), P(), tokens)
    out_specs = (tokens, tokens, tokens, tokens, P(), P(), P(), P(CTX, None))
    return jax.shard_map(
        shards, mesh=fine, in_specs=in_specs, out_specs=out_specs, check_vma=False
    )
```

```python
import math

import jax
import jax.numpy as jnp
from jax import lax
from jax.experimental import pallas as pl
from jax.experimental.pallas import tpu as pltpu
from jax.sharding import Mesh
from jax.sharding import PartitionSpec as P

F32 = jnp.float32
BF16 = jnp.bfloat16
CTX = ("xh", "co")
DP = ("y", "xl", "z")
CHIPS = ("xh", "y", "xl", "z")
ALL = ("xh", "co", "y", "xl", "z")

ROWS = 256
CHANS = 256
HALF = CHANS // 2
GROUPS = 16
LENGTH = 1024
STRIP = 32
PAD = 128
WIDE = LENGTH + PAD
FEATS = 8192
TAIL = 16
SHARES = 32
SHARE = FEATS // 4
SEGMENT = 8
SPREAD = 4
PIECES = 8
VMEM_LIMIT = 20 * 1024 * 1024


def call(kernel, name, out_shape, operands, scratch=(), scalars=0, flops=1 << 10, **more):
    spec = pl.BlockSpec(memory_space=pltpu.VMEM)
    in_specs = [pl.BlockSpec(memory_space=pltpu.SMEM)] * scalars
    in_specs += [spec] * (len(operands) - scalars)
    defaults = {"in_specs": in_specs, "out_specs": jax.tree.map(lambda _: spec, out_shape)}
    more = {**defaults, **more}
    placed = [
        x if s.memory_space == pltpu.SMEM else pltpu.with_memory_space_constraint(x, s.memory_space)
        for x, s in zip(operands, more["in_specs"])
    ]
    return pl.pallas_call(
        kernel,
        out_shape=out_shape,
        scratch_shapes=list(scratch),
        compiler_params=pltpu.CompilerParams(vmem_limit_bytes=VMEM_LIMIT),
        cost_estimate=pl.CostEstimate(flops=flops, bytes_accessed=1 << 10, transcendentals=0),
        name=name,
        **more,
    )(*placed)


def lane_groups():
    return lax.broadcasted_iota(jnp.int32, (STRIP, HALF), 1) // (CHANS // GROUPS)


def later(x, count):
    row = lax.broadcasted_iota(jnp.int32, x.shape, 0)
    return jnp.where(row >= count, pltpu.roll(x, count, 0), 0.0)


def strip_of(line):
    wide = jnp.broadcast_to(line, (STRIP, WIDE))
    return pltpu.roll(wide, 0, 1, stride=1, stride_axis=0)[:, :LENGTH].astype(BF16)


def two_windows(signal_ref, n, half):
    lanes = slice(half * HALF, (half + 1) * HALF)
    windows = [signal_ref[m * STRIP : m * STRIP + LENGTH, lanes] for m in (n, n + 1)]
    return jnp.concatenate(windows, axis=1)


def all_strips(strips_ref, signal_ref):
    ids = lane_groups()
    rows = GROUPS * STRIP // 2
    columns = []
    for half in range(2):
        parts = []
        for n in range(0, ROWS // STRIP, 2):
            result = jnp.dot(
                strips_ref[half * rows : (half + 1) * rows, :],
                two_windows(signal_ref, n, half),
                preferred_element_type=F32,
            )
            for m in range(2):
                out = jnp.zeros((STRIP, HALF), F32)
                for g in range(GROUPS // 2):
                    piece = result[g * STRIP : (g + 1) * STRIP, m * HALF : (m + 1) * HALF]
                    out = jnp.where(ids == g, piece, out)
                parts.append(out)
        columns.append(jnp.concatenate(parts, axis=0))
    return jnp.concatenate(columns, axis=1)


def with_tail(tail, block):
    joined = jnp.concatenate([tail.astype(F32), block.astype(F32)], axis=0)
    return joined[TAIL:], pltpu.roll(joined, 1, 0)[TAIL:], pltpu.roll(joined, 2, 0)[TAIL:]


def short_sum(taps_ref, i, parts):
    return sum(taps_ref[i, j : j + 1, :] * parts[j] for j in range(3))


def lines_of(filter_ref, turned):
    if not turned:
        return jnp.concatenate(
            [filter_ref[...].astype(F32), jnp.zeros((GROUPS, PAD), F32)], axis=1
        )
    row = lax.broadcasted_iota(jnp.int32, (CHANS, CHANS), 0)
    col = lax.broadcasted_iota(jnp.int32, (CHANS, CHANS), 1)
    turn = (row + col == CHANS - 1).astype(F32).astype(BF16)
    pieces = [
        jnp.dot(filter_ref[:, n * CHANS : (n + 1) * CHANS], turn, preferred_element_type=F32)
        for n in reversed(range(LENGTH // CHANS))
    ]
    wide = jnp.concatenate([*pieces, jnp.zeros((GROUPS, PAD), F32)], axis=1)
    return pltpu.roll(wide, WIDE - (STRIP - 1), 1)


def pre_kernel(
    cot_ref, weight_ref, lags_ref, d_gated_ref, strips_ref, cot_buffer, weight_buffer, filter_ref,
    sems, lags_sem,
):
    tile = FEATS // PIECES
    lags_copy = pltpu.make_async_copy(lags_ref, filter_ref, lags_sem)
    lags_copy.start()
    copies = []
    for n in range(PIECES):
        piece = slice(n * tile, (n + 1) * tile)
        pair = (
            pltpu.make_async_copy(cot_ref.at[:, piece], cot_buffer.at[n], sems.at[0, n]),
            pltpu.make_async_copy(weight_ref.at[piece, :], weight_buffer.at[n], sems.at[1, n]),
        )
        for copy in pair:
            copy.start()
        copies.append(pair)
    total = jnp.zeros((ROWS, CHANS), F32)
    for n in range(PIECES):
        if n == PIECES // 2:
            lags_copy.wait()
            lines = lines_of(filter_ref, True)
            for g in range(GROUPS):
                strips_ref[g * STRIP : (g + 1) * STRIP, :] = strip_of(lines[g : g + 1])
        for copy in copies[n]:
            copy.wait()
        total += jnp.dot(cot_buffer[n], weight_buffer[n], preferred_element_type=F32)
    d_gated_ref[...] = total.astype(BF16)


def pre_call(*operands):
    tile = FEATS // PIECES
    scratch = [
        pltpu.VMEM((PIECES, ROWS, tile), BF16),
        pltpu.VMEM((PIECES, tile, CHANS), BF16),
        pltpu.VMEM((GROUPS, LENGTH), BF16),
        pltpu.SemaphoreType.DMA((2, PIECES)),
        pltpu.SemaphoreType.DMA,
    ]
    in_specs = [pl.BlockSpec(memory_space=pltpu.HBM)] * 3
    out_shape = [
        pltpu.VMEM((ROWS, CHANS), BF16),
        pltpu.VMEM((GROUPS * STRIP, LENGTH), BF16),
    ]
    return call(pre_kernel, "pre", out_shape, operands, scratch, in_specs=in_specs, flops=1 << 30)


def d_inner_kernel(d_gated_ref, query_ref, tail_ref, taps_ref, out_ref):
    q_short = short_sum(taps_ref, 0, with_tail(tail_ref[...], query_ref[...]))
    out_ref[...] = (d_gated_ref[...].astype(F32) * q_short).astype(BF16)


def d_inner_call(*operands):
    return call(d_inner_kernel, "d_inner", pltpu.VMEM((ROWS, CHANS), BF16), operands)


def fwd_kernel(
    core_ref, strips_ref, pair_ref, cross_ref, cross_pair_ref, key_ref, value_ref, query_ref,
    tail_ref, taps_ref, skip_ref,
    gated_ref, inner_ref, signal_ref,
):
    upper = core_ref[0] == 1
    pair = pair_ref[...].astype(F32)
    cross_pair = cross_pair_ref[...].astype(F32)
    near = jnp.where(upper, pair, cross_pair)
    far = jnp.where(upper, cross_pair, 0.0)
    own = jnp.concatenate([key_ref[...], value_ref[...]], axis=1).astype(F32)
    both = jnp.concatenate([far, cross_ref[...].astype(F32), near, own], axis=0)
    shifted = (both, later(both, 1), later(both, 2))
    k_short = short_sum(taps_ref, 1, [part[:, :CHANS] for part in shifted])
    v_short = short_sum(taps_ref, 2, [part[:, CHANS:] for part in shifted])
    mixed = (k_short * v_short).astype(BF16)
    signal_ref[: ROWS - STRIP, :] = jnp.zeros((ROWS - STRIP, CHANS), BF16)
    signal_ref[ROWS - STRIP :, :] = mixed
    inner = all_strips(strips_ref, signal_ref) + skip_ref[...] * mixed[LENGTH - ROWS :].astype(F32)
    inner_ref[...] = inner
    q_short = short_sum(taps_ref, 0, with_tail(tail_ref[...], query_ref[...]))
    gated_ref[...] = (q_short * inner).astype(BF16)


def fwd_call(*operands):
    out_shape = [
        pltpu.VMEM((ROWS, CHANS), BF16),
        pltpu.VMEM((ROWS, CHANS), F32),
        pltpu.VMEM((LENGTH + ROWS - STRIP, CHANS), BF16),
    ]
    return call(fwd_kernel, "fwd", out_shape, operands, (), 1, 4 << 30)


def terms_kernel(core_ref, own_cot_ref, other_cot_ref, gated_ref, other_gated_ref, out_ref):
    dims = (((0,), (0,)), ((), ()))
    for half in range(2):
        start = pl.multiple_of((2 * half + core_ref[0]) * SHARE, SHARE)
        own_cot = own_cot_ref[:, pl.ds(start, SHARE)]
        other_cot = other_cot_ref[:, pl.ds(start, SHARE)]
        total = lax.dot_general(gated_ref[...], own_cot, dims, preferred_element_type=F32)
        total += lax.dot_general(other_gated_ref[...], other_cot, dims, preferred_element_type=F32)
        out_ref[half, :, :SHARE] = total.astype(BF16)


def terms_call(*operands):
    out_shape = pltpu.VMEM((2, CHANS, SHARE + HALF), BF16)
    return call(terms_kernel, "terms", out_shape, operands, scalars=1, flops=1 << 30)


def add_small_kernel(terms_ref, small_ref, other_small_ref, out_ref, parts_ref, sems):
    total = small_ref[...] + other_small_ref[...]
    parts_ref[...] = total.reshape(CHANS, HALF).astype(BF16)
    copies = [
        pltpu.make_async_copy(parts_ref, out_ref.at[half, :, pl.ds(SHARE, HALF)], sems.at[half])
        for half in range(2)
    ]
    for copy in copies:
        copy.start()
    for copy in copies:
        copy.wait()


def add_small_call(*operands):
    place = pl.BlockSpec(memory_space=pl.ANY)
    spec = pl.BlockSpec(memory_space=pltpu.VMEM)
    return pl.pallas_call(
        add_small_kernel,
        in_specs=[place, spec, spec],
        out_specs=place,
        out_shape=jax.ShapeDtypeStruct(operands[0].shape, BF16),
        scratch_shapes=[pltpu.VMEM((CHANS, HALF), BF16), pltpu.SemaphoreType.DMA((2,))],
        input_output_aliases={0: 0},
        compiler_params=pltpu.CompilerParams(vmem_limit_bytes=VMEM_LIMIT),
        name="add_small",
    )(
        operands[0],
        *(pltpu.with_memory_space_constraint(x, pltpu.VMEM) for x in operands[1:]),
    )


def place(row):
    return row % SHARES, row // SHARES


def tap_place(n, half):
    return place(GROUPS * LENGTH // HALF + 2 * n + half)


def turn_matrix(size, block):
    row = lax.broadcasted_iota(jnp.int32, (size, size), 0)
    col = lax.broadcasted_iota(jnp.int32, (size, size), 1)
    return ((row // block) * block + (block - 1 - row % block) == col).astype(F32)


def lag_kernel(d_inner_ref, signal_ref, filter_ref, outer_ref, stack_ref, sums_ref):
    turn = turn_matrix(ROWS, STRIP).astype(BF16)
    turned = jnp.dot(turn, d_inner_ref[...], preferred_element_type=F32)
    ids = lane_groups()
    count = GROUPS * STRIP // 2
    outer_ref[:, LENGTH:] = jnp.zeros((GROUPS * STRIP, PAD), F32)
    for half in range(2):
        rows = slice(half * count, (half + 1) * count)
        for n in range(0, ROWS // STRIP, 2):
            for m in range(2):
                start = (n + m) * STRIP
                piece = turned[start : start + STRIP, half * HALF : (half + 1) * HALF]
                for g in range(GROUPS // 2):
                    stack_ref[g * STRIP : (g + 1) * STRIP, m * HALF : (m + 1) * HALF] = jnp.where(
                        ids == g, piece, 0.0
                    ).astype(BF16)
            term = lax.dot_general(
                stack_ref[...],
                two_windows(signal_ref, n, half),
                (((1,), (1,)), ((), ())),
                preferred_element_type=F32,
            )
            if n == 0:
                outer_ref[rows, :LENGTH] = term
            else:
                outer_ref[rows, :LENGTH] += term
    for g in range(GROUPS):
        rows = outer_ref[g * STRIP : (g + 1) * STRIP, :]
        skewed = pltpu.roll(rows, WIDE - (STRIP - 1), 1, stride=1, stride_axis=0)
        sums_ref[g : g + 1, :] = jnp.sum(skewed, axis=0, keepdims=True)
    sums = pltpu.roll(sums_ref[...], STRIP - 1, 1)
    turn = turn_matrix(CHANS, CHANS)
    last = LENGTH // CHANS - 1
    for n in range(LENGTH // CHANS):
        filter_ref[:, n * CHANS : (n + 1) * CHANS] = jnp.dot(
            sums[:, (last - n) * CHANS : (last - n + 1) * CHANS],
            turn,
            precision=lax.Precision.HIGHEST,
            preferred_element_type=F32,
        )


def lag_call(*operands):
    scratch = [
        pltpu.VMEM((GROUPS * STRIP, WIDE), F32),
        pltpu.VMEM((GROUPS * STRIP // 2, CHANS), BF16),
        pltpu.VMEM((GROUPS, WIDE), F32),
    ]
    return call(lag_kernel, "lag_sums", pltpu.VMEM((GROUPS, LENGTH), F32), operands, scratch)


def bwd_kernel(
    core_ref, d0_ref, d1_ref, d2_ref, d3_ref, lags_ref, filter_ref, signal_ref, key_ref, value_ref,
    pair_ref, cross_pair_ref, query_ref, tail_ref, inner_ref, d_gated_ref, taps_ref, skip_ref,
    d_short_ref, head_ref, small_ref,
    strips_ref, ahead_ref,
):
    for n, ref in enumerate((d0_ref, d1_ref, d2_ref, d3_ref)):
        ahead_ref[n * ROWS : (n + 1) * ROWS, :] = ref[...]
    ahead_ref[LENGTH:, :] = jnp.zeros((ROWS, CHANS), BF16)
    lines = lines_of(lags_ref, False)
    for g in range(GROUPS):
        strips_ref[g * STRIP : (g + 1) * STRIP, :] = strip_of(lines[g : g + 1])
    d_inner = d0_ref[...].astype(F32)
    mixed = signal_ref[LENGTH - STRIP :, :]
    d_mixed = all_strips(strips_ref, ahead_ref) + skip_ref[...] * d_inner

    upper = core_ref[0] == 1
    last = slice(ROWS - TAIL, ROWS)
    near = jnp.where(upper, pair_ref[last, :].astype(F32), cross_pair_ref[last, :].astype(F32))
    k_parts = with_tail(near[:, :CHANS], key_ref[...])
    v_parts = with_tail(near[:, CHANS:], value_ref[...])
    q_parts = with_tail(tail_ref[...], query_ref[...])
    small_ref[...] = jnp.zeros_like(small_ref)
    sums = []
    d_qs = d_gated_ref[...].astype(F32) * inner_ref[...]
    d_ks = d_mixed * short_sum(taps_ref, 2, v_parts)
    d_vs = d_mixed * short_sum(taps_ref, 1, k_parts)
    for i, (grad, parts) in enumerate(((d_qs, q_parts), (d_ks, k_parts), (d_vs, v_parts))):
        d_short_ref[i] = grad
        head_ref[i] = grad[:8]
        for j in range(3):
            sums.append(jnp.sum(grad * parts[j], axis=0, keepdims=True))
    sums.append(jnp.sum(d_inner * mixed.astype(F32), axis=0, keepdims=True))
    for n, row in enumerate(sums):
        for half in range(2):
            share, slot = tap_place(n, half)
            small_ref[share, slot : slot + 1, :] = row[:, half * HALF : (half + 1) * HALF]

    for g in range(GROUPS):
        for n in range(LENGTH // HALF):
            share, slot = place(g * (LENGTH // HALF) + n)
            small_ref[share, slot : slot + 1, :] = filter_ref[g : g + 1, n * HALF : (n + 1) * HALF]


def bwd_call(*operands):
    out_shape = [
        pltpu.VMEM((3, ROWS, CHANS), F32),
        pltpu.VMEM((3, 8, CHANS), F32),
        pltpu.VMEM((SHARES, SEGMENT, HALF), F32),
    ]
    scratch = [
        pltpu.VMEM((GROUPS * STRIP, LENGTH), BF16),
        pltpu.VMEM((LENGTH + ROWS, CHANS), BF16),
    ]
    return call(bwd_kernel, "bwd", out_shape, operands, scratch, 1)


def input_grad_kernel(d_short_ref, next_ref, taps_ref, query_ref, key_ref, value_ref):
    for i, out_ref in enumerate((query_ref, key_ref, value_ref)):
        joined = jnp.concatenate([d_short_ref[i], next_ref[i]], axis=0)
        rows = joined.shape[0]
        parts = (
            joined[:ROWS],
            pltpu.roll(joined, rows - 1, 0)[:ROWS],
            pltpu.roll(joined, rows - 2, 0)[:ROWS],
        )
        out_ref[...] = short_sum(taps_ref, i, parts).astype(BF16)


def input_grad_call(*operands):
    out_shape = [jax.ShapeDtypeStruct((ROWS, CHANS), BF16)] * 3
    return call(input_grad_kernel, "input_grads", out_shape, operands)


def total_kernel(scale, terms_ref, out_ref):
    total = (jnp.sum(terms_ref[...].astype(F32), axis=0) * scale).astype(BF16)
    out_ref[...] = jnp.broadcast_to(total[None], out_ref.shape)


def total_call(terms, scale):
    out_shape = pltpu.VMEM((SHARES, *terms.shape[1:]), BF16)
    return call(lambda *refs: total_kernel(scale, *refs), "total", out_shape, (terms,))


def spread_kernel(
    shares_ref, weight_ref, taps_ref, filter_ref, skip_ref, turned_ref, sems
):
    tile = SHARE // SPREAD
    copies = []
    for n in range(SPREAD):
        piece = slice(n * tile, (n + 1) * tile)
        turned_ref[piece, :] = shares_ref[:, piece].astype(F32).T
        copies.append(
            pltpu.make_async_copy(turned_ref.at[piece, :], weight_ref.at[piece, :], sems.at[n])
        )
        copies[-1].start()
    small = shares_ref[:, SHARE:].astype(F32)

    def part(share, slot):
        return small[share * SEGMENT + slot : share * SEGMENT + slot + 1]

    for g in range(GROUPS):
        for n in range(LENGTH // HALF):
            piece = part(*place(g * (LENGTH // HALF) + n))
            filter_ref[g : g + 1, n * HALF : (n + 1) * HALF] = piece
    for half in range(2):
        lanes = slice(half * HALF, (half + 1) * HALF)
        for n in range(9):
            taps_ref[n // 3, n % 3 : n % 3 + 1, lanes] = part(*tap_place(n, half))
        skip_ref[:, lanes] = part(*tap_place(9, half))
    for copy in copies:
        copy.wait()


def spread_call(shares):
    out_shape = [
        jax.ShapeDtypeStruct((SHARE, CHANS), F32),
        jax.ShapeDtypeStruct((3, 3, CHANS), F32),
        jax.ShapeDtypeStruct((GROUPS, LENGTH), F32),
        jax.ShapeDtypeStruct((1, CHANS), F32),
    ]
    scratch = [pltpu.VMEM((SHARE, CHANS), F32), pltpu.SemaphoreType.DMA((SPREAD,))]
    out_specs = [pl.BlockSpec(memory_space=pl.ANY)]
    out_specs += [pl.BlockSpec(memory_space=pltpu.VMEM)] * 3
    shares = shares.reshape(CHANS, SHARE + HALF)
    return call(spread_kernel, "spread", out_shape, (shares,), scratch, out_specs=out_specs)


def sent(block, distance):
    count = 4
    route = [(i, i + distance) for i in range(count) if 0 <= i + distance < count]
    return lax.ppermute(block, CTX, route)


def shards(
    query_in, key_in, value_in, short_taps, long_filter, skip_gain, out_weight, out_cotangent
):
    query = query_in[0]
    cot = out_cotangent[0]
    taps = short_taps
    skip = skip_gain.reshape(1, CHANS)
    devices = lax.axis_size(ALL)
    tokens = ROWS * devices
    scale = 1.0 / math.sqrt(tokens)
    core = lax.axis_index("co").astype(jnp.int32).reshape(1)

    key = key_in[0]
    value = value_in[0]
    swap = [(0, 1), (1, 0)]
    own = jnp.concatenate([key, value], axis=1)
    tail = sent(query[ROWS - TAIL :], 1)
    cross = lax.ppermute(own, "xh", [(0, 1)])
    pair = lax.ppermute(own, "co", swap)
    other_cot = lax.ppermute(cot, "co", swap)

    d_gated, strips = pre_call(cot, out_weight, long_filter)
    cross, tail, d_gated = lax.optimization_barrier((cross, tail, d_gated))
    cross_pair = lax.ppermute(cross, "co", swap)
    d_inner = d_inner_call(d_gated, query, tail, taps)
    blocks = [d_inner] + [sent(d_inner, -distance) for distance in (1, 2, 3)]
    gated, inner, signal = fwd_call(
        core, strips, pair, cross, cross_pair, key, value, query, tail, taps, skip
    )
    other_gated = lax.ppermute(gated, "co", swap)
    lag_sums = lag_call(d_inner, signal)
    d_short, head, small = bwd_call(
        core, *blocks, long_filter, lag_sums, signal, key, value, pair, cross_pair, query, tail,
        inner, d_gated, taps, skip,
    )
    other_gated, head, small = lax.optimization_barrier((other_gated, head, small))
    other_small = lax.ppermute(small, "co", swap)
    terms = terms_call(core, cot, other_cot, gated, other_gated)
    terms, other_small = lax.optimization_barrier((terms, other_small))
    terms = add_small_call(terms, small, other_small)
    terms, head = lax.optimization_barrier((terms, head))
    terms = terms.reshape(2 * SHARES, CHANS // SHARES, SHARE + HALF)
    terms = lax.all_to_all(terms, CHIPS, 0, 0)
    following = sent(head, -1)
    grad_query, grad_key, grad_value = input_grad_call(d_short, following, taps)

    shares = lax.all_to_all(total_call(terms, scale), DP, 0, 0)
    grad_weight, grad_taps, grad_filter, grad_skip = spread_call(shares)
    return (
        gated[None],
        grad_query[None],
        grad_key[None],
        grad_value[None],
        grad_taps,
        grad_filter,
        grad_skip.reshape(CHANS),
        grad_weight,
    )


def solution(mesh):
    fine = Mesh(mesh.devices.reshape(2, 2, 4, 2, 4), ALL)
    tokens = P(DP, CTX, None)
    in_specs = (tokens, tokens, tokens, P(), P(), P(), P(), tokens)
    out_specs = (tokens, tokens, tokens, tokens, P(), P(), P(), P(CTX, None))
    return jax.shard_map(
        shards, mesh=fine, in_specs=in_specs, out_specs=out_specs, check_vma=False
    )
```

```python
import math

import jax
import jax.numpy as jnp
from jax import lax
from jax.experimental import pallas as pl
from jax.experimental.pallas import tpu as pltpu
from jax.sharding import Mesh
from jax.sharding import PartitionSpec as P

F32 = jnp.float32
BF16 = jnp.bfloat16
CTX = ("xh", "co")
DP = ("y", "xl", "z")
CHIPS = ("xh", "y", "xl", "z")
ALL = ("xh", "co", "y", "xl", "z")

ROWS = 256
CHANS = 256
HALF = CHANS // 2
GROUPS = 16
LENGTH = 1024
STRIP = 32
PAD = 128
WIDE = LENGTH + PAD
FEATS = 8192
TAIL = 16
SHARES = 32
SHARE = FEATS // 4
SEGMENT = 8
SPREAD = 4
PIECES = 8
VMEM_LIMIT = 20 * 1024 * 1024


def call(kernel, name, out_shape, operands, scratch=(), scalars=0, flops=1 << 10, **more):
    spec = pl.BlockSpec(memory_space=pltpu.VMEM)
    in_specs = [pl.BlockSpec(memory_space=pltpu.SMEM)] * scalars
    in_specs += [spec] * (len(operands) - scalars)
    defaults = {"in_specs": in_specs, "out_specs": jax.tree.map(lambda _: spec, out_shape)}
    more = {**defaults, **more}
    placed = [
        x if s.memory_space == pltpu.SMEM else pltpu.with_memory_space_constraint(x, s.memory_space)
        for x, s in zip(operands, more["in_specs"])
    ]
    return pl.pallas_call(
        kernel,
        out_shape=out_shape,
        scratch_shapes=list(scratch),
        compiler_params=pltpu.CompilerParams(vmem_limit_bytes=VMEM_LIMIT),
        cost_estimate=pl.CostEstimate(flops=flops, bytes_accessed=1 << 10, transcendentals=0),
        name=name,
        **more,
    )(*placed)


def lane_groups():
    return lax.broadcasted_iota(jnp.int32, (STRIP, HALF), 1) // (CHANS // GROUPS)


def later(x, count):
    row = lax.broadcasted_iota(jnp.int32, x.shape, 0)
    return jnp.where(row >= count, pltpu.roll(x, count, 0), 0.0)


def strip_of(line):
    wide = jnp.broadcast_to(line, (STRIP, WIDE))
    return pltpu.roll(wide, 0, 1, stride=1, stride_axis=0)[:, :LENGTH].astype(BF16)


def two_windows(signal_ref, n, half):
    lanes = slice(half * HALF, (half + 1) * HALF)
    windows = [signal_ref[m * STRIP : m * STRIP + LENGTH, lanes] for m in (n, n + 1)]
    return jnp.concatenate(windows, axis=1)


def all_strips(strips_ref, signal_ref):
    ids = lane_groups()
    rows = GROUPS * STRIP // 2
    columns = []
    for half in range(2):
        parts = []
        for n in range(0, ROWS // STRIP, 2):
            result = jnp.dot(
                strips_ref[half * rows : (half + 1) * rows, :],
                two_windows(signal_ref, n, half),
                preferred_element_type=F32,
            )
            for m in range(2):
                out = jnp.zeros((STRIP, HALF), F32)
                for g in range(GROUPS // 2):
                    piece = result[g * STRIP : (g + 1) * STRIP, m * HALF : (m + 1) * HALF]
                    out = jnp.where(ids == g, piece, out)
                parts.append(out)
        columns.append(jnp.concatenate(parts, axis=0))
    return jnp.concatenate(columns, axis=1)


def with_tail(tail, block):
    joined = jnp.concatenate([tail.astype(F32), block.astype(F32)], axis=0)
    return joined[TAIL:], pltpu.roll(joined, 1, 0)[TAIL:], pltpu.roll(joined, 2, 0)[TAIL:]


def short_sum(taps_ref, i, parts):
    return sum(taps_ref[i, j : j + 1, :] * parts[j] for j in range(3))


def lines_of(filter_ref, turned):
    if not turned:
        return jnp.concatenate(
            [filter_ref[...].astype(F32), jnp.zeros((GROUPS, PAD), F32)], axis=1
        )
    row = lax.broadcasted_iota(jnp.int32, (CHANS, CHANS), 0)
    col = lax.broadcasted_iota(jnp.int32, (CHANS, CHANS), 1)
    turn = (row + col == CHANS - 1).astype(F32).astype(BF16)
    pieces = [
        jnp.dot(filter_ref[:, n * CHANS : (n + 1) * CHANS], turn, preferred_element_type=F32)
        for n in reversed(range(LENGTH // CHANS))
    ]
    wide = jnp.concatenate([*pieces, jnp.zeros((GROUPS, PAD), F32)], axis=1)
    return pltpu.roll(wide, WIDE - (STRIP - 1), 1)


def pre_kernel(
    cot_ref, weight_ref, lags_ref, d_gated_ref, strips_ref, cot_buffer, weight_buffer, filter_ref,
    sems, lags_sem,
):
    tile = FEATS // PIECES
    lags_copy = pltpu.make_async_copy(lags_ref, filter_ref, lags_sem)
    lags_copy.start()
    copies = []
    for n in range(PIECES):
        piece = slice(n * tile, (n + 1) * tile)
        pair = (
            pltpu.make_async_copy(cot_ref.at[:, piece], cot_buffer.at[n], sems.at[0, n]),
            pltpu.make_async_copy(weight_ref.at[piece, :], weight_buffer.at[n], sems.at[1, n]),
        )
        for copy in pair:
            copy.start()
        copies.append(pair)
    total = jnp.zeros((ROWS, CHANS), F32)
    for n in range(PIECES):
        if n == PIECES // 2:
            lags_copy.wait()
            lines = lines_of(filter_ref, True)
            for g in range(GROUPS):
                strips_ref[g * STRIP : (g + 1) * STRIP, :] = strip_of(lines[g : g + 1])
        for copy in copies[n]:
            copy.wait()
        total += jnp.dot(cot_buffer[n], weight_buffer[n], preferred_element_type=F32)
    d_gated_ref[...] = total.astype(BF16)


def pre_call(*operands):
    tile = FEATS // PIECES
    scratch = [
        pltpu.VMEM((PIECES, ROWS, tile), BF16),
        pltpu.VMEM((PIECES, tile, CHANS), BF16),
        pltpu.VMEM((GROUPS, LENGTH), BF16),
        pltpu.SemaphoreType.DMA((2, PIECES)),
        pltpu.SemaphoreType.DMA,
    ]
    in_specs = [pl.BlockSpec(memory_space=pltpu.HBM)] * 3
    out_shape = [
        pltpu.VMEM((ROWS, CHANS), BF16),
        pltpu.VMEM((GROUPS * STRIP, LENGTH), BF16),
    ]
    return call(pre_kernel, "pre", out_shape, operands, scratch, in_specs=in_specs, flops=1 << 30)


def d_inner_kernel(d_gated_ref, query_ref, tail_ref, taps_ref, out_ref):
    q_short = short_sum(taps_ref, 0, with_tail(tail_ref[...], query_ref[...]))
    out_ref[...] = (d_gated_ref[...].astype(F32) * q_short).astype(BF16)


def d_inner_call(*operands):
    return call(d_inner_kernel, "d_inner", pltpu.VMEM((ROWS, CHANS), BF16), operands)


def fwd_kernel(
    core_ref, strips_ref, pair_ref, cross_ref, cross_pair_ref, key_ref, value_ref, query_ref,
    tail_ref, taps_ref, skip_ref,
    gated_ref, inner_ref, signal_ref,
):
    upper = core_ref[0] == 1
    pair = pair_ref[...].astype(F32)
    cross_pair = cross_pair_ref[...].astype(F32)
    near = jnp.where(upper, pair, cross_pair)
    far = jnp.where(upper, cross_pair, 0.0)
    own = jnp.concatenate([key_ref[...], value_ref[...]], axis=1).astype(F32)
    both = jnp.concatenate([far, cross_ref[...].astype(F32), near, own], axis=0)
    shifted = (both, later(both, 1), later(both, 2))
    k_short = short_sum(taps_ref, 1, [part[:, :CHANS] for part in shifted])
    v_short = short_sum(taps_ref, 2, [part[:, CHANS:] for part in shifted])
    mixed = (k_short * v_short).astype(BF16)
    signal_ref[: ROWS - STRIP, :] = jnp.zeros((ROWS - STRIP, CHANS), BF16)
    signal_ref[ROWS - STRIP :, :] = mixed
    inner = all_strips(strips_ref, signal_ref) + skip_ref[...] * mixed[LENGTH - ROWS :].astype(F32)
    inner_ref[...] = inner
    q_short = short_sum(taps_ref, 0, with_tail(tail_ref[...], query_ref[...]))
    gated_ref[...] = (q_short * inner).astype(BF16)


def fwd_call(*operands):
    out_shape = [
        pltpu.VMEM((ROWS, CHANS), BF16),
        pltpu.VMEM((ROWS, CHANS), F32),
        pltpu.VMEM((LENGTH + ROWS - STRIP, CHANS), BF16),
    ]
    return call(fwd_kernel, "fwd", out_shape, operands, (), 1, 4 << 30)


def terms_kernel(core_ref, own_cot_ref, other_cot_ref, gated_ref, other_gated_ref, out_ref):
    dims = (((0,), (0,)), ((), ()))
    for half in range(2):
        start = pl.multiple_of((2 * half + core_ref[0]) * SHARE, SHARE)
        own_cot = own_cot_ref[:, pl.ds(start, SHARE)]
        total = lax.dot_general(gated_ref[...], own_cot, dims, preferred_element_type=F32)
        total += lax.dot_general(other_gated_ref[...], other_cot_ref[half], dims, preferred_element_type=F32)
        out_ref[half, :, :SHARE] = total.astype(BF16)


def terms_call(*operands):
    out_shape = pltpu.VMEM((2, CHANS, SHARE + HALF), BF16)
    return call(terms_kernel, "terms", out_shape, operands, scalars=1, flops=1 << 30)


def add_small_kernel(terms_ref, small_ref, other_small_ref, out_ref, parts_ref, sems):
    total = small_ref[...] + other_small_ref[...]
    parts_ref[...] = total.reshape(CHANS, HALF).astype(BF16)
    copies = [
        pltpu.make_async_copy(parts_ref, out_ref.at[half, :, pl.ds(SHARE, HALF)], sems.at[half])
        for half in range(2)
    ]
    for copy in copies:
        copy.start()
    for copy in copies:
        copy.wait()


def add_small_call(*operands):
    place = pl.BlockSpec(memory_space=pl.ANY)
    spec = pl.BlockSpec(memory_space=pltpu.VMEM)
    return pl.pallas_call(
        add_small_kernel,
        in_specs=[place, spec, spec],
        out_specs=place,
        out_shape=jax.ShapeDtypeStruct(operands[0].shape, BF16),
        scratch_shapes=[pltpu.VMEM((CHANS, HALF), BF16), pltpu.SemaphoreType.DMA((2,))],
        input_output_aliases={0: 0},
        compiler_params=pltpu.CompilerParams(vmem_limit_bytes=VMEM_LIMIT),
        name="add_small",
    )(
        operands[0],
        *(pltpu.with_memory_space_constraint(x, pltpu.VMEM) for x in operands[1:]),
    )


def place(row):
    return row % SHARES, row // SHARES


def tap_place(n, half):
    return place(GROUPS * LENGTH // HALF + 2 * n + half)


def turn_matrix(size, block):
    row = lax.broadcasted_iota(jnp.int32, (size, size), 0)
    col = lax.broadcasted_iota(jnp.int32, (size, size), 1)
    return ((row // block) * block + (block - 1 - row % block) == col).astype(F32)


def lag_kernel(
    core_ref, cot_ref, d_inner_ref, signal_ref,
    filter_ref, part_ref,
    outer_ref, stack_ref, sums_ref, sems,
):
    copies = []
    for half in range(2):
        start = pl.multiple_of((2 * half + core_ref[0]) * SHARE, SHARE)
        copies.append(
            pltpu.make_async_copy(
                cot_ref.at[:, pl.ds(start, SHARE)], part_ref.at[half], sems.at[half]
            )
        )
        copies[-1].start()
    turn = turn_matrix(ROWS, STRIP).astype(BF16)
    turned = jnp.dot(turn, d_inner_ref[...], preferred_element_type=F32)
    ids = lane_groups()
    count = GROUPS * STRIP // 2
    outer_ref[:, LENGTH:] = jnp.zeros((GROUPS * STRIP, PAD), F32)
    for half in range(2):
        rows = slice(half * count, (half + 1) * count)
        for n in range(0, ROWS // STRIP, 2):
            for m in range(2):
                start = (n + m) * STRIP
                piece = turned[start : start + STRIP, half * HALF : (half + 1) * HALF]
                for g in range(GROUPS // 2):
                    stack_ref[g * STRIP : (g + 1) * STRIP, m * HALF : (m + 1) * HALF] = jnp.where(
                        ids == g, piece, 0.0
                    ).astype(BF16)
            term = lax.dot_general(
                stack_ref[...],
                two_windows(signal_ref, n, half),
                (((1,), (1,)), ((), ())),
                preferred_element_type=F32,
            )
            if n == 0:
                outer_ref[rows, :LENGTH] = term
            else:
                outer_ref[rows, :LENGTH] += term
    for g in range(GROUPS):
        rows = outer_ref[g * STRIP : (g + 1) * STRIP, :]
        skewed = pltpu.roll(rows, WIDE - (STRIP - 1), 1, stride=1, stride_axis=0)
        sums_ref[g : g + 1, :] = jnp.sum(skewed, axis=0, keepdims=True)
    sums = pltpu.roll(sums_ref[...], STRIP - 1, 1)
    turn = turn_matrix(CHANS, CHANS)
    last = LENGTH // CHANS - 1
    for n in range(LENGTH // CHANS):
        filter_ref[:, n * CHANS : (n + 1) * CHANS] = jnp.dot(
            sums[:, (last - n) * CHANS : (last - n + 1) * CHANS],
            turn,
            precision=lax.Precision.HIGHEST,
            preferred_element_type=F32,
        )
    for copy in copies:
        copy.wait()


def lag_call(*operands):
    scratch = [
        pltpu.VMEM((GROUPS * STRIP, WIDE), F32),
        pltpu.VMEM((GROUPS * STRIP // 2, CHANS), BF16),
        pltpu.VMEM((GROUPS, WIDE), F32),
        pltpu.SemaphoreType.DMA((2,)),
    ]
    out_shape = [pltpu.VMEM((GROUPS, LENGTH), F32), pltpu.VMEM((2, ROWS, SHARE), BF16)]
    in_specs = [pl.BlockSpec(memory_space=pltpu.SMEM), pl.BlockSpec(memory_space=pltpu.HBM)]
    in_specs += [pl.BlockSpec(memory_space=pltpu.VMEM)] * 2
    return call(lag_kernel, "lag_sums", out_shape, operands, scratch, in_specs=in_specs)


def bwd_kernel(
    core_ref, d0_ref, d1_ref, d2_ref, d3_ref, lags_ref, filter_ref, signal_ref, key_ref, value_ref,
    pair_ref, cross_pair_ref, query_ref, tail_ref, inner_ref, d_gated_ref, taps_ref, skip_ref,
    d_short_ref, head_ref, small_ref,
    strips_ref, ahead_ref,
):
    for n, ref in enumerate((d0_ref, d1_ref, d2_ref, d3_ref)):
        ahead_ref[n * ROWS : (n + 1) * ROWS, :] = ref[...]
    ahead_ref[LENGTH:, :] = jnp.zeros((ROWS, CHANS), BF16)
    lines = lines_of(lags_ref, False)
    for g in range(GROUPS):
        strips_ref[g * STRIP : (g + 1) * STRIP, :] = strip_of(lines[g : g + 1])
    d_inner = d0_ref[...].astype(F32)
    mixed = signal_ref[LENGTH - STRIP :, :]
    d_mixed = all_strips(strips_ref, ahead_ref) + skip_ref[...] * d_inner

    upper = core_ref[0] == 1
    last = slice(ROWS - TAIL, ROWS)
    near = jnp.where(upper, pair_ref[last, :].astype(F32), cross_pair_ref[last, :].astype(F32))
    k_parts = with_tail(near[:, :CHANS], key_ref[...])
    v_parts = with_tail(near[:, CHANS:], value_ref[...])
    q_parts = with_tail(tail_ref[...], query_ref[...])
    small_ref[...] = jnp.zeros_like(small_ref)
    sums = []
    d_qs = d_gated_ref[...].astype(F32) * inner_ref[...]
    d_ks = d_mixed * short_sum(taps_ref, 2, v_parts)
    d_vs = d_mixed * short_sum(taps_ref, 1, k_parts)
    for i, (grad, parts) in enumerate(((d_qs, q_parts), (d_ks, k_parts), (d_vs, v_parts))):
        d_short_ref[i] = grad
        head_ref[i] = grad[:8]
        for j in range(3):
            sums.append(jnp.sum(grad * parts[j], axis=0, keepdims=True))
    sums.append(jnp.sum(d_inner * mixed.astype(F32), axis=0, keepdims=True))
    for n, row in enumerate(sums):
        for half in range(2):
            share, slot = tap_place(n, half)
            small_ref[share, slot : slot + 1, :] = row[:, half * HALF : (half + 1) * HALF]

    for g in range(GROUPS):
        for n in range(LENGTH // HALF):
            share, slot = place(g * (LENGTH // HALF) + n)
            small_ref[share, slot : slot + 1, :] = filter_ref[g : g + 1, n * HALF : (n + 1) * HALF]


def bwd_call(*operands):
    out_shape = [
        pltpu.VMEM((3, ROWS, CHANS), F32),
        pltpu.VMEM((3, 8, CHANS), F32),
        pltpu.VMEM((SHARES, SEGMENT, HALF), F32),
    ]
    scratch = [
        pltpu.VMEM((GROUPS * STRIP, LENGTH), BF16),
        pltpu.VMEM((LENGTH + ROWS, CHANS), BF16),
    ]
    return call(bwd_kernel, "bwd", out_shape, operands, scratch, 1)


def input_grads(d_short_ref, next_ref, taps_ref, out_refs):
    for i, out_ref in enumerate(out_refs):
        joined = jnp.concatenate([d_short_ref[i], next_ref[i]], axis=0)
        rows = joined.shape[0]
        parts = (
            joined[:ROWS],
            pltpu.roll(joined, rows - 1, 0)[:ROWS],
            pltpu.roll(joined, rows - 2, 0)[:ROWS],
        )
        out_ref[...] = short_sum(taps_ref, i, parts).astype(BF16)


def total_kernel(scale, terms_ref, out_ref):
    total = (jnp.sum(terms_ref[...].astype(F32), axis=0) * scale).astype(BF16)
    out_ref[...] = jnp.broadcast_to(total[None], out_ref.shape)


def total_call(terms, scale):
    out_shape = pltpu.VMEM((SHARES, *terms.shape[1:]), BF16)
    return call(lambda *refs: total_kernel(scale, *refs), "total", out_shape, (terms,))


def spread_kernel(
    shares_ref, d_short_ref, next_ref, short_taps_ref,
    weight_ref, taps_ref, filter_ref, skip_ref, query_ref, key_ref, value_ref,
    turned_ref, sems,
):
    tile = SHARE // SPREAD
    copies = []
    for n in range(SPREAD):
        piece = slice(n * tile, (n + 1) * tile)
        turned_ref[piece, :] = shares_ref[:, piece].astype(F32).T
        copies.append(
            pltpu.make_async_copy(turned_ref.at[piece, :], weight_ref.at[piece, :], sems.at[n])
        )
        copies[-1].start()
    input_grads(d_short_ref, next_ref, short_taps_ref, (query_ref, key_ref, value_ref))
    small = shares_ref[:, SHARE:].astype(F32)

    def part(share, slot):
        return small[share * SEGMENT + slot : share * SEGMENT + slot + 1]

    for g in range(GROUPS):
        for n in range(LENGTH // HALF):
            piece = part(*place(g * (LENGTH // HALF) + n))
            filter_ref[g : g + 1, n * HALF : (n + 1) * HALF] = piece
    for half in range(2):
        lanes = slice(half * HALF, (half + 1) * HALF)
        for n in range(9):
            taps_ref[n // 3, n % 3 : n % 3 + 1, lanes] = part(*tap_place(n, half))
        skip_ref[:, lanes] = part(*tap_place(9, half))
    for copy in copies:
        copy.wait()


def spread_call(shares, *operands):
    out_shape = [
        jax.ShapeDtypeStruct((SHARE, CHANS), F32),
        jax.ShapeDtypeStruct((3, 3, CHANS), F32),
        jax.ShapeDtypeStruct((GROUPS, LENGTH), F32),
        jax.ShapeDtypeStruct((1, CHANS), F32),
        *[jax.ShapeDtypeStruct((ROWS, CHANS), BF16)] * 3,
    ]
    scratch = [pltpu.VMEM((SHARE, CHANS), F32), pltpu.SemaphoreType.DMA((SPREAD,))]
    out_specs = [pl.BlockSpec(memory_space=pl.ANY)]
    out_specs += [pl.BlockSpec(memory_space=pltpu.VMEM)] * 6
    shares = shares.reshape(CHANS, SHARE + HALF)
    operands = (shares, *operands)
    return call(spread_kernel, "spread", out_shape, operands, scratch, out_specs=out_specs)


def sent(block, distance):
    count = 4
    route = [(i, i + distance) for i in range(count) if 0 <= i + distance < count]
    return lax.ppermute(block, CTX, route)


def shards(
    query_in, key_in, value_in, short_taps, long_filter, skip_gain, out_weight, out_cotangent
):
    query = query_in[0]
    cot = out_cotangent[0]
    taps = short_taps
    skip = skip_gain.reshape(1, CHANS)
    devices = lax.axis_size(ALL)
    tokens = ROWS * devices
    scale = 1.0 / math.sqrt(tokens)
    core = lax.axis_index("co").astype(jnp.int32).reshape(1)

    key = key_in[0]
    value = value_in[0]
    swap = [(0, 1), (1, 0)]
    own = jnp.concatenate([key, value], axis=1)
    tail = sent(query[ROWS - TAIL :], 1)
    cross = lax.ppermute(own, "xh", [(0, 1)])
    pair = lax.ppermute(own, "co", swap)
    other_cot = lax.ppermute(cot, "co", swap)

    d_gated, strips = pre_call(cot, out_weight, long_filter)
    cross, tail, d_gated = lax.optimization_barrier((cross, tail, d_gated))
    cross_pair = lax.ppermute(cross, "co", swap)
    d_inner = d_inner_call(d_gated, query, tail, taps)
    blocks = [d_inner] + [sent(d_inner, -distance) for distance in (1, 2, 3)]
    gated, inner, signal = fwd_call(
        core, strips, pair, cross, cross_pair, key, value, query, tail, taps, skip
    )
    other_gated = lax.ppermute(gated, "co", swap)
    lag_sums, other_part = lag_call(core, other_cot, d_inner, signal)
    d_short, head, small = bwd_call(
        core, *blocks, long_filter, lag_sums, signal, key, value, pair, cross_pair, query, tail,
        inner, d_gated, taps, skip,
    )
    other_gated, head, small = lax.optimization_barrier((other_gated, head, small))
    other_small = lax.ppermute(small, "co", swap)
    terms = terms_call(core, cot, other_part, gated, other_gated)
    terms, other_small = lax.optimization_barrier((terms, other_small))
    terms = add_small_call(terms, small, other_small)
    terms, head = lax.optimization_barrier((terms, head))
    terms = terms.reshape(2 * SHARES, CHANS // SHARES, SHARE + HALF)
    terms = lax.all_to_all(terms, CHIPS, 0, 0)
    following = sent(head, -1)

    shares = lax.all_to_all(total_call(terms, scale), DP, 0, 0)
    grad_weight, grad_taps, grad_filter, grad_skip, *input_grad = spread_call(
        shares, d_short, following, taps
    )
    return (
        gated[None],
        *(grad[None] for grad in input_grad),
        grad_taps,
        grad_filter,
        grad_skip.reshape(CHANS),
        grad_weight,
    )


def solution(mesh):
    fine = Mesh(mesh.devices.reshape(2, 2, 4, 2, 4), ALL)
    tokens = P(DP, CTX, None)
    in_specs = (tokens, tokens, tokens, P(), P(), P(), P(), tokens)
    out_specs = (tokens, tokens, tokens, tokens, P(), P(), P(), P(CTX, None))
    return jax.shard_map(
        shards, mesh=fine, in_specs=in_specs, out_specs=out_specs, check_vma=False
    )
```

```python
import math

import jax
import jax.numpy as jnp
from jax import lax
from jax.experimental import pallas as pl
from jax.experimental.pallas import tpu as pltpu
from jax.sharding import Mesh
from jax.sharding import PartitionSpec as P

F32 = jnp.float32
BF16 = jnp.bfloat16
CTX = ("xh", "co")
DP = ("y", "xl", "z")
CHIPS = ("xh", "y", "xl", "z")
ALL = ("xh", "co", "y", "xl", "z")

ROWS = 256
CHANS = 256
HALF = CHANS // 2
GROUPS = 16
LENGTH = 1024
STRIP = 32
PAD = 128
WIDE = LENGTH + PAD
FEATS = 8192
TAIL = 16
SHARES = 32
SHARE = FEATS // 4
SEGMENT = 8
SPREAD = 4
PIECES = 8
VMEM_LIMIT = 20 * 1024 * 1024


def call(kernel, name, out_shape, operands, scratch=(), scalars=0, flops=1 << 10, **more):
    spec = pl.BlockSpec(memory_space=pltpu.VMEM)
    in_specs = [pl.BlockSpec(memory_space=pltpu.SMEM)] * scalars
    in_specs += [spec] * (len(operands) - scalars)
    defaults = {"in_specs": in_specs, "out_specs": jax.tree.map(lambda _: spec, out_shape)}
    more = {**defaults, **more}
    placed = [
        x if s.memory_space == pltpu.SMEM else pltpu.with_memory_space_constraint(x, s.memory_space)
        for x, s in zip(operands, more["in_specs"])
    ]
    return pl.pallas_call(
        kernel,
        out_shape=out_shape,
        scratch_shapes=list(scratch),
        compiler_params=pltpu.CompilerParams(vmem_limit_bytes=VMEM_LIMIT),
        cost_estimate=pl.CostEstimate(flops=flops, bytes_accessed=1 << 10, transcendentals=0),
        name=name,
        **more,
    )(*placed)


def lane_groups():
    return lax.broadcasted_iota(jnp.int32, (STRIP, HALF), 1) // (CHANS // GROUPS)


def later(x, count):
    row = lax.broadcasted_iota(jnp.int32, x.shape, 0)
    return jnp.where(row >= count, pltpu.roll(x, count, 0), 0.0)


def strip_of(line):
    wide = jnp.broadcast_to(line, (STRIP, WIDE))
    return pltpu.roll(wide, 0, 1, stride=1, stride_axis=0)[:, :LENGTH].astype(BF16)


def two_windows(signal_ref, n, half):
    lanes = slice(half * HALF, (half + 1) * HALF)
    windows = [signal_ref[m * STRIP : m * STRIP + LENGTH, lanes] for m in (n, n + 1)]
    return jnp.concatenate(windows, axis=1)


def all_strips(strips_ref, signal_ref):
    ids = lane_groups()
    rows = GROUPS * STRIP // 2
    columns = []
    for half in range(2):
        parts = []
        for n in range(0, ROWS // STRIP, 2):
            result = jnp.dot(
                strips_ref[half * rows : (half + 1) * rows, :],
                two_windows(signal_ref, n, half),
                preferred_element_type=F32,
            )
            for m in range(2):
                out = jnp.zeros((STRIP, HALF), F32)
                for g in range(GROUPS // 2):
                    piece = result[g * STRIP : (g + 1) * STRIP, m * HALF : (m + 1) * HALF]
                    out = jnp.where(ids == g, piece, out)
                parts.append(out)
        columns.append(jnp.concatenate(parts, axis=0))
    return jnp.concatenate(columns, axis=1)


def with_tail(tail, block):
    joined = jnp.concatenate([tail.astype(F32), block.astype(F32)], axis=0)
    return joined[TAIL:], pltpu.roll(joined, 1, 0)[TAIL:], pltpu.roll(joined, 2, 0)[TAIL:]


def short_sum(taps_ref, i, parts):
    return sum(taps_ref[i, j : j + 1, :] * parts[j] for j in range(3))


def lines_of(filter_ref, turned):
    if not turned:
        return jnp.concatenate(
            [filter_ref[...].astype(F32), jnp.zeros((GROUPS, PAD), F32)], axis=1
        )
    row = lax.broadcasted_iota(jnp.int32, (CHANS, CHANS), 0)
    col = lax.broadcasted_iota(jnp.int32, (CHANS, CHANS), 1)
    turn = (row + col == CHANS - 1).astype(F32).astype(BF16)
    pieces = [
        jnp.dot(filter_ref[:, n * CHANS : (n + 1) * CHANS], turn, preferred_element_type=F32)
        for n in reversed(range(LENGTH // CHANS))
    ]
    wide = jnp.concatenate([*pieces, jnp.zeros((GROUPS, PAD), F32)], axis=1)
    return pltpu.roll(wide, WIDE - (STRIP - 1), 1)


def pre_kernel(
    cot_ref, weight_ref, lags_ref, d_gated_ref, strips_ref, cot_buffer, weight_buffer, filter_ref,
    sems, lags_sem,
):
    tile = FEATS // PIECES
    lags_copy = pltpu.make_async_copy(lags_ref, filter_ref, lags_sem)
    lags_copy.start()
    copies = []
    for n in range(PIECES):
        piece = slice(n * tile, (n + 1) * tile)
        pair = (
            pltpu.make_async_copy(cot_ref.at[:, piece], cot_buffer.at[n], sems.at[0, n]),
            pltpu.make_async_copy(weight_ref.at[piece, :], weight_buffer.at[n], sems.at[1, n]),
        )
        for copy in pair:
            copy.start()
        copies.append(pair)
    total = jnp.zeros((ROWS, CHANS), F32)
    for n in range(PIECES):
        if n == PIECES // 2:
            lags_copy.wait()
            lines = lines_of(filter_ref, True)
            for g in range(GROUPS):
                strips_ref[g * STRIP : (g + 1) * STRIP, :] = strip_of(lines[g : g + 1])
        for copy in copies[n]:
            copy.wait()
        total += jnp.dot(cot_buffer[n], weight_buffer[n], preferred_element_type=F32)
    d_gated_ref[...] = total.astype(BF16)


def pre_call(*operands):
    tile = FEATS // PIECES
    scratch = [
        pltpu.VMEM((PIECES, ROWS, tile), BF16),
        pltpu.VMEM((PIECES, tile, CHANS), BF16),
        pltpu.VMEM((GROUPS, LENGTH), BF16),
        pltpu.SemaphoreType.DMA((2, PIECES)),
        pltpu.SemaphoreType.DMA,
    ]
    in_specs = [pl.BlockSpec(memory_space=pltpu.HBM)] * 3
    out_shape = [
        pltpu.VMEM((ROWS, CHANS), BF16),
        pltpu.VMEM((GROUPS * STRIP, LENGTH), BF16),
    ]
    return call(pre_kernel, "pre", out_shape, operands, scratch, in_specs=in_specs, flops=1 << 30)


def d_inner_kernel(d_gated_ref, query_ref, tail_ref, taps_ref, out_ref):
    q_short = short_sum(taps_ref, 0, with_tail(tail_ref[...], query_ref[...]))
    out_ref[...] = (d_gated_ref[...].astype(F32) * q_short).astype(BF16)


def d_inner_call(*operands):
    return call(d_inner_kernel, "d_inner", pltpu.VMEM((ROWS, CHANS), BF16), operands)


def fwd_kernel(
    core_ref, strips_ref, pair_ref, cross_ref, cross_pair_ref, key_ref, value_ref, query_ref,
    tail_ref, taps_ref, skip_ref,
    gated_ref, inner_ref, signal_ref,
):
    upper = core_ref[0] == 1
    pair = pair_ref[...].astype(F32)
    cross_pair = cross_pair_ref[...].astype(F32)
    near = jnp.where(upper, pair, cross_pair)
    far = jnp.where(upper, cross_pair, 0.0)
    own = jnp.concatenate([key_ref[...], value_ref[...]], axis=1).astype(F32)
    both = jnp.concatenate([far, cross_ref[...].astype(F32), near, own], axis=0)
    shifted = (both, later(both, 1), later(both, 2))
    k_short = short_sum(taps_ref, 1, [part[:, :CHANS] for part in shifted])
    v_short = short_sum(taps_ref, 2, [part[:, CHANS:] for part in shifted])
    mixed = (k_short * v_short).astype(BF16)
    signal_ref[: ROWS - STRIP, :] = jnp.zeros((ROWS - STRIP, CHANS), BF16)
    signal_ref[ROWS - STRIP :, :] = mixed
    inner = all_strips(strips_ref, signal_ref) + skip_ref[...] * mixed[LENGTH - ROWS :].astype(F32)
    inner_ref[...] = inner
    q_short = short_sum(taps_ref, 0, with_tail(tail_ref[...], query_ref[...]))
    gated_ref[...] = (q_short * inner).astype(BF16)


def fwd_call(*operands):
    out_shape = [
        pltpu.VMEM((ROWS, CHANS), BF16),
        pltpu.VMEM((ROWS, CHANS), F32),
        pltpu.VMEM((LENGTH + ROWS - STRIP, CHANS), BF16),
    ]
    return call(fwd_kernel, "fwd", out_shape, operands, (), 1, 4 << 30)


def terms_kernel(core_ref, own_cot_ref, other_cot_ref, gated_ref, other_gated_ref, out_ref):
    dims = (((0,), (0,)), ((), ()))
    for half in range(2):
        start = pl.multiple_of((2 * half + core_ref[0]) * SHARE, SHARE)
        own_cot = own_cot_ref[:, pl.ds(start, SHARE)]
        total = lax.dot_general(gated_ref[...], own_cot, dims, preferred_element_type=F32)
        total += lax.dot_general(other_gated_ref[...], other_cot_ref[half], dims, preferred_element_type=F32)
        out_ref[half, :, :SHARE] = total.astype(BF16)


def terms_call(*operands):
    out_shape = pltpu.VMEM((2, CHANS, SHARE + HALF), BF16)
    return call(terms_kernel, "terms", out_shape, operands, scalars=1, flops=1 << 30)


def add_small_kernel(terms_ref, small_ref, other_small_ref, out_ref, parts_ref, sems):
    total = small_ref[...] + other_small_ref[...]
    parts_ref[...] = total.reshape(CHANS, HALF).astype(BF16)
    copies = [
        pltpu.make_async_copy(parts_ref, out_ref.at[half, :, pl.ds(SHARE, HALF)], sems.at[half])
        for half in range(2)
    ]
    for copy in copies:
        copy.start()
    for copy in copies:
        copy.wait()


def add_small_call(*operands):
    place = pl.BlockSpec(memory_space=pl.ANY)
    spec = pl.BlockSpec(memory_space=pltpu.VMEM)
    return pl.pallas_call(
        add_small_kernel,
        in_specs=[place, spec, spec],
        out_specs=place,
        out_shape=jax.ShapeDtypeStruct(operands[0].shape, BF16),
        scratch_shapes=[pltpu.VMEM((CHANS, HALF), BF16), pltpu.SemaphoreType.DMA((2,))],
        input_output_aliases={0: 0},
        compiler_params=pltpu.CompilerParams(vmem_limit_bytes=VMEM_LIMIT),
        name="add_small",
    )(
        operands[0],
        *(pltpu.with_memory_space_constraint(x, pltpu.VMEM) for x in operands[1:]),
    )


def place(row):
    return row % SHARES, row // SHARES


def tap_place(n, half):
    return place(GROUPS * LENGTH // HALF + 2 * n + half)


def turn_matrix(size, block):
    row = lax.broadcasted_iota(jnp.int32, (size, size), 0)
    col = lax.broadcasted_iota(jnp.int32, (size, size), 1)
    return ((row // block) * block + (block - 1 - row % block) == col).astype(F32)


def lag_kernel(
    core_ref, cot_ref, d_inner_ref, signal_ref,
    filter_ref, part_ref,
    outer_ref, stack_ref, sums_ref, sems,
):
    copies = []
    for half in range(2):
        start = pl.multiple_of((2 * half + core_ref[0]) * SHARE, SHARE)
        copies.append(
            pltpu.make_async_copy(
                cot_ref.at[:, pl.ds(start, SHARE)], part_ref.at[half], sems.at[half]
            )
        )
        copies[-1].start()
    turn = turn_matrix(ROWS, STRIP).astype(BF16)
    turned = jnp.dot(turn, d_inner_ref[...], preferred_element_type=F32)
    ids = lane_groups()
    count = GROUPS * STRIP // 2
    outer_ref[:, LENGTH:] = jnp.zeros((GROUPS * STRIP, PAD), F32)
    for half in range(2):
        rows = slice(half * count, (half + 1) * count)
        for n in range(0, ROWS // STRIP, 2):
            for m in range(2):
                start = (n + m) * STRIP
                piece = turned[start : start + STRIP, half * HALF : (half + 1) * HALF]
                for g in range(GROUPS // 2):
                    stack_ref[g * STRIP : (g + 1) * STRIP, m * HALF : (m + 1) * HALF] = jnp.where(
                        ids == g, piece, 0.0
                    ).astype(BF16)
            term = lax.dot_general(
                stack_ref[...],
                two_windows(signal_ref, n, half),
                (((1,), (1,)), ((), ())),
                preferred_element_type=F32,
            )
            if n == 0:
                outer_ref[rows, :LENGTH] = term
            else:
                outer_ref[rows, :LENGTH] += term
    for g in range(GROUPS):
        rows = outer_ref[g * STRIP : (g + 1) * STRIP, :]
        skewed = pltpu.roll(rows, WIDE - (STRIP - 1), 1, stride=1, stride_axis=0)
        sums_ref[g : g + 1, :] = jnp.sum(skewed, axis=0, keepdims=True)
    sums = pltpu.roll(sums_ref[...], STRIP - 1, 1)
    turn = turn_matrix(CHANS, CHANS)
    last = LENGTH // CHANS - 1
    for n in range(LENGTH // CHANS):
        filter_ref[:, n * CHANS : (n + 1) * CHANS] = jnp.dot(
            sums[:, (last - n) * CHANS : (last - n + 1) * CHANS],
            turn,
            precision=lax.Precision.HIGHEST,
            preferred_element_type=F32,
        )
    for copy in copies:
        copy.wait()


def lag_call(*operands):
    scratch = [
        pltpu.VMEM((GROUPS * STRIP, WIDE), F32),
        pltpu.VMEM((GROUPS * STRIP // 2, CHANS), BF16),
        pltpu.VMEM((GROUPS, WIDE), F32),
        pltpu.SemaphoreType.DMA((2,)),
    ]
    out_shape = [pltpu.VMEM((GROUPS, LENGTH), F32), pltpu.VMEM((2, ROWS, SHARE), BF16)]
    in_specs = [pl.BlockSpec(memory_space=pltpu.SMEM), pl.BlockSpec(memory_space=pltpu.HBM)]
    in_specs += [pl.BlockSpec(memory_space=pltpu.VMEM)] * 2
    return call(lag_kernel, "lag_sums", out_shape, operands, scratch, in_specs=in_specs)


def bwd_kernel(
    core_ref, d0_ref, d_pair_ref, d_cross_ref, d_cross_pair_ref, lags_ref, filter_ref, signal_ref, key_ref, value_ref,
    pair_ref, cross_pair_ref, query_ref, tail_ref, inner_ref, d_gated_ref, taps_ref, skip_ref,
    d_short_ref, head_ref, small_ref,
    strips_ref, ahead_ref,
):
    upper = core_ref[0] == 1
    d_pair = d_pair_ref[...].astype(F32)
    d_cross_pair = d_cross_pair_ref[...].astype(F32)
    later_blocks = (
        d0_ref[...],
        jnp.where(upper, d_cross_pair, d_pair).astype(BF16),
        d_cross_ref[...],
        jnp.where(upper, 0.0, d_cross_pair).astype(BF16),
    )
    for n, block in enumerate(later_blocks):
        ahead_ref[n * ROWS : (n + 1) * ROWS, :] = block
    ahead_ref[LENGTH:, :] = jnp.zeros((ROWS, CHANS), BF16)
    lines = lines_of(lags_ref, False)
    for g in range(GROUPS):
        strips_ref[g * STRIP : (g + 1) * STRIP, :] = strip_of(lines[g : g + 1])
    d_inner = d0_ref[...].astype(F32)
    mixed = signal_ref[LENGTH - STRIP :, :]
    d_mixed = all_strips(strips_ref, ahead_ref) + skip_ref[...] * d_inner

    last = slice(ROWS - TAIL, ROWS)
    near = jnp.where(upper, pair_ref[last, :].astype(F32), cross_pair_ref[last, :].astype(F32))
    k_parts = with_tail(near[:, :CHANS], key_ref[...])
    v_parts = with_tail(near[:, CHANS:], value_ref[...])
    q_parts = with_tail(tail_ref[...], query_ref[...])
    small_ref[...] = jnp.zeros_like(small_ref)
    sums = []
    d_qs = d_gated_ref[...].astype(F32) * inner_ref[...]
    d_ks = d_mixed * short_sum(taps_ref, 2, v_parts)
    d_vs = d_mixed * short_sum(taps_ref, 1, k_parts)
    for i, (grad, parts) in enumerate(((d_qs, q_parts), (d_ks, k_parts), (d_vs, v_parts))):
        d_short_ref[i] = grad
        head_ref[i] = grad[:8]
        for j in range(3):
            sums.append(jnp.sum(grad * parts[j], axis=0, keepdims=True))
    sums.append(jnp.sum(d_inner * mixed.astype(F32), axis=0, keepdims=True))
    for n, row in enumerate(sums):
        for half in range(2):
            share, slot = tap_place(n, half)
            small_ref[share, slot : slot + 1, :] = row[:, half * HALF : (half + 1) * HALF]

    for g in range(GROUPS):
        for n in range(LENGTH // HALF):
            share, slot = place(g * (LENGTH // HALF) + n)
            small_ref[share, slot : slot + 1, :] = filter_ref[g : g + 1, n * HALF : (n + 1) * HALF]


def bwd_call(*operands):
    out_shape = [
        pltpu.VMEM((3, ROWS, CHANS), F32),
        pltpu.VMEM((3, 8, CHANS), F32),
        pltpu.VMEM((SHARES, SEGMENT, HALF), F32),
    ]
    scratch = [
        pltpu.VMEM((GROUPS * STRIP, LENGTH), BF16),
        pltpu.VMEM((LENGTH + ROWS, CHANS), BF16),
    ]
    return call(bwd_kernel, "bwd", out_shape, operands, scratch, 1)


def input_grads(d_short_ref, next_ref, taps_ref, out_refs):
    for i, out_ref in enumerate(out_refs):
        joined = jnp.concatenate([d_short_ref[i], next_ref[i]], axis=0)
        rows = joined.shape[0]
        parts = (
            joined[:ROWS],
            pltpu.roll(joined, rows - 1, 0)[:ROWS],
            pltpu.roll(joined, rows - 2, 0)[:ROWS],
        )
        out_ref[...] = short_sum(taps_ref, i, parts).astype(BF16)


def total_kernel(scale, terms_ref, out_ref):
    total = (jnp.sum(terms_ref[...].astype(F32), axis=0) * scale).astype(BF16)
    out_ref[...] = jnp.broadcast_to(total[None], out_ref.shape)


def total_call(terms, scale):
    out_shape = pltpu.VMEM((SHARES, *terms.shape[1:]), BF16)
    return call(lambda *refs: total_kernel(scale, *refs), "total", out_shape, (terms,))


def spread_kernel(
    shares_ref, d_short_ref, next_ref, short_taps_ref,
    weight_ref, taps_ref, filter_ref, skip_ref, query_ref, key_ref, value_ref,
    turned_ref, sems,
):
    tile = SHARE // SPREAD
    copies = []
    for n in range(SPREAD):
        piece = slice(n * tile, (n + 1) * tile)
        turned_ref[piece, :] = shares_ref[:, piece].astype(F32).T
        copies.append(
            pltpu.make_async_copy(turned_ref.at[piece, :], weight_ref.at[piece, :], sems.at[n])
        )
        copies[-1].start()
    input_grads(d_short_ref, next_ref, short_taps_ref, (query_ref, key_ref, value_ref))
    small = shares_ref[:, SHARE:].astype(F32)

    def part(share, slot):
        return small[share * SEGMENT + slot : share * SEGMENT + slot + 1]

    for g in range(GROUPS):
        for n in range(LENGTH // HALF):
            piece = part(*place(g * (LENGTH // HALF) + n))
            filter_ref[g : g + 1, n * HALF : (n + 1) * HALF] = piece
    for half in range(2):
        lanes = slice(half * HALF, (half + 1) * HALF)
        for n in range(9):
            taps_ref[n // 3, n % 3 : n % 3 + 1, lanes] = part(*tap_place(n, half))
        skip_ref[:, lanes] = part(*tap_place(9, half))
    for copy in copies:
        copy.wait()


def spread_call(shares, *operands):
    out_shape = [
        jax.ShapeDtypeStruct((SHARE, CHANS), F32),
        jax.ShapeDtypeStruct((3, 3, CHANS), F32),
        jax.ShapeDtypeStruct((GROUPS, LENGTH), F32),
        jax.ShapeDtypeStruct((1, CHANS), F32),
        *[jax.ShapeDtypeStruct((ROWS, CHANS), BF16)] * 3,
    ]
    scratch = [pltpu.VMEM((SHARE, CHANS), F32), pltpu.SemaphoreType.DMA((SPREAD,))]
    out_specs = [pl.BlockSpec(memory_space=pl.ANY)]
    out_specs += [pl.BlockSpec(memory_space=pltpu.VMEM)] * 6
    shares = shares.reshape(CHANS, SHARE + HALF)
    operands = (shares, *operands)
    return call(spread_kernel, "spread", out_shape, operands, scratch, out_specs=out_specs)


def sent(block, distance):
    count = 4
    route = [(i, i + distance) for i in range(count) if 0 <= i + distance < count]
    return lax.ppermute(block, CTX, route)


def shards(
    query_in, key_in, value_in, short_taps, long_filter, skip_gain, out_weight, out_cotangent
):
    query = query_in[0]
    cot = out_cotangent[0]
    taps = short_taps
    skip = skip_gain.reshape(1, CHANS)
    devices = lax.axis_size(ALL)
    tokens = ROWS * devices
    scale = 1.0 / math.sqrt(tokens)
    core = lax.axis_index("co").astype(jnp.int32).reshape(1)

    key = key_in[0]
    value = value_in[0]
    swap = [(0, 1), (1, 0)]
    own = jnp.concatenate([key, value], axis=1)
    tail = sent(query[ROWS - TAIL :], 1)
    cross = lax.ppermute(own, "xh", [(0, 1)])
    pair = lax.ppermute(own, "co", swap)
    other_cot = lax.ppermute(cot, "co", swap)

    d_gated, strips = pre_call(cot, out_weight, long_filter)
    cross, tail, d_gated = lax.optimization_barrier((cross, tail, d_gated))
    cross_pair = lax.ppermute(cross, "co", swap)
    d_inner = d_inner_call(d_gated, query, tail, taps)
    d_cross = lax.ppermute(d_inner, "xh", [(1, 0)])
    d_pair = lax.ppermute(d_inner, "co", swap)
    gated, inner, signal = fwd_call(
        core, strips, pair, cross, cross_pair, key, value, query, tail, taps, skip
    )
    other_gated = lax.ppermute(gated, "co", swap)
    d_cross, signal = lax.optimization_barrier((d_cross, signal))
    d_cross_pair = lax.ppermute(d_cross, "co", swap)
    lag_sums, other_part = lag_call(core, other_cot, d_inner, signal)
    d_short, head, small = bwd_call(
        core, d_inner, d_pair, d_cross, d_cross_pair, long_filter, lag_sums, signal, key, value, pair, cross_pair, query, tail,
        inner, d_gated, taps, skip,
    )
    other_gated, head, small = lax.optimization_barrier((other_gated, head, small))
    other_small = lax.ppermute(small, "co", swap)
    terms = terms_call(core, cot, other_part, gated, other_gated)
    terms, other_small = lax.optimization_barrier((terms, other_small))
    terms = add_small_call(terms, small, other_small)
    terms, head = lax.optimization_barrier((terms, head))
    terms = terms.reshape(2 * SHARES, CHANS // SHARES, SHARE + HALF)
    terms = lax.all_to_all(terms, CHIPS, 0, 0)
    following = sent(head, -1)

    shares = lax.all_to_all(total_call(terms, scale), DP, 0, 0)
    grad_weight, grad_taps, grad_filter, grad_skip, *input_grad = spread_call(
        shares, d_short, following, taps
    )
    return (
        gated[None],
        *(grad[None] for grad in input_grad),
        grad_taps,
        grad_filter,
        grad_skip.reshape(CHANS),
        grad_weight,
    )


def solution(mesh):
    fine = Mesh(mesh.devices.reshape(2, 2, 4, 2, 4), ALL)
    tokens = P(DP, CTX, None)
    in_specs = (tokens, tokens, tokens, P(), P(), P(), P(), tokens)
    out_specs = (tokens, tokens, tokens, tokens, P(), P(), P(), P(CTX, None))
    return jax.shard_map(
        shards, mesh=fine, in_specs=in_specs, out_specs=out_specs, check_vma=False
    )
```

```python
import math

import jax
import jax.numpy as jnp
from jax import lax
from jax.experimental import pallas as pl
from jax.experimental.pallas import tpu as pltpu
from jax.sharding import Mesh
from jax.sharding import PartitionSpec as P

F32 = jnp.float32
BF16 = jnp.bfloat16
CTX = ("xh", "co")
DP = ("y", "xl", "z")
CHIPS = ("xh", "y", "xl", "z")
ALL = ("xh", "co", "y", "xl", "z")

ROWS = 256
CHANS = 256
HALF = CHANS // 2
GROUPS = 16
LENGTH = 1024
STRIP = 32
PAD = 128
WIDE = LENGTH + PAD
FEATS = 8192
TAIL = 16
SHARES = 32
SHARE = FEATS // 4
SEGMENT = 8
SPREAD = 4
PIECES = 8
VMEM_LIMIT = 20 * 1024 * 1024


def call(kernel, name, out_shape, operands, scratch=(), scalars=0, flops=1 << 10, **more):
    spec = pl.BlockSpec(memory_space=pltpu.VMEM)
    in_specs = [pl.BlockSpec(memory_space=pltpu.SMEM)] * scalars
    in_specs += [spec] * (len(operands) - scalars)
    defaults = {"in_specs": in_specs, "out_specs": jax.tree.map(lambda _: spec, out_shape)}
    more = {**defaults, **more}
    placed = [
        x if s.memory_space == pltpu.SMEM else pltpu.with_memory_space_constraint(x, s.memory_space)
        for x, s in zip(operands, more["in_specs"])
    ]
    return pl.pallas_call(
        kernel,
        out_shape=out_shape,
        scratch_shapes=list(scratch),
        compiler_params=pltpu.CompilerParams(vmem_limit_bytes=VMEM_LIMIT),
        cost_estimate=pl.CostEstimate(flops=flops, bytes_accessed=1 << 10, transcendentals=0),
        name=name,
        **more,
    )(*placed)


def lane_groups():
    return lax.broadcasted_iota(jnp.int32, (STRIP, HALF), 1) // (CHANS // GROUPS)


def later(x, count):
    row = lax.broadcasted_iota(jnp.int32, x.shape, 0)
    return jnp.where(row >= count, pltpu.roll(x, count, 0), 0.0)


def strip_of(line):
    wide = jnp.broadcast_to(line, (STRIP, WIDE))
    return pltpu.roll(wide, 0, 1, stride=1, stride_axis=0)[:, :LENGTH].astype(BF16)


def two_windows(signal_ref, n, half):
    lanes = slice(half * HALF, (half + 1) * HALF)
    windows = [signal_ref[m * STRIP : m * STRIP + LENGTH, lanes] for m in (n, n + 1)]
    return jnp.concatenate(windows, axis=1)


def all_strips(strips_ref, signal_ref):
    ids = lane_groups()
    rows = GROUPS * STRIP // 2
    columns = []
    for half in range(2):
        parts = []
        for n in range(0, ROWS // STRIP, 2):
            result = jnp.dot(
                strips_ref[half * rows : (half + 1) * rows, :],
                two_windows(signal_ref, n, half),
                preferred_element_type=F32,
            )
            for m in range(2):
                out = jnp.zeros((STRIP, HALF), F32)
                for g in range(GROUPS // 2):
                    piece = result[g * STRIP : (g + 1) * STRIP, m * HALF : (m + 1) * HALF]
                    out = jnp.where(ids == g, piece, out)
                parts.append(out)
        columns.append(jnp.concatenate(parts, axis=0))
    return jnp.concatenate(columns, axis=1)


def with_tail(tail, block):
    joined = jnp.concatenate([tail.astype(F32), block.astype(F32)], axis=0)
    return joined[TAIL:], pltpu.roll(joined, 1, 0)[TAIL:], pltpu.roll(joined, 2, 0)[TAIL:]


def short_sum(taps_ref, i, parts):
    return sum(taps_ref[i, j : j + 1, :] * parts[j] for j in range(3))


def lines_of(filter_ref, turned):
    if not turned:
        return jnp.concatenate(
            [filter_ref[...].astype(F32), jnp.zeros((GROUPS, PAD), F32)], axis=1
        )
    row = lax.broadcasted_iota(jnp.int32, (CHANS, CHANS), 0)
    col = lax.broadcasted_iota(jnp.int32, (CHANS, CHANS), 1)
    turn = (row + col == CHANS - 1).astype(F32).astype(BF16)
    pieces = [
        jnp.dot(filter_ref[:, n * CHANS : (n + 1) * CHANS], turn, preferred_element_type=F32)
        for n in reversed(range(LENGTH // CHANS))
    ]
    wide = jnp.concatenate([*pieces, jnp.zeros((GROUPS, PAD), F32)], axis=1)
    return pltpu.roll(wide, WIDE - (STRIP - 1), 1)


def pre_kernel(
    cot_ref, weight_ref, lags_ref, d_gated_ref, strips_ref, cot_buffer, weight_buffer, filter_ref,
    sems, lags_sem,
):
    tile = FEATS // PIECES
    lags_copy = pltpu.make_async_copy(lags_ref, filter_ref, lags_sem)
    lags_copy.start()
    copies = []
    for n in range(PIECES):
        piece = slice(n * tile, (n + 1) * tile)
        pair = (
            pltpu.make_async_copy(cot_ref.at[:, piece], cot_buffer.at[n], sems.at[0, n]),
            pltpu.make_async_copy(weight_ref.at[piece, :], weight_buffer.at[n], sems.at[1, n]),
        )
        for copy in pair:
            copy.start()
        copies.append(pair)
    total = jnp.zeros((ROWS, CHANS), F32)
    for n in range(PIECES):
        if n == PIECES // 2:
            lags_copy.wait()
            lines = lines_of(filter_ref, True)
            for g in range(GROUPS):
                strips_ref[g * STRIP : (g + 1) * STRIP, :] = strip_of(lines[g : g + 1])
        for copy in copies[n]:
            copy.wait()
        total += jnp.dot(cot_buffer[n], weight_buffer[n], preferred_element_type=F32)
    d_gated_ref[...] = total.astype(BF16)


def pre_call(*operands):
    tile = FEATS // PIECES
    scratch = [
        pltpu.VMEM((PIECES, ROWS, tile), BF16),
        pltpu.VMEM((PIECES, tile, CHANS), BF16),
        pltpu.VMEM((GROUPS, LENGTH), BF16),
        pltpu.SemaphoreType.DMA((2, PIECES)),
        pltpu.SemaphoreType.DMA,
    ]
    in_specs = [pl.BlockSpec(memory_space=pltpu.HBM)] * 3
    out_shape = [
        pltpu.VMEM((ROWS, CHANS), BF16),
        pltpu.VMEM((GROUPS * STRIP, LENGTH), BF16),
    ]
    return call(pre_kernel, "pre", out_shape, operands, scratch, in_specs=in_specs, flops=1 << 30)


def d_inner_kernel(d_gated_ref, query_ref, tail_ref, taps_ref, out_ref):
    q_short = short_sum(taps_ref, 0, with_tail(tail_ref[...], query_ref[...]))
    out_ref[...] = (d_gated_ref[...].astype(F32) * q_short).astype(BF16)


def d_inner_call(*operands):
    return call(d_inner_kernel, "d_inner", pltpu.VMEM((ROWS, CHANS), BF16), operands)


def fwd_kernel(
    core_ref, strips_ref, pair_ref, cross_ref, cross_pair_ref, key_ref, value_ref, query_ref,
    tail_ref, taps_ref, skip_ref,
    gated_ref, inner_ref, signal_ref,
):
    upper = core_ref[0] == 1
    pair = pair_ref[...].astype(F32)
    cross_pair = cross_pair_ref[...].astype(F32)
    near = jnp.where(upper, pair, cross_pair)
    far = jnp.where(upper, cross_pair, 0.0)
    own = jnp.concatenate([key_ref[...], value_ref[...]], axis=1).astype(F32)
    both = jnp.concatenate([far, cross_ref[...].astype(F32), near, own], axis=0)
    shifted = (both, later(both, 1), later(both, 2))
    k_short = short_sum(taps_ref, 1, [part[:, :CHANS] for part in shifted])
    v_short = short_sum(taps_ref, 2, [part[:, CHANS:] for part in shifted])
    mixed = (k_short * v_short).astype(BF16)
    signal_ref[: ROWS - STRIP, :] = jnp.zeros((ROWS - STRIP, CHANS), BF16)
    signal_ref[ROWS - STRIP :, :] = mixed
    inner = all_strips(strips_ref, signal_ref) + skip_ref[...] * mixed[LENGTH - ROWS :].astype(F32)
    inner_ref[...] = inner
    q_short = short_sum(taps_ref, 0, with_tail(tail_ref[...], query_ref[...]))
    gated_ref[...] = (q_short * inner).astype(BF16)


def fwd_call(*operands):
    out_shape = [
        pltpu.VMEM((ROWS, CHANS), BF16),
        pltpu.VMEM((ROWS, CHANS), F32),
        pltpu.VMEM((LENGTH + ROWS - STRIP, CHANS), BF16),
    ]
    return call(fwd_kernel, "fwd", out_shape, operands, (), 1, 4 << 30)


def terms_kernel(core_ref, own_cot_ref, other_cot_ref, gated_ref, other_gated_ref, out_ref):
    dims = (((0,), (0,)), ((), ()))
    for half in range(2):
        start = pl.multiple_of((2 * half + core_ref[0]) * SHARE, SHARE)
        own_cot = own_cot_ref[:, pl.ds(start, SHARE)]
        total = lax.dot_general(gated_ref[...], own_cot, dims, preferred_element_type=F32)
        total += lax.dot_general(other_gated_ref[...], other_cot_ref[half], dims, preferred_element_type=F32)
        out_ref[half, :, :SHARE] = total.astype(BF16)


def terms_call(*operands):
    out_shape = pltpu.VMEM((2, CHANS, SHARE + HALF), BF16)
    return call(terms_kernel, "terms", out_shape, operands, scalars=1, flops=1 << 30)


def add_small_kernel(terms_ref, small_ref, other_small_ref, out_ref, parts_ref, sems):
    total = small_ref[...] + other_small_ref[...]
    parts_ref[...] = total.reshape(CHANS, HALF).astype(BF16)
    copies = [
        pltpu.make_async_copy(parts_ref, out_ref.at[half, :, pl.ds(SHARE, HALF)], sems.at[half])
        for half in range(2)
    ]
    for copy in copies:
        copy.start()
    for copy in copies:
        copy.wait()


def add_small_call(*operands):
    place = pl.BlockSpec(memory_space=pl.ANY)
    spec = pl.BlockSpec(memory_space=pltpu.VMEM)
    return pl.pallas_call(
        add_small_kernel,
        in_specs=[place, spec, spec],
        out_specs=place,
        out_shape=jax.ShapeDtypeStruct(operands[0].shape, BF16),
        scratch_shapes=[pltpu.VMEM((CHANS, HALF), BF16), pltpu.SemaphoreType.DMA((2,))],
        input_output_aliases={0: 0},
        compiler_params=pltpu.CompilerParams(vmem_limit_bytes=VMEM_LIMIT),
        name="add_small",
    )(
        operands[0],
        *(pltpu.with_memory_space_constraint(x, pltpu.VMEM) for x in operands[1:]),
    )


def place(row):
    return row % SHARES, row // SHARES


def tap_place(n, half):
    return place(GROUPS * LENGTH // HALF + 2 * n + half)


def turn_matrix(size, block):
    row = lax.broadcasted_iota(jnp.int32, (size, size), 0)
    col = lax.broadcasted_iota(jnp.int32, (size, size), 1)
    return ((row // block) * block + (block - 1 - row % block) == col).astype(F32)


def lag_kernel(
    core_ref, cot_ref, d_inner_ref, signal_ref,
    filter_ref, part_ref,
    outer_ref, stack_ref, sums_ref, sems,
):
    copies = []
    for half in range(2):
        start = pl.multiple_of((2 * half + core_ref[0]) * SHARE, SHARE)
        copies.append(
            pltpu.make_async_copy(
                cot_ref.at[:, pl.ds(start, SHARE)], part_ref.at[half], sems.at[half]
            )
        )
        copies[-1].start()
    turn = turn_matrix(ROWS, STRIP).astype(BF16)
    turned = jnp.dot(turn, d_inner_ref[...], preferred_element_type=F32)
    ids = lane_groups()
    count = GROUPS * STRIP // 2
    outer_ref[:, LENGTH:] = jnp.zeros((GROUPS * STRIP, PAD), F32)
    for half in range(2):
        rows = slice(half * count, (half + 1) * count)
        for n in range(0, ROWS // STRIP, 2):
            for m in range(2):
                start = (n + m) * STRIP
                piece = turned[start : start + STRIP, half * HALF : (half + 1) * HALF]
                for g in range(GROUPS // 2):
                    stack_ref[g * STRIP : (g + 1) * STRIP, m * HALF : (m + 1) * HALF] = jnp.where(
                        ids == g, piece, 0.0
                    ).astype(BF16)
            term = lax.dot_general(
                stack_ref[...],
                two_windows(signal_ref, n, half),
                (((1,), (1,)), ((), ())),
                preferred_element_type=F32,
            )
            if n == 0:
                outer_ref[rows, :LENGTH] = term
            else:
                outer_ref[rows, :LENGTH] += term
    for g in range(GROUPS):
        rows = outer_ref[g * STRIP : (g + 1) * STRIP, :]
        skewed = pltpu.roll(rows, WIDE - (STRIP - 1), 1, stride=1, stride_axis=0)
        sums_ref[g : g + 1, :] = jnp.sum(skewed, axis=0, keepdims=True)
    sums = pltpu.roll(sums_ref[...], STRIP - 1, 1)
    turn = turn_matrix(CHANS, CHANS)
    last = LENGTH // CHANS - 1
    for n in range(LENGTH // CHANS):
        filter_ref[:, n * CHANS : (n + 1) * CHANS] = jnp.dot(
            sums[:, (last - n) * CHANS : (last - n + 1) * CHANS],
            turn,
            precision=lax.Precision.HIGHEST,
            preferred_element_type=F32,
        )
    for copy in copies:
        copy.wait()


def lag_call(*operands):
    scratch = [
        pltpu.VMEM((GROUPS * STRIP, WIDE), F32),
        pltpu.VMEM((GROUPS * STRIP // 2, CHANS), BF16),
        pltpu.VMEM((GROUPS, WIDE), F32),
        pltpu.SemaphoreType.DMA((2,)),
    ]
    out_shape = [pltpu.VMEM((GROUPS, LENGTH), F32), pltpu.VMEM((2, ROWS, SHARE), BF16)]
    in_specs = [pl.BlockSpec(memory_space=pltpu.SMEM), pl.BlockSpec(memory_space=pltpu.HBM)]
    in_specs += [pl.BlockSpec(memory_space=pltpu.VMEM)] * 2
    return call(lag_kernel, "lag_sums", out_shape, operands, scratch, in_specs=in_specs)


def bwd_kernel(
    core_ref, d0_ref, d_pair_ref, d_cross_ref, d_cross_pair_ref, lags_ref, filter_ref, signal_ref, key_ref, value_ref,
    pair_ref, cross_pair_ref, query_ref, tail_ref, inner_ref, d_gated_ref, taps_ref, skip_ref,
    d_short_ref, head_ref, small_ref,
    strips_ref, ahead_ref,
):
    upper = core_ref[0] == 1
    d_pair = d_pair_ref[...].astype(F32)
    d_cross_pair = d_cross_pair_ref[...].astype(F32)
    later_blocks = (
        d0_ref[...],
        jnp.where(upper, d_cross_pair, d_pair).astype(BF16),
        d_cross_ref[...],
        jnp.where(upper, 0.0, d_cross_pair).astype(BF16),
    )
    for n, block in enumerate(later_blocks):
        ahead_ref[n * ROWS : (n + 1) * ROWS, :] = block
    ahead_ref[LENGTH:, :] = jnp.zeros((ROWS, CHANS), BF16)
    lines = lines_of(lags_ref, False)
    for g in range(GROUPS):
        strips_ref[g * STRIP : (g + 1) * STRIP, :] = strip_of(lines[g : g + 1])
    d_inner = d0_ref[...].astype(F32)
    mixed = signal_ref[LENGTH - STRIP :, :]
    d_mixed = all_strips(strips_ref, ahead_ref) + skip_ref[...] * d_inner

    last = slice(ROWS - TAIL, ROWS)
    near = jnp.where(upper, pair_ref[last, :].astype(F32), cross_pair_ref[last, :].astype(F32))
    k_parts = with_tail(near[:, :CHANS], key_ref[...])
    v_parts = with_tail(near[:, CHANS:], value_ref[...])
    q_parts = with_tail(tail_ref[...], query_ref[...])
    small_ref[...] = jnp.zeros_like(small_ref)
    sums = []
    d_qs = d_gated_ref[...].astype(F32) * inner_ref[...]
    d_ks = d_mixed * short_sum(taps_ref, 2, v_parts)
    d_vs = d_mixed * short_sum(taps_ref, 1, k_parts)
    for i, (grad, parts) in enumerate(((d_qs, q_parts), (d_ks, k_parts), (d_vs, v_parts))):
        d_short_ref[i] = grad
        head_ref[i] = grad[:8]
        for j in range(3):
            sums.append(jnp.sum(grad * parts[j], axis=0, keepdims=True))
    sums.append(jnp.sum(d_inner * mixed.astype(F32), axis=0, keepdims=True))
    for n, row in enumerate(sums):
        for half in range(2):
            share, slot = tap_place(n, half)
            small_ref[share, slot : slot + 1, :] = row[:, half * HALF : (half + 1) * HALF]

    for g in range(GROUPS):
        for n in range(LENGTH // HALF):
            share, slot = place(g * (LENGTH // HALF) + n)
            small_ref[share, slot : slot + 1, :] = filter_ref[g : g + 1, n * HALF : (n + 1) * HALF]


def bwd_call(*operands):
    out_shape = [
        pltpu.VMEM((3, ROWS, CHANS), F32),
        pltpu.VMEM((3, 8, CHANS), F32),
        pltpu.VMEM((SHARES, SEGMENT, HALF), F32),
    ]
    scratch = [
        pltpu.VMEM((GROUPS * STRIP, LENGTH), BF16),
        pltpu.VMEM((LENGTH + ROWS, CHANS), BF16),
    ]
    return call(bwd_kernel, "bwd", out_shape, operands, scratch, 1)


def input_grads(d_short_ref, next_ref, taps_ref, out_refs):
    for i, out_ref in enumerate(out_refs):
        joined = jnp.concatenate([d_short_ref[i], next_ref[i]], axis=0)
        rows = joined.shape[0]
        parts = (
            joined[:ROWS],
            pltpu.roll(joined, rows - 1, 0)[:ROWS],
            pltpu.roll(joined, rows - 2, 0)[:ROWS],
        )
        out_ref[...] = short_sum(taps_ref, i, parts).astype(BF16)


def total_kernel(scale, terms_ref, out_ref):
    total = (jnp.sum(terms_ref[...].astype(F32), axis=0) * scale).astype(BF16)
    out_ref[...] = jnp.broadcast_to(total[None], out_ref.shape)


def total_call(terms, scale):
    out_shape = pltpu.VMEM((SHARES, *terms.shape[1:]), BF16)
    return call(lambda *refs: total_kernel(scale, *refs), "total", out_shape, (terms,))


def spread_kernel(
    shares_ref, d_short_ref, next_ref, short_taps_ref,
    weight_ref, taps_ref, filter_ref, skip_ref, query_ref, key_ref, value_ref,
    turned_ref, sems,
):
    tile = SHARE // SPREAD
    copies = []
    for n in range(SPREAD):
        piece = slice(n * tile, (n + 1) * tile)
        turned_ref[piece, :] = shares_ref[:, piece].astype(F32).T
        copies.append(
            pltpu.make_async_copy(turned_ref.at[piece, :], weight_ref.at[piece, :], sems.at[n])
        )
        copies[-1].start()
    input_grads(d_short_ref, next_ref, short_taps_ref, (query_ref, key_ref, value_ref))
    small = shares_ref[:, SHARE:].astype(F32)

    def part(share, slot):
        return small[share * SEGMENT + slot : share * SEGMENT + slot + 1]

    for g in range(GROUPS):
        for n in range(LENGTH // HALF):
            piece = part(*place(g * (LENGTH // HALF) + n))
            filter_ref[g : g + 1, n * HALF : (n + 1) * HALF] = piece
    for half in range(2):
        lanes = slice(half * HALF, (half + 1) * HALF)
        for n in range(9):
            taps_ref[n // 3, n % 3 : n % 3 + 1, lanes] = part(*tap_place(n, half))
        skip_ref[:, lanes] = part(*tap_place(9, half))
    for copy in copies:
        copy.wait()


def spread_call(shares, *operands):
    out_shape = [
        jax.ShapeDtypeStruct((SHARE, CHANS), F32),
        jax.ShapeDtypeStruct((3, 3, CHANS), F32),
        jax.ShapeDtypeStruct((GROUPS, LENGTH), F32),
        jax.ShapeDtypeStruct((1, CHANS), F32),
        *[jax.ShapeDtypeStruct((ROWS, CHANS), BF16)] * 3,
    ]
    scratch = [pltpu.VMEM((SHARE, CHANS), F32), pltpu.SemaphoreType.DMA((SPREAD,))]
    out_specs = [pl.BlockSpec(memory_space=pl.ANY)]
    out_specs += [pl.BlockSpec(memory_space=pltpu.VMEM)] * 6
    shares = shares.reshape(CHANS, SHARE + HALF)
    operands = (shares, *operands)
    return call(spread_kernel, "spread", out_shape, operands, scratch, out_specs=out_specs)


def sent(block, distance):
    count = 4
    route = [(i, i + distance) for i in range(count) if 0 <= i + distance < count]
    return lax.ppermute(block, CTX, route)


def shards(
    query_in, key_in, value_in, short_taps, long_filter, skip_gain, out_weight, out_cotangent
):
    query = query_in[0]
    cot = out_cotangent[0]
    taps = short_taps
    skip = skip_gain.reshape(1, CHANS)
    devices = lax.axis_size(ALL)
    tokens = ROWS * devices
    scale = 1.0 / math.sqrt(tokens)
    core = lax.axis_index("co").astype(jnp.int32).reshape(1)

    key = key_in[0]
    value = value_in[0]
    swap = [(0, 1), (1, 0)]
    own = jnp.concatenate([key, value], axis=1)
    tail = sent(query[ROWS - TAIL :], 1)
    cross = lax.ppermute(own, "xh", [(0, 1)])
    pair = lax.ppermute(own, "co", swap)
    other_cot = lax.ppermute(cot, "co", swap)

    d_gated, strips = pre_call(cot, out_weight, long_filter)
    cross, tail, d_gated = lax.optimization_barrier((cross, tail, d_gated))
    cross_pair = lax.ppermute(cross, "co", swap)
    d_inner = d_inner_call(d_gated, query, tail, taps)
    d_cross = lax.ppermute(d_inner, "xh", [(1, 0)])
    d_pair = lax.ppermute(d_inner, "co", swap)
    gated, inner, signal = fwd_call(
        core, strips, pair, cross, cross_pair, key, value, query, tail, taps, skip
    )
    other_gated = lax.ppermute(gated, "co", swap)
    lag_sums, other_part = lag_call(core, other_cot, d_inner, signal)
    d_cross, lag_sums = lax.optimization_barrier((d_cross, lag_sums))
    d_cross_pair = lax.ppermute(d_cross, "co", swap)
    d_short, head, small = bwd_call(
        core, d_inner, d_pair, d_cross, d_cross_pair, long_filter, lag_sums, signal, key, value, pair, cross_pair, query, tail,
        inner, d_gated, taps, skip,
    )
    other_gated, head, small = lax.optimization_barrier((other_gated, head, small))
    other_small = lax.ppermute(small, "co", swap)
    terms = terms_call(core, cot, other_part, gated, other_gated)
    terms, other_small = lax.optimization_barrier((terms, other_small))
    terms = add_small_call(terms, small, other_small)
    terms, head = lax.optimization_barrier((terms, head))
    terms = terms.reshape(2 * SHARES, CHANS // SHARES, SHARE + HALF)
    terms = lax.all_to_all(terms, CHIPS, 0, 0)
    following = sent(head, -1)

    shares = lax.all_to_all(total_call(terms, scale), DP, 0, 0)
    grad_weight, grad_taps, grad_filter, grad_skip, *input_grad = spread_call(
        shares, d_short, following, taps
    )
    return (
        gated[None],
        *(grad[None] for grad in input_grad),
        grad_taps,
        grad_filter,
        grad_skip.reshape(CHANS),
        grad_weight,
    )


def solution(mesh):
    fine = Mesh(mesh.devices.reshape(2, 2, 4, 2, 4), ALL)
    tokens = P(DP, CTX, None)
    in_specs = (tokens, tokens, tokens, P(), P(), P(), P(), tokens)
    out_specs = (tokens, tokens, tokens, tokens, P(), P(), P(), P(CTX, None))
    return jax.shard_map(
        shards, mesh=fine, in_specs=in_specs, out_specs=out_specs, check_vma=False
    )
```

```python
import math

import jax
import jax.numpy as jnp
from jax import lax
from jax.experimental import pallas as pl
from jax.experimental.pallas import tpu as pltpu
from jax.sharding import Mesh
from jax.sharding import PartitionSpec as P

F32 = jnp.float32
BF16 = jnp.bfloat16
CTX = ("xh", "co")
DP = ("y", "xl", "z")
CHIPS = ("xh", "y", "xl", "z")
ALL = ("xh", "co", "y", "xl", "z")

ROWS = 256
CHANS = 256
HALF = CHANS // 2
GROUPS = 16
LENGTH = 1024
STRIP = 32
PAD = 128
WIDE = LENGTH + PAD
FEATS = 8192
TAIL = 16
SHARES = 32
SHARE = FEATS // 4
SEGMENT = 8
SPREAD = 4
PIECES = 8
VMEM_LIMIT = 20 * 1024 * 1024


def call(kernel, name, out_shape, operands, scratch=(), scalars=0, flops=1 << 10, **more):
    spec = pl.BlockSpec(memory_space=pltpu.VMEM)
    in_specs = [pl.BlockSpec(memory_space=pltpu.SMEM)] * scalars
    in_specs += [spec] * (len(operands) - scalars)
    defaults = {"in_specs": in_specs, "out_specs": jax.tree.map(lambda _: spec, out_shape)}
    more = {**defaults, **more}
    placed = [
        x if s.memory_space == pltpu.SMEM else pltpu.with_memory_space_constraint(x, s.memory_space)
        for x, s in zip(operands, more["in_specs"])
    ]
    return pl.pallas_call(
        kernel,
        out_shape=out_shape,
        scratch_shapes=list(scratch),
        compiler_params=pltpu.CompilerParams(vmem_limit_bytes=VMEM_LIMIT),
        cost_estimate=pl.CostEstimate(flops=flops, bytes_accessed=1 << 10, transcendentals=0),
        name=name,
        **more,
    )(*placed)


def lane_groups():
    return lax.broadcasted_iota(jnp.int32, (STRIP, HALF), 1) // (CHANS // GROUPS)


def later(x, count):
    row = lax.broadcasted_iota(jnp.int32, x.shape, 0)
    return jnp.where(row >= count, pltpu.roll(x, count, 0), 0.0)


def strip_of(line):
    wide = jnp.broadcast_to(line, (STRIP, WIDE))
    return pltpu.roll(wide, 0, 1, stride=1, stride_axis=0)[:, :LENGTH].astype(BF16)


def two_windows(signal_ref, n, half):
    lanes = slice(half * HALF, (half + 1) * HALF)
    windows = [signal_ref[m * STRIP : m * STRIP + LENGTH, lanes] for m in (n, n + 1)]
    return jnp.concatenate(windows, axis=1)


def all_strips(strips_ref, signal_ref):
    ids = lane_groups()
    rows = GROUPS * STRIP // 2
    columns = []
    for half in range(2):
        parts = []
        for n in range(0, ROWS // STRIP, 2):
            result = jnp.dot(
                strips_ref[half * rows : (half + 1) * rows, :],
                two_windows(signal_ref, n, half),
                preferred_element_type=F32,
            )
            for m in range(2):
                out = jnp.zeros((STRIP, HALF), F32)
                for g in range(GROUPS // 2):
                    piece = result[g * STRIP : (g + 1) * STRIP, m * HALF : (m + 1) * HALF]
                    out = jnp.where(ids == g, piece, out)
                parts.append(out)
        columns.append(jnp.concatenate(parts, axis=0))
    return jnp.concatenate(columns, axis=1)


def with_tail(tail, block):
    joined = jnp.concatenate([tail.astype(F32), block.astype(F32)], axis=0)
    return joined[TAIL:], pltpu.roll(joined, 1, 0)[TAIL:], pltpu.roll(joined, 2, 0)[TAIL:]


def short_sum(taps_ref, i, parts):
    return sum(taps_ref[i, j : j + 1, :] * parts[j] for j in range(3))


def lines_of(filter_ref, turned):
    if not turned:
        return jnp.concatenate(
            [filter_ref[...].astype(F32), jnp.zeros((GROUPS, PAD), F32)], axis=1
        )
    row = lax.broadcasted_iota(jnp.int32, (CHANS, CHANS), 0)
    col = lax.broadcasted_iota(jnp.int32, (CHANS, CHANS), 1)
    turn = (row + col == CHANS - 1).astype(F32).astype(BF16)
    pieces = [
        jnp.dot(filter_ref[:, n * CHANS : (n + 1) * CHANS], turn, preferred_element_type=F32)
        for n in reversed(range(LENGTH // CHANS))
    ]
    wide = jnp.concatenate([*pieces, jnp.zeros((GROUPS, PAD), F32)], axis=1)
    return pltpu.roll(wide, WIDE - (STRIP - 1), 1)


def pre_kernel(
    cot_ref, weight_ref, lags_ref, d_gated_ref, strips_ref, cot_buffer, weight_buffer, filter_ref,
    sems, lags_sem,
):
    tile = FEATS // PIECES
    lags_copy = pltpu.make_async_copy(lags_ref, filter_ref, lags_sem)
    lags_copy.start()
    copies = []
    for n in range(PIECES):
        piece = slice(n * tile, (n + 1) * tile)
        pair = (
            pltpu.make_async_copy(cot_ref.at[:, piece], cot_buffer.at[n], sems.at[0, n]),
            pltpu.make_async_copy(weight_ref.at[piece, :], weight_buffer.at[n], sems.at[1, n]),
        )
        for copy in pair:
            copy.start()
        copies.append(pair)
    total = jnp.zeros((ROWS, CHANS), F32)
    for n in range(PIECES):
        if n == PIECES // 2:
            lags_copy.wait()
            lines = lines_of(filter_ref, True)
            for g in range(GROUPS):
                strips_ref[g * STRIP : (g + 1) * STRIP, :] = strip_of(lines[g : g + 1])
        for copy in copies[n]:
            copy.wait()
        total += jnp.dot(cot_buffer[n], weight_buffer[n], preferred_element_type=F32)
    d_gated_ref[...] = total.astype(BF16)


def pre_call(*operands):
    tile = FEATS // PIECES
    scratch = [
        pltpu.VMEM((PIECES, ROWS, tile), BF16),
        pltpu.VMEM((PIECES, tile, CHANS), BF16),
        pltpu.VMEM((GROUPS, LENGTH), BF16),
        pltpu.SemaphoreType.DMA((2, PIECES)),
        pltpu.SemaphoreType.DMA,
    ]
    in_specs = [pl.BlockSpec(memory_space=pltpu.HBM)] * 3
    out_shape = [
        pltpu.VMEM((ROWS, CHANS), BF16),
        pltpu.VMEM((GROUPS * STRIP, LENGTH), BF16),
    ]
    return call(pre_kernel, "pre", out_shape, operands, scratch, in_specs=in_specs, flops=1 << 30)


def d_inner_kernel(d_gated_ref, query_ref, tail_ref, taps_ref, out_ref):
    q_short = short_sum(taps_ref, 0, with_tail(tail_ref[...], query_ref[...]))
    out_ref[...] = (d_gated_ref[...].astype(F32) * q_short).astype(BF16)


def d_inner_call(*operands):
    return call(d_inner_kernel, "d_inner", pltpu.VMEM((ROWS, CHANS), BF16), operands)


def fwd_kernel(
    core_ref, strips_ref, pair_ref, cross_ref, cross_pair_ref, key_ref, value_ref, query_ref,
    tail_ref, taps_ref, skip_ref,
    gated_ref, inner_ref, signal_ref,
):
    upper = core_ref[0] == 1
    pair = pair_ref[...].astype(F32)
    cross_pair = cross_pair_ref[...].astype(F32)
    near = jnp.where(upper, pair, cross_pair)
    far = jnp.where(upper, cross_pair, 0.0)
    own = jnp.concatenate([key_ref[...], value_ref[...]], axis=1).astype(F32)
    both = jnp.concatenate([far, cross_ref[...].astype(F32), near, own], axis=0)
    shifted = (both, later(both, 1), later(both, 2))
    k_short = short_sum(taps_ref, 1, [part[:, :CHANS] for part in shifted])
    v_short = short_sum(taps_ref, 2, [part[:, CHANS:] for part in shifted])
    mixed = (k_short * v_short).astype(BF16)
    signal_ref[: ROWS - STRIP, :] = jnp.zeros((ROWS - STRIP, CHANS), BF16)
    signal_ref[ROWS - STRIP :, :] = mixed
    inner = all_strips(strips_ref, signal_ref) + skip_ref[...] * mixed[LENGTH - ROWS :].astype(F32)
    inner_ref[...] = inner
    q_short = short_sum(taps_ref, 0, with_tail(tail_ref[...], query_ref[...]))
    gated_ref[...] = (q_short * inner).astype(BF16)


def fwd_call(*operands):
    out_shape = [
        pltpu.VMEM((ROWS, CHANS), BF16),
        pltpu.VMEM((ROWS, CHANS), F32),
        pltpu.VMEM((LENGTH + ROWS - STRIP, CHANS), BF16),
    ]
    return call(fwd_kernel, "fwd", out_shape, operands, (), 1, 4 << 30)


def terms_kernel(own_cot_ref, other_cot_ref, gated_ref, other_gated_ref, out_ref):
    dims = (((0,), (0,)), ((), ()))
    for half in range(2):
        total = lax.dot_general(gated_ref[...], own_cot_ref[half], dims, preferred_element_type=F32)
        total += lax.dot_general(other_gated_ref[...], other_cot_ref[half], dims, preferred_element_type=F32)
        out_ref[half, :, :SHARE] = total.astype(BF16)


def terms_call(*operands):
    out_shape = pltpu.VMEM((2, CHANS, SHARE + HALF), BF16)
    return call(terms_kernel, "terms", out_shape, operands, flops=1 << 30)


def add_small_kernel(terms_ref, small_ref, other_small_ref, out_ref, parts_ref, sems):
    total = small_ref[...] + other_small_ref[...]
    parts_ref[...] = total.reshape(CHANS, HALF).astype(BF16)
    copies = [
        pltpu.make_async_copy(parts_ref, out_ref.at[half, :, pl.ds(SHARE, HALF)], sems.at[half])
        for half in range(2)
    ]
    for copy in copies:
        copy.start()
    for copy in copies:
        copy.wait()


def add_small_call(*operands):
    place = pl.BlockSpec(memory_space=pl.ANY)
    spec = pl.BlockSpec(memory_space=pltpu.VMEM)
    return pl.pallas_call(
        add_small_kernel,
        in_specs=[place, spec, spec],
        out_specs=place,
        out_shape=jax.ShapeDtypeStruct(operands[0].shape, BF16),
        scratch_shapes=[pltpu.VMEM((CHANS, HALF), BF16), pltpu.SemaphoreType.DMA((2,))],
        input_output_aliases={0: 0},
        compiler_params=pltpu.CompilerParams(vmem_limit_bytes=VMEM_LIMIT),
        name="add_small",
    )(
        operands[0],
        *(pltpu.with_memory_space_constraint(x, pltpu.VMEM) for x in operands[1:]),
    )


def place(row):
    return row % SHARES, row // SHARES


def tap_place(n, half):
    return place(GROUPS * LENGTH // HALF + 2 * n + half)


def turn_matrix(size, block):
    row = lax.broadcasted_iota(jnp.int32, (size, size), 0)
    col = lax.broadcasted_iota(jnp.int32, (size, size), 1)
    return ((row // block) * block + (block - 1 - row % block) == col).astype(F32)


def lag_kernel(
    core_ref, own_cot_ref, other_cot_ref, d_inner_ref, signal_ref,
    filter_ref, own_part_ref, other_part_ref,
    outer_ref, stack_ref, sums_ref, sems,
):
    copies = []
    for half in range(2):
        start = pl.multiple_of((2 * half + core_ref[0]) * SHARE, SHARE)
        pairs = ((own_cot_ref, own_part_ref), (other_cot_ref, other_part_ref))
        for n, (cot_ref, part_ref) in enumerate(pairs):
            copies.append(
                pltpu.make_async_copy(
                    cot_ref.at[:, pl.ds(start, SHARE)], part_ref.at[half], sems.at[n, half]
                )
            )
            copies[-1].start()
    turn = turn_matrix(ROWS, STRIP).astype(BF16)
    turned = jnp.dot(turn, d_inner_ref[...], preferred_element_type=F32)
    ids = lane_groups()
    count = GROUPS * STRIP // 2
    outer_ref[:, LENGTH:] = jnp.zeros((GROUPS * STRIP, PAD), F32)
    for half in range(2):
        rows = slice(half * count, (half + 1) * count)
        for n in range(0, ROWS // STRIP, 2):
            for m in range(2):
                start = (n + m) * STRIP
                piece = turned[start : start + STRIP, half * HALF : (half + 1) * HALF]
                for g in range(GROUPS // 2):
                    stack_ref[g * STRIP : (g + 1) * STRIP, m * HALF : (m + 1) * HALF] = jnp.where(
                        ids == g, piece, 0.0
                    ).astype(BF16)
            term = lax.dot_general(
                stack_ref[...],
                two_windows(signal_ref, n, half),
                (((1,), (1,)), ((), ())),
                preferred_element_type=F32,
            )
            if n == 0:
                outer_ref[rows, :LENGTH] = term
            else:
                outer_ref[rows, :LENGTH] += term
    for g in range(GROUPS):
        rows = outer_ref[g * STRIP : (g + 1) * STRIP, :]
        skewed = pltpu.roll(rows, WIDE - (STRIP - 1), 1, stride=1, stride_axis=0)
        sums_ref[g : g + 1, :] = jnp.sum(skewed, axis=0, keepdims=True)
    sums = pltpu.roll(sums_ref[...], STRIP - 1, 1)
    turn = turn_matrix(CHANS, CHANS)
    last = LENGTH // CHANS - 1
    for n in range(LENGTH // CHANS):
        filter_ref[:, n * CHANS : (n + 1) * CHANS] = jnp.dot(
            sums[:, (last - n) * CHANS : (last - n + 1) * CHANS],
            turn,
            precision=lax.Precision.HIGHEST,
            preferred_element_type=F32,
        )
    for copy in copies:
        copy.wait()


def lag_call(*operands):
    scratch = [
        pltpu.VMEM((GROUPS * STRIP, WIDE), F32),
        pltpu.VMEM((GROUPS * STRIP // 2, CHANS), BF16),
        pltpu.VMEM((GROUPS, WIDE), F32),
        pltpu.SemaphoreType.DMA((2, 2)),
    ]
    out_shape = [pltpu.VMEM((GROUPS, LENGTH), F32)] + [pltpu.VMEM((2, ROWS, SHARE), BF16)] * 2
    in_specs = [pl.BlockSpec(memory_space=pltpu.SMEM)] + [pl.BlockSpec(memory_space=pltpu.HBM)] * 2
    in_specs += [pl.BlockSpec(memory_space=pltpu.VMEM)] * 2
    return call(lag_kernel, "lag_sums", out_shape, operands, scratch, in_specs=in_specs)


def bwd_kernel(
    core_ref, d0_ref, d_pair_ref, d_cross_ref, d_cross_pair_ref, lags_ref, filter_ref, signal_ref, key_ref, value_ref,
    pair_ref, cross_pair_ref, query_ref, tail_ref, inner_ref, d_gated_ref, taps_ref, skip_ref,
    d_short_ref, head_ref, small_ref,
    strips_ref, ahead_ref,
):
    upper = core_ref[0] == 1
    d_pair = d_pair_ref[...].astype(F32)
    d_cross_pair = d_cross_pair_ref[...].astype(F32)
    later_blocks = (
        d0_ref[...],
        jnp.where(upper, d_cross_pair, d_pair).astype(BF16),
        d_cross_ref[...],
        jnp.where(upper, 0.0, d_cross_pair).astype(BF16),
    )
    for n, block in enumerate(later_blocks):
        ahead_ref[n * ROWS : (n + 1) * ROWS, :] = block
    ahead_ref[LENGTH:, :] = jnp.zeros((ROWS, CHANS), BF16)
    lines = lines_of(lags_ref, False)
    for g in range(GROUPS):
        strips_ref[g * STRIP : (g + 1) * STRIP, :] = strip_of(lines[g : g + 1])
    d_inner = d0_ref[...].astype(F32)
    mixed = signal_ref[LENGTH - STRIP :, :]
    d_mixed = all_strips(strips_ref, ahead_ref) + skip_ref[...] * d_inner

    last = slice(ROWS - TAIL, ROWS)
    near = jnp.where(upper, pair_ref[last, :].astype(F32), cross_pair_ref[last, :].astype(F32))
    k_parts = with_tail(near[:, :CHANS], key_ref[...])
    v_parts = with_tail(near[:, CHANS:], value_ref[...])
    q_parts = with_tail(tail_ref[...], query_ref[...])
    small_ref[...] = jnp.zeros_like(small_ref)
    sums = []
    d_qs = d_gated_ref[...].astype(F32) * inner_ref[...]
    d_ks = d_mixed * short_sum(taps_ref, 2, v_parts)
    d_vs = d_mixed * short_sum(taps_ref, 1, k_parts)
    for i, (grad, parts) in enumerate(((d_qs, q_parts), (d_ks, k_parts), (d_vs, v_parts))):
        d_short_ref[i] = grad
        head_ref[i] = grad[:8]
        for j in range(3):
            sums.append(jnp.sum(grad * parts[j], axis=0, keepdims=True))
    sums.append(jnp.sum(d_inner * mixed.astype(F32), axis=0, keepdims=True))
    for n, row in enumerate(sums):
        for half in range(2):
            share, slot = tap_place(n, half)
            small_ref[share, slot : slot + 1, :] = row[:, half * HALF : (half + 1) * HALF]

    for g in range(GROUPS):
        for n in range(LENGTH // HALF):
            share, slot = place(g * (LENGTH // HALF) + n)
            small_ref[share, slot : slot + 1, :] = filter_ref[g : g + 1, n * HALF : (n + 1) * HALF]


def bwd_call(*operands):
    out_shape = [
        pltpu.VMEM((3, ROWS, CHANS), F32),
        pltpu.VMEM((3, 8, CHANS), F32),
        pltpu.VMEM((SHARES, SEGMENT, HALF), F32),
    ]
    scratch = [
        pltpu.VMEM((GROUPS * STRIP, LENGTH), BF16),
        pltpu.VMEM((LENGTH + ROWS, CHANS), BF16),
    ]
    return call(bwd_kernel, "bwd", out_shape, operands, scratch, 1)


def input_grads(d_short_ref, next_ref, taps_ref, out_refs):
    for i, out_ref in enumerate(out_refs):
        joined = jnp.concatenate([d_short_ref[i], next_ref[i]], axis=0)
        rows = joined.shape[0]
        parts = (
            joined[:ROWS],
            pltpu.roll(joined, rows - 1, 0)[:ROWS],
            pltpu.roll(joined, rows - 2, 0)[:ROWS],
        )
        out_ref[...] = short_sum(taps_ref, i, parts).astype(BF16)


def total_kernel(scale, terms_ref, out_ref):
    total = (jnp.sum(terms_ref[...].astype(F32), axis=0) * scale).astype(BF16)
    out_ref[...] = jnp.broadcast_to(total[None], out_ref.shape)


def total_call(terms, scale):
    out_shape = pltpu.VMEM((SHARES, *terms.shape[1:]), BF16)
    return call(lambda *refs: total_kernel(scale, *refs), "total", out_shape, (terms,))


def spread_kernel(
    shares_ref, d_short_ref, next_ref, short_taps_ref,
    weight_ref, taps_ref, filter_ref, skip_ref, query_ref, key_ref, value_ref,
    turned_ref, sems,
):
    tile = SHARE // SPREAD
    copies = []
    for n in range(SPREAD):
        piece = slice(n * tile, (n + 1) * tile)
        turned_ref[piece, :] = shares_ref[:, piece].astype(F32).T
        copies.append(
            pltpu.make_async_copy(turned_ref.at[piece, :], weight_ref.at[piece, :], sems.at[n])
        )
        copies[-1].start()
    input_grads(d_short_ref, next_ref, short_taps_ref, (query_ref, key_ref, value_ref))
    small = shares_ref[:, SHARE:].astype(F32)

    def part(share, slot):
        return small[share * SEGMENT + slot : share * SEGMENT + slot + 1]

    for g in range(GROUPS):
        for n in range(LENGTH // HALF):
            piece = part(*place(g * (LENGTH // HALF) + n))
            filter_ref[g : g + 1, n * HALF : (n + 1) * HALF] = piece
    for half in range(2):
        lanes = slice(half * HALF, (half + 1) * HALF)
        for n in range(9):
            taps_ref[n // 3, n % 3 : n % 3 + 1, lanes] = part(*tap_place(n, half))
        skip_ref[:, lanes] = part(*tap_place(9, half))
    for copy in copies:
        copy.wait()


def spread_call(shares, *operands):
    out_shape = [
        jax.ShapeDtypeStruct((SHARE, CHANS), F32),
        jax.ShapeDtypeStruct((3, 3, CHANS), F32),
        jax.ShapeDtypeStruct((GROUPS, LENGTH), F32),
        jax.ShapeDtypeStruct((1, CHANS), F32),
        *[jax.ShapeDtypeStruct((ROWS, CHANS), BF16)] * 3,
    ]
    scratch = [pltpu.VMEM((SHARE, CHANS), F32), pltpu.SemaphoreType.DMA((SPREAD,))]
    out_specs = [pl.BlockSpec(memory_space=pl.ANY)]
    out_specs += [pl.BlockSpec(memory_space=pltpu.VMEM)] * 6
    shares = shares.reshape(CHANS, SHARE + HALF)
    operands = (shares, *operands)
    return call(spread_kernel, "spread", out_shape, operands, scratch, out_specs=out_specs)


def sent(block, distance):
    count = 4
    route = [(i, i + distance) for i in range(count) if 0 <= i + distance < count]
    return lax.ppermute(block, CTX, route)


def shards(
    query_in, key_in, value_in, short_taps, long_filter, skip_gain, out_weight, out_cotangent
):
    query = query_in[0]
    cot = out_cotangent[0]
    taps = short_taps
    skip = skip_gain.reshape(1, CHANS)
    devices = lax.axis_size(ALL)
    tokens = ROWS * devices
    scale = 1.0 / math.sqrt(tokens)
    core = lax.axis_index("co").astype(jnp.int32).reshape(1)

    key = key_in[0]
    value = value_in[0]
    swap = [(0, 1), (1, 0)]
    own = jnp.concatenate([key, value], axis=1)
    tail = sent(query[ROWS - TAIL :], 1)
    cross = lax.ppermute(own, "xh", [(0, 1)])
    pair = lax.ppermute(own, "co", swap)
    other_cot = lax.ppermute(cot, "co", swap)

    d_gated, strips = pre_call(cot, out_weight, long_filter)
    cross, tail, d_gated = lax.optimization_barrier((cross, tail, d_gated))
    cross_pair = lax.ppermute(cross, "co", swap)
    d_inner = d_inner_call(d_gated, query, tail, taps)
    d_cross = lax.ppermute(d_inner, "xh", [(1, 0)])
    d_pair = lax.ppermute(d_inner, "co", swap)
    gated, inner, signal = fwd_call(
        core, strips, pair, cross, cross_pair, key, value, query, tail, taps, skip
    )
    other_gated = lax.ppermute(gated, "co", swap)
    lag_sums, own_part, other_part = lag_call(core, cot, other_cot, d_inner, signal)
    d_cross, lag_sums = lax.optimization_barrier((d_cross, lag_sums))
    d_cross_pair = lax.ppermute(d_cross, "co", swap)
    d_short, head, small = bwd_call(
        core, d_inner, d_pair, d_cross, d_cross_pair, long_filter, lag_sums, signal, key, value, pair, cross_pair, query, tail,
        inner, d_gated, taps, skip,
    )
    other_gated, head, small = lax.optimization_barrier((other_gated, head, small))
    other_small = lax.ppermute(small, "co", swap)
    terms = terms_call(own_part, other_part, gated, other_gated)
    terms, other_small = lax.optimization_barrier((terms, other_small))
    terms = add_small_call(terms, small, other_small)
    terms, head = lax.optimization_barrier((terms, head))
    terms = terms.reshape(2 * SHARES, CHANS // SHARES, SHARE + HALF)
    terms = lax.all_to_all(terms, CHIPS, 0, 0)
    following = sent(head, -1)

    shares = lax.all_to_all(total_call(terms, scale), DP, 0, 0)
    grad_weight, grad_taps, grad_filter, grad_skip, *input_grad = spread_call(
        shares, d_short, following, taps
    )
    return (
        gated[None],
        *(grad[None] for grad in input_grad),
        grad_taps,
        grad_filter,
        grad_skip.reshape(CHANS),
        grad_weight,
    )


def solution(mesh):
    fine = Mesh(mesh.devices.reshape(2, 2, 4, 2, 4), ALL)
    tokens = P(DP, CTX, None)
    in_specs = (tokens, tokens, tokens, P(), P(), P(), P(), tokens)
    out_specs = (tokens, tokens, tokens, tokens, P(), P(), P(), P(CTX, None))
    return jax.shard_map(
        shards, mesh=fine, in_specs=in_specs, out_specs=out_specs, check_vma=False
    )
```
